512 devices in a mesh: stream: 8 (over y), span: 16 (over z, core), vert: 4 (over x).
Axes of the slice: x: 4, y: 8, z: 8, core: 2. Of those that a mesh axis runs over, the one named last changes fastest.
Arguments:
- fields: float32 [5, 128, 256, 1024], P(None, 'vert', 'span', 'stream'), may hold values from -6 to 6
- solid_frac: float32 [128, 256, 1024], P('vert', 'span', 'stream'), may hold values from 0 to 1
- panels: float32 [32768, 5, 256], P(('stream', 'span', 'vert')), may hold values from -0.015625 to 0.015625
- panel_owner: int32 [32768, 1], P(('stream', 'span', 'vert')), may hold values from 0 to 63; in each aligned block of 64 rows (0 to 63, 64 to 127, ...) at most 2 rows name the same one
- deck_cells: int32 [4, 16, 8, 2048], P('vert', 'span', 'stream'), may hold values from 0 to 65535
- deck_geom: float32 [4, 16, 8, 3, 2048], P('vert', None, 'stream'), may hold values from -6 to 6
- strip_ids: int32 [4, 16, 8, 2048], P('vert', None, 'stream'), may hold values from 0 to 63, as said below
- mode_shapes: float32 [3, 64, 32], replicated, may hold values from -0.0034179688 to 0.0034179688
Outputs:
- new_fields: float32 [5, 128, 256, 1024], P(None, 'vert', 'span', 'stream')
- modal_force: float32 [32], replicated
The draws below stay inside these ranges and needn't reach their ends.
Inputs may be any that keep to these rules, and one draw needn't show every extreme that they name: `panel_owner`: tile number s * 4 + v for along-deck tile s and vertical tile v. Among the 64 panels of one device no tile is named more than 2 times; some device names some tile exactly 2 times. `strip_ids`: cells of along-deck tile s belong to strips s * 4 to (s + 1) * 4 - 1.
All inputs are finite; a program needn't handle non-finite values.
Results may differ from the reference program's by a relative error of at most 0.00012.
Values sent between devices are 32-bit elements; how exact they have to be, the bound alone decides.
No kernel may reach another device: no remote copies, remote signals or barrier semaphores. Data moves between devices by JAX's collectives and lax.ppermute only.
A program may use at most 128 MiB of HBM per device.

```python
import math
import jax
import jax.numpy as jnp
import numpy as np
from jax import lax

CX = 128
CY = 16
CZ = 32
SPEC = 128
CAP = 2
DECK_DEV = 2048
STRIP_DEV = 4
MODES = 32
NX = 1024
NY = 256
NZ = 128
PAN_DEV = 64
PANELS = 32768
NSTRIP = 64
N_STREAM = 8
N_SPAN = 16
N_VERT = 4
DEVICES = 512


def draw_strip_ids(key, part):
    offsets = jax.random.randint(key, (N_VERT, N_SPAN, N_STREAM, DECK_DEV), 0, STRIP_DEV, dtype=jnp.int32)
    starts = (jnp.arange(N_SPAN, dtype=jnp.int32) * STRIP_DEV)[None, :, None, None]
    return (starts + offsets).astype(jnp.int32)


def touch_ends(values, own_key, low, high):
    longest = values.shape.index(max(values.shape))
    spots = []
    for shift in (0, 1):
        where = [jax.random.randint(jax.random.fold_in(own_key, axis), (), 0, length) for axis, length in enumerate(values.shape)]
        where[longest] = (where[longest] + shift) % values.shape[longest]
        spots.append(tuple(where))
    return values.at[spots[0]].set(low).at[spots[1]].set(high)


def levels(stream_key, extent, split, low, largest):
    level, own = 1.0, jax.random.fold_in(stream_key, 6)
    for position, parts in split:
        draws = jnp.exp(jax.random.uniform(jax.random.fold_in(own, position), (parts,), jnp.float32, low / len(split), largest / len(split)))
        level = level * jnp.repeat(draws, extent[position] // parts).reshape([-1 if axis == position else 1 for axis in range(len(extent))])
    return level


def routed_block(rng, own, number, rows, amount, top, bound, slope):
    sequence = jax.random.permutation(rng, amount)
    heavy_load, ordinary = load_shares(amount, rows * top, bound, slope, True), load_shares(amount, rows * top, bound, slope, False)
    places = jnp.arange(amount)

    def named(tallies, turn):
        used = int((tallies > 0).sum())
        fixed = max(1, used // 4)
        passed = fixed + (places - fixed + turn * (used - fixed)) % max(1, amount - fixed)
        return jnp.zeros((amount,), jnp.int32).at[sequence[jnp.where(places < fixed, places, passed)]].set(jnp.asarray(tallies, jnp.int32))

    tallies = jnp.where(number % 4 == 0, named(heavy_load, number // 4), named(ordinary, number - number // 4 - 1))
    mixed = jax.random.permutation(jax.random.fold_in(own, 3), amount)
    source_of, sink = mixed[0:amount // 2 * 2:2], mixed[1:amount // 2 * 2:2]
    slack = jnp.minimum(tallies[source_of] - 1, bound - tallies[sink]) // 2
    slack = jnp.where((source_of == sequence[0]) | (sink == sequence[0]) | (tallies[sink] == 0), 0, jnp.maximum(slack, 0))
    passed = jax.random.randint(jax.random.fold_in(own, 4), (amount // 2,), 0, 1 << 20) % (slack + 1)
    tallies = tallies.at[source_of].add(-passed).at[sink].add(passed)
    labels = jnp.searchsorted(jnp.cumsum(tallies), jnp.arange(rows * top), side="right").astype(jnp.int32)
    table = labels.reshape(top, rows).T
    table = table[jax.random.permutation(jax.random.fold_in(own, 1), rows)]
    turn = jax.random.randint(jax.random.fold_in(own, 2), (rows, 1), 0, top)
    return jnp.take_along_axis(table, (jnp.arange(top)[None, :] + turn) % top, axis=1)


def load_shares(count, total, reach, lean, full):
    weights = [(1 << 20) // math.isqrt(rank ** lean) + 1 for rank in range(1, count + 1)]
    largest = reach if full else min(reach, max(-(-total // count), total * weights[0] // sum(weights)))
    least = 1 if total - largest >= count - 1 else 0
    given, surplus = [largest] + [least] * (count - 1), total - largest - least * (count - 1)
    while surplus > 0:
        candidates = [i for i in range(1, count) if given[i] < largest] or [i for i in range(1, count) if given[i] < reach]
        mass, left = sum([weights[i] for i in candidates]), surplus
        for i in candidates:
            extra = min(reach - given[i], max(1, left * weights[i] // mass), surplus)
            given[i] = given[i] + extra
            surplus = surplus - extra
    return np.array(given)


def scatter_about(own_key, shape, scale, bound, cuts=(), kind=jnp.bfloat16):
    drawn = jax.random.normal(own_key, shape, jnp.float32) * scale
    if len(cuts) > 0:
        drawn = levels(own_key, shape, cuts, -0.22, 0.18) * drawn
    return jnp.clip(drawn, min=-bound, max=bound).astype(kind)


def setup_inputs(seed: int = 0) -> dict:
    seeds = jax.random.split(jax.random.key(seed), 9)
    fields = scatter_about(seeds[0], (5, NZ, NY, NX), 1.0, 6.0, ((1, 4), (2, 16), (3, 8)), jnp.float32)
    solid_frac = jnp.clip(1.0 * jax.random.uniform(seeds[1], (NZ, NY, NX), jnp.float32) ** levels(seeds[1], (NZ, NY, NX), ((0, 4), (1, 16), (2, 8)), -0.2, 0.2), 0.0, 1.0)
    panels = scatter_about(seeds[2], (PANELS, 5, 2 * SPEC), (2 * SPEC * PAN_DEV * N_STREAM) ** -0.5, 0.015625, ((0, 512),), jnp.float32)
    panel_owner_keys = jax.random.split(jax.random.fold_in(seeds[3], 1), PANELS // PAN_DEV)
    panel_owner_turns = jax.random.permutation(jax.random.fold_in(seeds[3], 3), PANELS // PAN_DEV)
    panel_owner = jax.vmap(lambda own, number: routed_block(jax.random.fold_in(seeds[3], 2), own, number, PAN_DEV, N_SPAN * N_VERT, 1, CAP, 2))(panel_owner_keys, panel_owner_turns).reshape((PANELS, 1))
    deck_cells = touch_ends(jax.random.randint(seeds[4], (N_VERT, N_SPAN, N_STREAM, DECK_DEV), 0, CX * CY * CZ), jax.random.fold_in(seeds[4], 1), 0, (CX * CY * CZ) - 1).astype(jnp.int32)
    deck_geom = scatter_about(seeds[5], (N_VERT, N_SPAN, N_STREAM, 3, DECK_DEV), 1.0, 6.0, ((0, 4), (2, 8)), jnp.float32)
    strip_ids = draw_strip_ids(jax.random.fold_in(seeds[8], 71), 0)
    mode_shapes = scatter_about(seeds[7], (3, NSTRIP, MODES), (3 * DECK_DEV * DEVICES) ** -0.5, 0.0034179688, (), jnp.float32)
    return dict(fields=fields, solid_frac=solid_frac, panels=panels, panel_owner=panel_owner, deck_cells=deck_cells, deck_geom=deck_geom, strip_ids=strip_ids, mode_shapes=mode_shapes)


time_step = 0.15
viscous = 0.05
heat_diff = 0.03
sound_sq = 1.0
buoyant = 0.5
penalty = 0.5
relax_time = 0.5
relax_depth = 8.0
wave_cols = 16


def wave_basis(heights, widths, total_z, total_y, spec):
    modes = jnp.arange(spec, dtype=jnp.int32)
    across = (modes % wave_cols)[:, None, None]
    upward = (modes // wave_cols)[:, None, None]
    period = total_y * total_z
    phase = (across * widths[None, None, :] * total_z + upward * heights[None, :, None] * total_y) % period
    angle = phase.astype(jnp.float32) * (2.0 * math.pi / period)
    return jnp.concatenate([jnp.cos(angle), jnp.sin(angle)], axis=0)


def relax_weights(positions, limit):
    spots = positions.astype(jnp.float32)
    return jnp.where(positions < limit, jnp.exp(-spots / relax_depth) / relax_time, 0.0)


def rates(padded, solid_frac, relax_rate, target_plane):
    centre = padded[:, 1:-1, 1:-1, 1:-1]
    east_side = padded[:, 1:-1, 1:-1, 2:]
    west_side = padded[:, 1:-1, 1:-1, :-2]
    north_side = padded[:, 1:-1, 2:, 1:-1]
    south_side = padded[:, 1:-1, :-2, 1:-1]
    upper_side = padded[:, 2:, 1:-1, 1:-1]
    lower_side = padded[:, :-2, 1:-1, 1:-1]
    grad_x = 0.5 * (east_side - west_side)
    grad_y = 0.5 * (north_side - south_side)
    grad_z = 0.5 * (upper_side - lower_side)
    laplace = east_side + west_side + north_side + south_side + upper_side + lower_side - 6.0 * centre
    speed_x = centre[0]
    speed_y = centre[1]
    speed_z = centre[2]
    carried = speed_x * grad_x + speed_y * grad_y + speed_z * grad_z
    coeffs = jnp.array([viscous, viscous, viscous, viscous, heat_diff], jnp.float32)[:, None, None, None]
    damping = solid_frac / penalty
    nudging = relax_rate[None, None, None, :] * (target_plane[:, :, :, None] - centre)
    common = coeffs * laplace - carried + nudging
    extra_terms = jnp.stack([
        -grad_x[3] - damping * speed_x,
        -grad_y[3] - damping * speed_y,
        -grad_z[3] - damping * speed_z + buoyant * centre[4],
        -sound_sq * (grad_x[0] + grad_y[1] + grad_z[2]),
        jnp.zeros_like(speed_x)])
    return common + extra_terms


def reference(fields, solid_frac, panels, panel_owner, deck_cells, deck_geom, strip_ids, mode_shapes):
    tile_count = N_SPAN * N_VERT
    coeffs = jax.ops.segment_sum(panels.reshape(panels.shape[0], -1), panel_owner[:, 0], num_segments=tile_count)
    coeffs = coeffs.reshape(N_SPAN, N_VERT, 5, 2 * SPEC)
    wave_table = wave_basis(jnp.arange(NZ, dtype=jnp.int32), jnp.arange(NY, dtype=jnp.int32), NZ, NY, SPEC)
    wave_table = wave_table.reshape(2 * SPEC, N_VERT, CZ, N_SPAN, CY)
    inflow_plane = jnp.einsum('svfk,kvisj->fvisj', coeffs, wave_table, precision=lax.Precision.HIGHEST)
    inflow_plane = inflow_plane.reshape(5, NZ, NY)
    target_plane = inflow_plane + jnp.array([1.0, 0.0, 0.0, 0.0, 0.0], jnp.float32)[:, None, None]
    relax_rate = relax_weights(jnp.arange(NX, dtype=jnp.int32), CX // 2)

    def advance(state):
        padded = jnp.pad(state, ((0, 0), (1, 1), (1, 1), (1, 1)))
        return rates(padded, solid_frac, relax_rate, target_plane)

    first_update = fields + time_step * advance(fields)
    new_fields = 0.5 * (fields + first_update + time_step * advance(first_update))

    pressure = new_fields[3].reshape(N_VERT, CZ, N_SPAN, CY, N_STREAM, CX)
    pressure = pressure.transpose(0, 2, 4, 1, 3, 5).reshape(N_VERT, N_SPAN, N_STREAM, CZ * CY * CX)
    sampled = jnp.take_along_axis(pressure, deck_cells, axis=3)
    traction = sampled[:, :, :, None, :] * deck_geom
    traction = traction.transpose(3, 0, 1, 2, 4).reshape(3, -1)
    forces = jax.ops.segment_sum(traction.T, strip_ids.reshape(-1), num_segments=NSTRIP)
    modal_force = jnp.einsum('jc,cjm->m', forces, mode_shapes, precision=lax.Precision.HIGHEST)
    return new_fields, modal_force
```

```python
import math

import jax
import jax.numpy as jnp
import numpy as np
from jax import lax
from jax.experimental import pallas as pl
from jax.experimental.pallas import tpu as pltpu
from jax.sharding import PartitionSpec as P

time_step = 0.15
viscous = 0.05
heat_diff = 0.03
sound_sq = 1.0
buoyant = 0.5
penalty = 0.5
relax_time = 0.5
relax_depth = 8.0
wave_cols = 16

HI = lax.Precision.HIGHEST
NF = 5
ROWS = 16


def mdot(a, b, dims):
    return lax.dot_general(
        a, b, (dims, ((), ())), precision=HI, preferred_element_type=jnp.float32
    )


def wave_tables(cz, cy, n_span, n_vert, spec):
    modes = np.arange(spec)
    across = (modes % wave_cols).astype(np.float64)
    upward = (modes // wave_cols).astype(np.float64)
    ny, nz = cy * n_span, cz * n_vert

    def basis(z, y):
        turn = across[None] * y[:, None] / ny + upward[None] * z[:, None] / nz
        angle = 2.0 * math.pi * turn
        return np.concatenate([np.cos(angle), np.sin(angle)], axis=1)

    z, y = np.arange(cz, dtype=np.float64), np.arange(cy, dtype=np.float64)
    plane = basis(np.repeat(z, cy), np.tile(y, cz)).astype(np.float32)
    edges = np.zeros((2 * spec, 128), np.float64)
    at = 0
    for part in (
        basis(z, 0 * z + cy - 1),
        basis(z, 0 * z),
        basis(0 * y + cz - 1, y),
        basis(0 * y, y),
    ):
        edges[:, at : at + part.shape[0]] = part.T
        at += part.shape[0]
    s, v = np.repeat(np.arange(n_span), n_vert), np.tile(np.arange(n_vert), n_span)
    turn = basis(1.0 * v * cz, 1.0 * s * cy).astype(np.float32)
    return plane, edges.astype(np.float32), turn


def sum_panels(n_vert, panels, owner, turn, edge_table, out):
    tiles = turn.shape[0]
    spec = turn.shape[1] // 2
    held = owner.shape[0]
    named = (owner[...] == lax.broadcasted_iota(jnp.int32, (held, tiles), 1)).astype(jnp.float32)
    cos_t, sin_t = turn[:, :spec], turn[:, spec:]
    lane = lax.broadcasted_iota(jnp.int32, (tiles, 128), 1)
    for f in range(NF):
        total = mdot(named, panels[:, f, :], ((0,), (0,)))
        c, s = total[:, :spec], total[:, spec:]
        c2 = c * cos_t + s * sin_t
        s2 = s * cos_t - c * sin_t
        out[pl.ds(f, tiles, stride=ROWS), :] = c2
        out[pl.ds(8 + f, tiles, stride=ROWS), :] = s2
        e = mdot(c2, edge_table[:spec, :], ((1,), (0,))) + mdot(
            s2, edge_table[spec:, :], ((1,), (0,))
        )
        row = jnp.where(
            lane < 32,
            jnp.roll(e, n_vert, 0),
            jnp.where(
                lane < 64,
                jnp.roll(e, -n_vert, 0),
                jnp.where(lane < 80, jnp.roll(e, 1, 0), jnp.roll(e, -1, 0)),
            ),
        )
        at = 5 + f if f < 3 else 10 + f
        out[pl.ds(at, tiles, stride=ROWS), :] = row
    out[pl.ds(15, tiles, stride=ROWS), :] = jnp.zeros((tiles, 128), jnp.float32)


def sum_sources(got, out):
    tiles = got.shape[0]
    total = jnp.sum(got[...], axis=0)
    for i in range(out.shape[0]):
        out[i] = total


def lane_ids(shape):
    return lax.broadcasted_iota(jnp.int32, shape, len(shape) - 1)


def packed_x(acc, v, z):
    lane = lane_ids((8, 128))
    for h in range(2):
        k = 2 * z + h
        acc = jnp.where((lane >> 1) == k, pltpu.roll(v[8 * h : 8 * h + 8], 2 * k + 1, 1), acc)
    return acc


def pack_faces(fields, xf, ylo, yhi, zlo, zhi):
    cz = fields.shape[1]

    def body(z, accs):
        return tuple(packed_x(accs[f], fields[f, z], z) for f in range(NF))

    zero = jnp.zeros((8, 128), jnp.float32)
    accs = lax.fori_loop(0, cz, body, (zero,) * NF, unroll=4)
    for f in range(NF):
        xf[f] = accs[f]
    store_faces(fields, ylo, yhi, zlo, zhi)


def store_faces(state, ylo, yhi, zlo, zhi):
    cz, cy = state.shape[1], state.shape[2]
    for f in range(NF):
        ylo[f] = state[f, :, 0, :]
        yhi[f] = state[f, :, cy - 1, :]
        zlo[f] = state[f, 0]
        zhi[f] = state[f, cz - 1]


def ghosts_x(xw, xe):
    lane = lane_ids((8, 128))
    return [jnp.where((lane & 1) == 0, xw[f], pltpu.roll(xe[f], 126, 1)) for f in range(NF)]


def slab_rates(q, xg, damp, relax, z):
    lane = lane_ids((16, 128))
    cs, gx, gy, gz, lap = [], [], [], [], []
    for f in range(NF):
        c = q[f, z + 1, 8:24, :]
        up, down = q[f, z + 2, 8:24, :], q[f, z, 8:24, :]
        north, south = q[f, z + 1, 9:25, :], q[f, z + 1, 7:23, :]
        side = jnp.concatenate(
            [
                pltpu.roll(xg[f], (128 - 4 * z) & 127, 1),
                pltpu.roll(xg[f], (126 - 4 * z) & 127, 1),
            ],
            axis=0,
        )
        west = jnp.where(lane == 0, side, pltpu.roll(c, 1, 1))
        east = jnp.where(lane == 127, side, pltpu.roll(c, 127, 1))
        cs.append(c)
        gx.append(0.5 * (east - west))
        gy.append(0.5 * (north - south))
        gz.append(0.5 * (up - down))
        lap.append(east + west + north + south + up + down - 6.0 * c)
    u, v, w = cs[0], cs[1], cs[2]
    out = []
    for f in range(NF):
        nu = heat_diff if f == 4 else viscous
        r = nu * lap[f] - (u * gx[f] + v * gy[f] + w * gz[f]) - relax * cs[f]
        if f == 0:
            r = r - gx[3] - damp * u
        elif f == 1:
            r = r - gy[3] - damp * v
        elif f == 2:
            r = r - gz[3] - damp * w + buoyant * cs[4]
        elif f == 3:
            r = r - sound_sq * (gx[0] + gy[1] + gz[2])
        out.append(r)
    return cs, out


def first_step(fields, solid, xw, xe, ys, yn, zd, zu, relax, base, xf, ylo, yhi, zlo, zhi, q):
    cz = fields.shape[1]
    for f in range(NF):
        q[f, 1 : cz + 1, 7, :] = ys[f]
        q[f, 1 : cz + 1, 24, :] = yn[f]
        q[f, 0, 8:24, :] = zd[f]
        q[f, cz + 1, 8:24, :] = zu[f]

    def fill(z, carry):
        for f in range(NF):
            q[f, z + 1, 8:24, :] = fields[f, z]
        return carry

    lax.fori_loop(0, cz, fill, 0, unroll=4)
    xg = ghosts_x(xw, xe)
    relax_row = relax[...]

    def body(z, accs):
        damp = solid[z] * (1.0 / penalty)
        cs, rs = slab_rates(q, xg, damp, relax_row, z)
        new = []
        for f in range(NF):
            b = cs[f] + time_step * rs[f]
            base[f, z] = b
            new.append(packed_x(accs[f], b, z))
        return tuple(new)

    zero = jnp.zeros((8, 128), jnp.float32)
    accs = lax.fori_loop(0, cz, body, (zero,) * NF)
    for f in range(NF):
        xf[f] = accs[f]
    store_faces(base, ylo, yhi, zlo, zhi)


def second_step(
    flags,
    coeffs,
    plane_table,
    fields,
    base,
    solid,
    xw,
    xe,
    ys,
    yn,
    zd,
    zu,
    relax,
    cells,
    geom,
    strips,
    shapes,
    out,
    modal,
    q,
    target,
    geom_v,
    strips_v,
    sems,
):
    cz, cy = fields.shape[1], fields.shape[2]
    spec = plane_table.shape[1] // 2
    span_pos = flags[0]
    get_geom = pltpu.make_async_copy(geom.at[0, span_pos, 0], geom_v, sems.at[0])
    get_strips = pltpu.make_async_copy(strips.at[0, span_pos], strips_v, sems.at[1])
    get_geom.start()
    get_strips.start()
    chunk = coeffs[0]
    for i in range(1, coeffs.shape[0]):
        chunk = chunk + coeffs[i]
    low, high = chunk[0:8], chunk[8:16]
    one = jnp.where(lane_ids((1, 8)) == 0, 1.0, 0.0)
    target[...] = (
        mdot(plane_table[:, :spec], low, ((1,), (1,)))
        + mdot(plane_table[:, spec:], high, ((1,), (1,)))
        + one
    )
    n_edge = 2 * cz + 2 * cy
    pick = (
        lax.broadcasted_iota(jnp.int32, (n_edge, 128), 0) == lane_ids((n_edge, 128))
    ).astype(jnp.float32)
    e_low = mdot(pick, low, ((1,), (1,)))
    e_high = mdot(pick, high, ((1,), (1,)))
    relax_row = relax[...]
    push = time_step * relax_row
    for f in range(NF):
        col = e_low[:, 5 + f : 6 + f] if f < 3 else e_high[:, 2 + f : 3 + f]
        if f == 0:
            col = col + 1.0
        col = col * push

        def masked(part, flag):
            return jnp.where(flags[flag] > 0, part, 0.0)

        q[f, 1 : cz + 1, 7, :] = ys[f] + masked(col[0:cz], 1)
        q[f, 1 : cz + 1, 24, :] = yn[f] + masked(col[cz : 2 * cz], 2)
        q[f, 0, 8:24, :] = zd[f] + masked(col[2 * cz : 2 * cz + cy], 3)
        q[f, cz + 1, 8:24, :] = zu[f] + masked(col[2 * cz + cy :], 4)

    def fill(z, carry):
        t = target[pl.ds(pl.multiple_of(z * cy, cy), cy), :]
        for f in range(NF):
            q[f, z + 1, 8:24, :] = base[f, z] + push * t[:, f : f + 1]
        return carry

    lax.fori_loop(0, cz, fill, 0, unroll=2)
    xg = ghosts_x(xw, xe)

    def body(z, carry):
        damp = solid[z] * (1.0 / penalty)
        t = target[pl.ds(pl.multiple_of(z * cy, cy), cy), :]
        cs, rs = slab_rates(q, xg, damp, relax_row, z)
        for f in range(NF):
            r = rs[f] + relax_row * t[:, f : f + 1]
            out[f, z] = 0.5 * (fields[f, z] + cs[f] + time_step * r)
        return carry

    lax.fori_loop(0, cz, body, 0)

    pressure = jnp.reshape(out[3], (cz * cy, 128))
    p_hi = pressure.astype(jnp.bfloat16)
    rest = pressure - p_hi.astype(jnp.float32)
    p_mid = rest.astype(jnp.bfloat16)
    p_lo = (rest - p_mid.astype(jnp.float32)).astype(jnp.bfloat16)
    get_geom.wait()
    get_strips.wait()
    count = cells.shape[1]
    step = 512
    forces = jnp.zeros((8, shapes.shape[1]), jnp.float32)
    for at in range(0, count, step):
        where = cells[:, at : at + step]
        rows = lax.broadcasted_iota(jnp.int32, (cz * cy, step), 0)
        hit = jnp.where(rows == (where >> 7), 1.0, 0.0).astype(jnp.bfloat16)
        picked = jnp.zeros((128, step), jnp.float32)
        for part in (p_hi, p_mid, p_lo):
            picked = picked + lax.dot_general(
                part, hit, (((0,), (0,)), ((), ())), preferred_element_type=jnp.float32
            )
        lanes = lax.broadcasted_iota(jnp.int32, (128, step), 0)
        sample = jnp.sum(jnp.where(lanes == (where & 127), picked, 0.0), axis=0, keepdims=True)
        traction = sample * geom_v[:, at : at + step]
        traction = jnp.concatenate(
            [traction, jnp.zeros((8 - traction.shape[0], step), jnp.float32)], axis=0
        )
        strip = lax.broadcasted_iota(jnp.int32, (shapes.shape[1], step), 0)
        member = jnp.where(strip == strips_v[:, at : at + step], 1.0, 0.0)
        forces = forces + mdot(traction, member, ((1,), (1,)))
    total = jnp.zeros((1, shapes.shape[2]), jnp.float32)
    for c in range(shapes.shape[0]):
        total = total + mdot(forces[c : c + 1], shapes[c], ((1,), (0,)))
    total = jnp.concatenate(
        [total, jnp.zeros((1, 128 - shapes.shape[2]), jnp.float32)], axis=1
    )
    modal[...] = jnp.broadcast_to(total, modal.shape)


def f32(*shape):
    return jax.ShapeDtypeStruct(shape, jnp.float32)


VM = pl.BlockSpec(memory_space=pltpu.VMEM)
SM = pl.BlockSpec(memory_space=pltpu.SMEM)
AN = pl.BlockSpec(memory_space=pl.ANY)
BIG = pltpu.CompilerParams(vmem_limit_bytes=40 * 1024 * 1024)


def swap_faces(faces):
    xf, ylo, yhi, zlo, zhi = faces

    def moved(block, axis, up):
        count = lax.axis_size(axis)
        pairs = [(i, i + 1) for i in range(count - 1)]
        if not up:
            pairs = [(b, a) for a, b in pairs]
        return lax.ppermute(block, axis, pairs)

    return (
        moved(xf, "stream", True),
        moved(xf, "stream", False),
        moved(yhi, "span", True),
        moved(ylo, "span", False),
        moved(zhi, "vert", True),
        moved(zlo, "vert", False),
    )


def on_device(
    fields, solid_frac, panels, panel_owner, deck_cells, deck_geom, strip_ids, mode_shapes
):
    cz, cy, cx = fields.shape[1:]
    n_stream = lax.axis_size("stream")
    n_span = lax.axis_size("span")
    n_vert = lax.axis_size("vert")
    stream_pos = lax.axis_index("stream")
    span_pos = lax.axis_index("span")
    vert_pos = lax.axis_index("vert")
    tiles = n_span * n_vert
    spec = panels.shape[2] // 2
    plane, edges, turn = wave_tables(cz, cy, n_span, n_vert, spec)
    spots = np.arange(cx)
    relax_np = np.where(spots < cx // 2, np.exp(-spots / relax_depth) / relax_time, 0.0)
    relax = jnp.where(stream_pos == 0, jnp.asarray(relax_np, jnp.float32), 0.0).reshape(1, cx)
    flags = jnp.stack(
        [
            span_pos,
            (span_pos > 0).astype(jnp.int32),
            (span_pos < n_span - 1).astype(jnp.int32),
            (vert_pos > 0).astype(jnp.int32),
            (vert_pos < n_vert - 1).astype(jnp.int32),
        ]
    ).astype(jnp.int32)

    def panel_kernel(*refs):
        sum_panels(n_vert, *refs)

    sent = pl.pallas_call(
        panel_kernel,
        out_shape=f32(tiles * ROWS, 128),
        in_specs=[VM] * 4,
        out_specs=VM,
        compiler_params=BIG,
        name="panel_sums",
    )(panels, panel_owner, jnp.asarray(turn), jnp.asarray(edges))
    got = lax.all_to_all(
        sent.reshape(tiles, ROWS, 128), ("span", "vert"), 0, 0, tiled=True
    )
    face_shapes = (
        f32(NF, 8, 128),
        f32(NF, cz, cx),
        f32(NF, cz, cx),
        f32(NF, cy, cx),
        f32(NF, cy, cx),
    )
    faces = pl.pallas_call(
        pack_faces,
        out_shape=face_shapes,
        in_specs=[VM],
        out_specs=(VM,) * 5,
        compiler_params=BIG,
        name="pack_faces",
    )(fields)
    ghosts = swap_faces(faces)
    scratch = pltpu.VMEM((NF, cz + 2, 32, cx), jnp.float32)
    base, *faces = pl.pallas_call(
        first_step,
        out_shape=(f32(NF, cz, cy, cx),) + face_shapes,
        in_specs=[VM] * 9,
        out_specs=(VM,) * 6,
        scratch_shapes=[scratch],
        compiler_params=BIG,
        name="first_step",
    )(fields, solid_frac, *ghosts, relax)
    ghosts = swap_faces(faces)
    summed = pl.pallas_call(
        sum_sources,
        out_shape=f32(n_stream, ROWS, 128),
        in_specs=[VM],
        out_specs=VM,
        compiler_params=BIG,
        name="sum_sources",
    )(got)
    coeffs = lax.all_to_all(summed, "stream", 0, 0, tiled=True)
    deck = deck_cells.shape[3]
    new_fields, modal = pl.pallas_call(
        second_step,
        out_shape=(f32(NF, cz, cy, cx), f32(tiles, 128)),
        in_specs=[SM] + [VM] * 13 + [AN, AN, VM],
        out_specs=(VM, VM),
        scratch_shapes=[
            scratch,
            pltpu.VMEM((cz * cy, 8), jnp.float32),
            pltpu.VMEM((3, deck), jnp.float32),
            pltpu.VMEM((1, deck), jnp.int32),
            pltpu.SemaphoreType.DMA((2,)),
        ],
        compiler_params=BIG,
        name="second_step",
    )(
        flags,
        coeffs,
        jnp.asarray(plane),
        fields,
        base,
        solid_frac,
        *ghosts,
        relax,
        deck_cells.reshape(1, deck),
        deck_geom,
        strip_ids,
        mode_shapes,
    )
    part = lax.all_to_all(modal, ("span", "vert"), 0, 0, tiled=True)
    part = jnp.broadcast_to(jnp.sum(part, axis=0, keepdims=True), (n_stream, 128))
    part = lax.all_to_all(part, "stream", 0, 0, tiled=True)
    modal_force = jnp.sum(part, axis=0)[: mode_shapes.shape[2]]
    return (new_fields, modal_force)


def solution(mesh):
    return jax.shard_map(
        on_device,
        mesh=mesh,
        in_specs=(
            P(None, "vert", "span", "stream"),
            P("vert", "span", "stream"),
            P(("stream", "span", "vert"), None, None),
            P(("stream", "span", "vert"), None),
            P("vert", "span", "stream", None),
            P("vert", None, "stream", None, None),
            P("vert", None, "stream", None),
            P(),
        ),
        out_specs=(P(None, "vert", "span", "stream"), P()),
        check_vma=False,
    )
```

```python
import math

import jax
import jax.numpy as jnp
import numpy as np
from jax import lax
from jax.experimental import pallas as pl
from jax.experimental.pallas import tpu as pltpu
from jax.sharding import PartitionSpec as P

time_step = 0.15
viscous = 0.05
heat_diff = 0.03
sound_sq = 1.0
buoyant = 0.5
penalty = 0.5
relax_time = 0.5
relax_depth = 8.0
wave_cols = 16

HI = lax.Precision.HIGHEST
NF = 5
ROWS = 16


def mdot(a, b, dims):
    return lax.dot_general(
        a, b, (dims, ((), ())), precision=HI, preferred_element_type=jnp.float32
    )


def wave_tables(cz, cy, n_span, n_vert, spec):
    modes = np.arange(spec)
    across = (modes % wave_cols).astype(np.float64)
    upward = (modes // wave_cols).astype(np.float64)
    ny, nz = cy * n_span, cz * n_vert

    def basis(z, y):
        turn = across[None] * y[:, None] / ny + upward[None] * z[:, None] / nz
        angle = 2.0 * math.pi * turn
        return np.concatenate([np.cos(angle), np.sin(angle)], axis=1)

    z, y = np.arange(cz, dtype=np.float64), np.arange(cy, dtype=np.float64)
    plane = basis(np.repeat(z, cy), np.tile(y, cz)).astype(np.float32)
    edges = np.zeros((2 * spec, 128), np.float64)
    at = 0
    for part in (
        basis(z, 0 * z + cy - 1),
        basis(z, 0 * z),
        basis(0 * y + cz - 1, y),
        basis(0 * y, y),
    ):
        edges[:, at : at + part.shape[0]] = part.T
        at += part.shape[0]
    s, v = np.repeat(np.arange(n_span), n_vert), np.tile(np.arange(n_vert), n_span)
    turn = basis(1.0 * v * cz, 1.0 * s * cy).astype(np.float32)
    return plane, edges.astype(np.float32), turn


def sum_panels(panels, owner, turn, edge_table, out):
    n_vert = lax.axis_size("vert")
    tiles = turn.shape[0]
    spec = turn.shape[1] // 2
    held = owner.shape[1]
    named = (owner[...] == lax.broadcasted_iota(jnp.int32, (tiles, held), 0)).astype(jnp.float32)
    cos_t, sin_t = turn[:, :spec], turn[:, spec:]
    lane = lax.broadcasted_iota(jnp.int32, (tiles, 128), 1)
    for f in range(NF):
        total = mdot(named, panels[f], ((1,), (0,)))
        c, s = total[:, :spec], total[:, spec:]
        c2 = c * cos_t + s * sin_t
        s2 = s * cos_t - c * sin_t
        out[pl.ds(f, tiles, stride=ROWS), :] = c2
        out[pl.ds(8 + f, tiles, stride=ROWS), :] = s2
        e = mdot(c2, edge_table[:spec, :], ((1,), (0,))) + mdot(
            s2, edge_table[spec:, :], ((1,), (0,))
        )
        row = jnp.where(
            lane < 32,
            jnp.roll(e, n_vert, 0),
            jnp.where(
                lane < 64,
                jnp.roll(e, -n_vert, 0),
                jnp.where(lane < 80, jnp.roll(e, 1, 0), jnp.roll(e, -1, 0)),
            ),
        )
        at = 5 + f if f < 3 else 10 + f
        out[pl.ds(at, tiles, stride=ROWS), :] = row
    out[pl.ds(15, tiles, stride=ROWS), :] = jnp.zeros((tiles, 128), jnp.float32)


def lane_ids(shape):
    return lax.broadcasted_iota(jnp.int32, shape, len(shape) - 1)


INNER = 8


def packed_x(acc, v, zi):
    lane = lane_ids((8, 128))
    for h in range(2):
        k = 2 * zi + h
        acc = jnp.where((lane >> 1) == k, pltpu.roll(v[8 * h : 8 * h + 8], 2 * k + 1, 1), acc)
    return acc


def placed(whole, part, zo):
    width = 4 * INNER
    lane = lane_ids((8, 128))
    return jnp.where(lane // width == zo, pltpu.roll(part, zo * width, 1), whole)


def face_choice(axis):
    return lax.rem(lax.axis_index(axis), 2) == 0


def store_faces(state, ye, yo, ze, zo):
    cz, cy = state.shape[1], state.shape[2]
    y_low, z_low = face_choice("span"), face_choice("vert")
    for f in range(NF):
        low, high = state[f, :, 0, :], state[f, :, cy - 1, :]
        ye[f] = jnp.where(y_low, high, low)
        yo[f] = jnp.where(y_low, low, high)
        low, high = state[f, 0], state[f, cz - 1]
        ze[f] = jnp.where(z_low, high, low)
        zo[f] = jnp.where(z_low, low, high)


def pack_faces(fields, xf, ye, yo, ze, zo):
    cz = fields.shape[1]
    zero = jnp.zeros((8, 128), jnp.float32)

    def body(g, accs):
        new = []
        for f in range(NF):
            part = zero
            for i in range(INNER):
                part = packed_x(part, fields[f, g * INNER + i], i)
            new.append(placed(accs[f], part, g))
        return tuple(new)

    accs = lax.fori_loop(0, cz // INNER, body, (zero,) * NF)
    for f in range(NF):
        xf[f] = accs[f]
    store_faces(fields, ye, yo, ze, zo)


def fill_ghosts(q, ye, yo, ze, zo, extra=None):
    cz = q.shape[1] - 2
    y_low, z_low = face_choice("span"), face_choice("vert")
    for f in range(NF):
        south = jnp.where(y_low, yo[f], ye[f])
        north = jnp.where(y_low, ye[f], yo[f])
        down = jnp.where(z_low, zo[f], ze[f])
        up = jnp.where(z_low, ze[f], zo[f])
        if extra is not None:
            es, en, ed, eu = extra(f)
            south, north, down, up = south + es, north + en, down + ed, up + eu
        q[f, 1 : cz + 1, 7, :] = south
        q[f, 1 : cz + 1, 24, :] = north
        q[f, 0, 8:24, :] = down
        q[f, cz + 1, 8:24, :] = up


def ghosts_x(west, east):
    lane = lane_ids((8, 128))
    return [jnp.where((lane & 1) == 0, west[f], pltpu.roll(east[f], 126, 1)) for f in range(NF)]


def slab_rates(q, xg, damp2, decay, z, zi):
    lane = lane_ids((16, 128))
    first, last = lane == 0, lane == 127
    cs, dx, dy, dz, rs = [], [], [], [], []
    for f in range(NF):
        c = q[f, z + 1, 8:24, :]
        up, down = q[f, z + 2, 8:24, :], q[f, z, 8:24, :]
        north, south = q[f, z + 1, 9:25, :], q[f, z + 1, 7:23, :]
        side = jnp.concatenate(
            [
                pltpu.roll(xg[f], (128 - 4 * zi) % 128, 1),
                pltpu.roll(xg[f], (126 - 4 * zi) % 128, 1),
            ],
            axis=0,
        )
        west = jnp.where(first, side, pltpu.roll(c, 1, 1))
        east = jnp.where(last, side, pltpu.roll(c, 127, 1))
        nu = heat_diff if f == 4 else viscous
        around = (east + west) + (north + south) + (up + down)
        cs.append(c)
        dx.append(east - west)
        dy.append(north - south)
        dz.append(up - down)
        rs.append(nu * around - decay[f == 4] * c)
    hu, hv, hw = 0.5 * cs[0], 0.5 * cs[1], 0.5 * cs[2]
    out = []
    for f in range(NF):
        r = rs[f] - (hu * dx[f] + hv * dy[f] + hw * dz[f])
        if f == 0:
            r = r - 0.5 * dx[3] - damp2 * hu
        elif f == 1:
            r = r - 0.5 * dy[3] - damp2 * hv
        elif f == 2:
            r = r - 0.5 * dz[3] - damp2 * hw + buoyant * cs[4]
        elif f == 3:
            r = r - (0.5 * sound_sq) * (dx[0] + dy[1] + dz[2])
        out.append(r)
    return cs, out


def relax_weights(cx):
    lane = lane_ids((1, cx))
    weight = jnp.exp(lane.astype(jnp.float32) * (-1.0 / relax_depth)) / relax_time
    return jnp.where((lax.axis_index("stream") == 0) & (lane < cx // 2), weight, 0.0)


def first_step(got, fields, solid, xe, xo, ye, yo, ze, zo, base, carry_out, ye1, yo1, ze1, zo1, q):
    cz = fields.shape[1]
    fill_ghosts(q, ye, yo, ze, zo)

    def fill(z, carry):
        for f in range(NF):
            q[f, z + 1, 8:24, :] = fields[f, z]
        return carry

    lax.fori_loop(0, cz, fill, 0, unroll=4)
    x_low = face_choice("stream")
    xg = ghosts_x(
        [jnp.where(x_low, xo[f], xe[f]) for f in range(NF)],
        [jnp.where(x_low, xe[f], xo[f]) for f in range(NF)],
    )
    relax = relax_weights(fields.shape[3])
    decay = (6.0 * viscous + relax, 6.0 * heat_diff + relax)
    zero = jnp.zeros((8, 128), jnp.float32)

    def body(g, accs):
        turned = [pltpu.roll(xg[f], (128 - 4 * INNER * g) & 127, 1) for f in range(NF)]
        parts = [zero] * NF
        for i in range(INNER):
            z = g * INNER + i
            damp2 = solid[z] * (2.0 / penalty)
            cs, rs = slab_rates(q, turned, damp2, decay, z, i)
            for f in range(NF):
                b = cs[f] + time_step * rs[f]
                base[f, z] = b
                parts[f] = packed_x(parts[f], b, i)
        return tuple(placed(accs[f], parts[f], g) for f in range(NF))

    accs = lax.fori_loop(0, cz // INNER, body, (zero,) * NF)
    total = got[0:ROWS]
    for i in range(1, got.shape[0] // ROWS):
        total = total + got[ROWS * i : ROWS * i + ROWS]
    for i in range(carry_out.shape[0]):
        carry_out[i, 0:ROWS] = total
        for f in range(NF):
            carry_out[i, ROWS + 8 * f : ROWS + 8 * f + 8] = accs[f]
    store_faces(base, ye1, yo1, ze1, zo1)


def second_step(
    carried,
    plane_table,
    fields,
    base,
    solid,
    ye,
    yo,
    ze,
    zo,
    cells,
    geom,
    strips,
    shapes,
    out,
    modal,
    q,
    target,
    geom_v,
    strips_v,
    sems,
):
    cz, cy, cx = fields.shape[1:]
    spec = plane_table.shape[1] // 2
    n_stream = carried.shape[0]
    span_pos = lax.axis_index("span")
    vert_pos = lax.axis_index("vert")
    stream_pos = lax.axis_index("stream")
    get_geom = pltpu.make_async_copy(geom.at[0, span_pos], geom_v, sems.at[0])
    get_strips = pltpu.make_async_copy(strips.at[0, span_pos], strips_v, sems.at[1])
    get_geom.start()
    get_strips.start()
    low, high = carried[0, 0:8], carried[0, 8:16]
    for i in range(1, n_stream):
        low = low + carried[i, 0:8]
        high = high + carried[i, 8:16]
    one = jnp.where(lane_ids((1, 8)) == 0, 1.0, 0.0)
    target[...] = (
        mdot(plane_table[:, :spec], low, ((1,), (1,)))
        + mdot(plane_table[:, spec:], high, ((1,), (1,)))
        + one
    )
    n_edge = 2 * cz + 2 * cy
    pick = (
        lax.broadcasted_iota(jnp.int32, (n_edge, 128), 0) == lane_ids((n_edge, 128))
    ).astype(jnp.float32)
    e_low = mdot(pick, low, ((1,), (1,)))
    e_high = mdot(pick, high, ((1,), (1,)))
    relax = relax_weights(cx)
    decay = (6.0 * viscous + relax, 6.0 * heat_diff + relax)
    push = time_step * relax

    def edge_push(f):
        col = e_low[:, 5 + f : 6 + f] if f < 3 else e_high[:, 2 + f : 3 + f]
        if f == 0:
            col = col + 1.0
        col = col * push
        return (
            jnp.where(span_pos > 0, col[0:cz], 0.0),
            jnp.where(span_pos < lax.axis_size("span") - 1, col[cz : 2 * cz], 0.0),
            jnp.where(vert_pos > 0, col[2 * cz : 2 * cz + cy], 0.0),
            jnp.where(vert_pos < lax.axis_size("vert") - 1, col[2 * cz + cy :], 0.0),
        )

    fill_ghosts(q, ye, yo, ze, zo, edge_push)

    def fill(g, carry):
        for i in range(4):
            z = g * 4 + i
            t = target[pl.ds(pl.multiple_of(z * cy, cy), cy), :]
            for f in range(NF):
                pushed = push * t[:, f : f + 1]
                q[f, z + 1, 8:24, :] = base[f, z] + pushed
                out[f, z] = fields[f, z] + pushed
        return carry

    lax.fori_loop(0, cz // 4, fill, 0)
    west_at = jnp.maximum(stream_pos - 1, 0)
    east_at = jnp.minimum(stream_pos + 1, n_stream - 1)
    west, east = [], []
    for f in range(NF):
        rows = slice(ROWS + 8 * f, ROWS + 8 * f + 8)
        west.append(jnp.where(stream_pos > 0, carried[west_at, rows], 0.0))
        east.append(jnp.where(stream_pos < n_stream - 1, carried[east_at, rows], 0.0))
    xg = ghosts_x(west, east)

    def body(g, carry):
        turned = [pltpu.roll(xg[f], (128 - 4 * INNER * g) & 127, 1) for f in range(NF)]
        for i in range(INNER):
            z = g * INNER + i
            damp2 = solid[z] * (2.0 / penalty)
            cs, rs = slab_rates(q, turned, damp2, decay, z, i)
            for f in range(NF):
                out[f, z] = 0.5 * (out[f, z] + cs[f] + time_step * rs[f])
        return carry

    lax.fori_loop(0, cz // INNER, body, 0)

    pressure = jnp.transpose(jnp.reshape(out[3], (cz * cy, cx)))
    p_hi = pressure.astype(jnp.bfloat16)
    p_lo = (pressure - p_hi.astype(jnp.float32)).astype(jnp.bfloat16)
    parts = jnp.concatenate([p_hi, p_lo], axis=0)
    get_geom.wait()
    get_strips.wait()
    count = cells.shape[1]
    step = 512
    n_comp = geom_v.shape[0]
    forces = jnp.zeros((8, shapes.shape[2]), jnp.float32)
    for at in range(0, count, step):
        where = cells[:, at : at + step]
        rows = lax.broadcasted_iota(jnp.int32, (cz * cy, step), 0)
        hit = jnp.where(rows == (where >> 7), 1.0, 0.0).astype(jnp.bfloat16)
        picked = lax.dot_general(
            parts, hit, (((1,), (0,)), ((), ())), preferred_element_type=jnp.float32
        )
        picked = picked[:cx] + picked[cx:]
        lanes = lax.broadcasted_iota(jnp.int32, (cx, step), 0)
        sample = jnp.sum(jnp.where(lanes == (where & 127), picked, 0.0), axis=0, keepdims=True)
        traction = jnp.concatenate(
            [sample * geom_v[c, :, at : at + step] for c in range(n_comp)]
            + [jnp.zeros((8 - n_comp, step), jnp.float32)],
            axis=0,
        )
        strip = lax.broadcasted_iota(jnp.int32, (shapes.shape[2], step), 0)
        member = jnp.where(strip == strips_v[:, at : at + step], 1.0, 0.0)
        forces = forces + mdot(traction, member, ((1,), (1,)))
    total = jnp.zeros((1, shapes.shape[1]), jnp.float32)
    for c in range(n_comp):
        total = total + mdot(forces[c : c + 1], shapes[c], ((1,), (1,)))
    total = jnp.concatenate(
        [total, jnp.zeros((1, 128 - shapes.shape[1]), jnp.float32)], axis=1
    )
    modal[...] = jnp.broadcast_to(total, modal.shape)


def f32(*shape):
    return jax.ShapeDtypeStruct(shape, jnp.float32)


VM = pl.BlockSpec(memory_space=pltpu.VMEM)
AN = pl.BlockSpec(memory_space=pl.ANY)
BIG = pltpu.CompilerParams(vmem_limit_bytes=16 * 1024 * 1024)


def swapped(block, axis, odd):
    pairs = []
    for i in range(odd, lax.axis_size(axis) - 1, 2):
        pairs += [(i, i + 1), (i + 1, i)]
    return lax.ppermute(block, axis, pairs)


def on_device(
    fields, solid_frac, panels, panel_owner, deck_cells, deck_geom, strip_ids, mode_shapes
):
    cz, cy, cx = fields.shape[1:]
    n_stream = lax.axis_size("stream")
    n_span = lax.axis_size("span")
    n_vert = lax.axis_size("vert")
    tiles = n_span * n_vert
    spec = panels.shape[2] // 2
    plane, edges, turn = wave_tables(cz, cy, n_span, n_vert, spec)
    sent = pl.pallas_call(
        sum_panels,
        out_shape=f32(tiles * ROWS, 128),
        compiler_params=BIG,
        name="panel_sums",
    )(
        panels.transpose(1, 0, 2),
        panel_owner.reshape(1, -1),
        jnp.asarray(turn),
        jnp.asarray(edges),
    )
    got = lax.all_to_all(
        sent.reshape(tiles, ROWS, 128), ("span", "vert"), 0, 0, tiled=True
    ).reshape(tiles * ROWS, 128)
    yz_shapes = (f32(NF, cz, cx), f32(NF, cz, cx), f32(NF, cy, cx), f32(NF, cy, cx))

    def swap_yz(ye, yo, ze, zo):
        return (
            swapped(ye, "span", 0),
            swapped(yo, "span", 1),
            swapped(ze, "vert", 0),
            swapped(zo, "vert", 1),
        )

    xf, *faces = pl.pallas_call(
        pack_faces,
        out_shape=(f32(NF, 8, 128),) + yz_shapes,
        in_specs=[VM],
        out_specs=(VM,) * 5,
        compiler_params=BIG,
        name="pack_faces",
    )(fields)
    ghosts = (swapped(xf, "stream", 0), swapped(xf, "stream", 1)) + swap_yz(*faces)
    scratch = pltpu.VMEM((NF, cz + 2, 32, cx), jnp.float32)
    base, carry, *faces = pl.pallas_call(
        first_step,
        out_shape=(f32(NF, cz, cy, cx), f32(n_stream, ROWS + 8 * NF, 128)) + yz_shapes,
        in_specs=[VM] * 9,
        out_specs=(VM,) * 6,
        scratch_shapes=[scratch],
        compiler_params=BIG,
        name="first_step",
    )(got, fields, solid_frac, *ghosts)
    carried = lax.all_to_all(carry, "stream", 0, 0, tiled=True)
    ghosts = swap_yz(*faces)
    deck = deck_cells.shape[3]
    new_fields, modal = pl.pallas_call(
        second_step,
        out_shape=(f32(NF, cz, cy, cx), f32(tiles, 128)),
        in_specs=[VM] * 10 + [AN, AN, VM],
        out_specs=(VM, VM),
        scratch_shapes=[
            scratch,
            pltpu.VMEM((cz * cy, 8), jnp.float32),
            pltpu.VMEM((3, 1, deck), jnp.float32),
            pltpu.VMEM((1, deck), jnp.int32),
            pltpu.SemaphoreType.DMA((2,)),
        ],
        compiler_params=BIG,
        name="second_step",
    )(
        carried,
        jnp.asarray(plane),
        fields,
        base,
        solid_frac,
        *ghosts,
        deck_cells.reshape(1, deck),
        deck_geom.transpose(0, 1, 3, 2, 4),
        strip_ids,
        mode_shapes.transpose(0, 2, 1),
    )
    part = lax.all_to_all(modal, ("span", "vert"), 0, 0, tiled=True)
    part = jnp.broadcast_to(jnp.sum(part, axis=0, keepdims=True), (n_stream, 128))
    part = lax.all_to_all(part, "stream", 0, 0, tiled=True)
    modal_force = jnp.sum(part, axis=0)[: mode_shapes.shape[2]]
    return (new_fields, modal_force)


def solution(mesh):
    return jax.shard_map(
        on_device,
        mesh=mesh,
        in_specs=(
            P(None, "vert", "span", "stream"),
            P("vert", "span", "stream"),
            P(("stream", "span", "vert"), None, None),
            P(("stream", "span", "vert"), None),
            P("vert", "span", "stream", None),
            P("vert", None, "stream", None, None),
            P("vert", None, "stream", None),
            P(),
        ),
        out_specs=(P(None, "vert", "span", "stream"), P()),
        check_vma=False,
    )
```

```python
import math

import jax
import jax.numpy as jnp
import numpy as np
from jax import lax
from jax.experimental import pallas as pl
from jax.experimental.pallas import tpu as pltpu
from jax.sharding import PartitionSpec as P

time_step = 0.15
viscous = 0.05
heat_diff = 0.03
sound_sq = 1.0
buoyant = 0.5
penalty = 0.5
relax_time = 0.5
relax_depth = 8.0
wave_cols = 16

HI = lax.Precision.HIGHEST
NF = 5
ROWS = 16


def mdot(a, b, dims):
    return lax.dot_general(
        a, b, (dims, ((), ())), precision=HI, preferred_element_type=jnp.float32
    )


def wave_tables(cz, cy, n_span, n_vert, spec):
    modes = np.arange(spec)
    across = (modes % wave_cols).astype(np.float64)
    upward = (modes // wave_cols).astype(np.float64)
    ny, nz = cy * n_span, cz * n_vert

    def basis(z, y):
        turn = across[None] * y[:, None] / ny + upward[None] * z[:, None] / nz
        angle = 2.0 * math.pi * turn
        return np.concatenate([np.cos(angle), np.sin(angle)], axis=1)

    z, y = np.arange(cz, dtype=np.float64), np.arange(cy, dtype=np.float64)
    plane = basis(np.repeat(z, cy), np.tile(y, cz)).astype(np.float32)
    edges = np.zeros((2 * spec, 128), np.float64)
    at = 0
    for part in (
        basis(z, 0 * z + cy - 1),
        basis(z, 0 * z),
        basis(0 * y + cz - 1, y),
        basis(0 * y, y),
    ):
        edges[:, at : at + part.shape[0]] = part.T
        at += part.shape[0]
    s, v = np.repeat(np.arange(n_span), n_vert), np.tile(np.arange(n_vert), n_span)
    turn = basis(1.0 * v * cz, 1.0 * s * cy).astype(np.float32)
    return plane, edges.astype(np.float32), turn


def fetch(sources, targets, sems, at=0):
    copies = [
        pltpu.make_async_copy(a, b, sems.at[at + i])
        for i, (a, b) in enumerate(zip(sources, targets))
    ]
    for c in copies:
        c.start()
    return copies


def wait_all(copies):
    for c in copies:
        c.wait()


def sum_panels(panels_h, owner_h, turn_h, edge_h, out, panels, owner, turn, edge_table, sems):
    wait_all(
        fetch((panels_h, owner_h, turn_h, edge_h), (panels, owner, turn, edge_table), sems)
    )
    n_vert = lax.axis_size("vert")
    tiles = turn.shape[0]
    spec = turn.shape[1] // 2
    held = owner.shape[1]
    named = (owner[...] == lax.broadcasted_iota(jnp.int32, (tiles, held), 0)).astype(jnp.float32)
    cos_t, sin_t = turn[:, :spec], turn[:, spec:]
    lane = lax.broadcasted_iota(jnp.int32, (tiles, 128), 1)
    for f in range(NF):
        total = mdot(named, panels[f], ((1,), (0,)))
        c, s = total[:, :spec], total[:, spec:]
        c2 = c * cos_t + s * sin_t
        s2 = s * cos_t - c * sin_t
        out[pl.ds(f, tiles, stride=ROWS), :] = c2
        out[pl.ds(8 + f, tiles, stride=ROWS), :] = s2
        e = mdot(c2, edge_table[:spec, :], ((1,), (0,))) + mdot(
            s2, edge_table[spec:, :], ((1,), (0,))
        )
        row = jnp.where(
            lane < 32,
            jnp.roll(e, n_vert, 0),
            jnp.where(
                lane < 64,
                jnp.roll(e, -n_vert, 0),
                jnp.where(lane < 80, jnp.roll(e, 1, 0), jnp.roll(e, -1, 0)),
            ),
        )
        at = 5 + f if f < 3 else 10 + f
        out[pl.ds(at, tiles, stride=ROWS), :] = row
    out[pl.ds(15, tiles, stride=ROWS), :] = jnp.zeros((tiles, 128), jnp.float32)


def lane_ids(shape):
    return lax.broadcasted_iota(jnp.int32, shape, len(shape) - 1)


INNER = 8


def packed_x(acc, v, zi):
    lane = lane_ids((8, 128))
    for h in range(2):
        k = 2 * zi + h
        acc = jnp.where((lane >> 1) == k, pltpu.roll(v[8 * h : 8 * h + 8], 2 * k + 1, 1), acc)
    return acc


def placed(whole, part, zo):
    width = 4 * INNER
    lane = lane_ids((8, 128))
    return jnp.where(lane // width == zo, pltpu.roll(part, zo * width, 1), whole)


def face_choice(axis):
    return lax.rem(lax.axis_index(axis), 2) == 0


def store_faces(state, ye, yo, ze, zo):
    cz, cy = state.shape[1], state.shape[2]
    y_low, z_low = face_choice("span"), face_choice("vert")
    for f in range(NF):
        low, high = state[f, :, 0, :], state[f, :, cy - 1, :]
        ye[f] = jnp.where(y_low, high, low)
        yo[f] = jnp.where(y_low, low, high)
        low, high = state[f, 0], state[f, cz - 1]
        ze[f] = jnp.where(z_low, high, low)
        zo[f] = jnp.where(z_low, low, high)


def pack_faces(fields, xf, ye, yo, ze, zo):
    cz = fields.shape[1]
    zero = jnp.zeros((8, 128), jnp.float32)

    def body(g, accs):
        new = []
        for f in range(NF):
            part = zero
            for i in range(INNER):
                part = packed_x(part, fields[f, g * INNER + i], i)
            new.append(placed(accs[f], part, g))
        return tuple(new)

    accs = lax.fori_loop(0, cz // INNER, body, (zero,) * NF)
    for f in range(NF):
        xf[f] = accs[f]
    store_faces(fields, ye, yo, ze, zo)


def fill_ghosts(q, ye, yo, ze, zo, extra=None):
    cz = q.shape[1] - 2
    y_low, z_low = face_choice("span"), face_choice("vert")
    for f in range(NF):
        south = jnp.where(y_low, yo[f], ye[f])
        north = jnp.where(y_low, ye[f], yo[f])
        down = jnp.where(z_low, zo[f], ze[f])
        up = jnp.where(z_low, ze[f], zo[f])
        if extra is not None:
            es, en, ed, eu = extra(f)
            south, north, down, up = south + es, north + en, down + ed, up + eu
        q[f, 1 : cz + 1, 7, :] = south
        q[f, 1 : cz + 1, 24, :] = north
        q[f, 0, 8:24, :] = down
        q[f, cz + 1, 8:24, :] = up


def ghosts_x(west, east):
    lane = lane_ids((8, 128))
    return [jnp.where((lane & 1) == 0, west[f], pltpu.roll(east[f], 126, 1)) for f in range(NF)]


def slab_rates(q, xg, damp2, decay, z, zi):
    lane = lane_ids((16, 128))
    first, last = lane == 0, lane == 127
    cs, dx, dy, dz, rs = [], [], [], [], []
    for f in range(NF):
        c = q[f, z + 1, 8:24, :]
        up, down = q[f, z + 2, 8:24, :], q[f, z, 8:24, :]
        north, south = q[f, z + 1, 9:25, :], q[f, z + 1, 7:23, :]
        side = jnp.concatenate(
            [
                pltpu.roll(xg[f], (128 - 4 * zi) % 128, 1),
                pltpu.roll(xg[f], (126 - 4 * zi) % 128, 1),
            ],
            axis=0,
        )
        west = jnp.where(first, side, pltpu.roll(c, 1, 1))
        east = jnp.where(last, side, pltpu.roll(c, 127, 1))
        nu = heat_diff if f == 4 else viscous
        around = (east + west) + (north + south) + (up + down)
        cs.append(c)
        dx.append(east - west)
        dy.append(north - south)
        dz.append(up - down)
        rs.append(nu * around - decay[f == 4] * c)
    hu, hv, hw = 0.5 * cs[0], 0.5 * cs[1], 0.5 * cs[2]
    out = []
    for f in range(NF):
        r = rs[f] - (hu * dx[f] + hv * dy[f] + hw * dz[f])
        if f == 0:
            r = r - 0.5 * dx[3] - damp2 * hu
        elif f == 1:
            r = r - 0.5 * dy[3] - damp2 * hv
        elif f == 2:
            r = r - 0.5 * dz[3] - damp2 * hw + buoyant * cs[4]
        elif f == 3:
            r = r - (0.5 * sound_sq) * (dx[0] + dy[1] + dz[2])
        out.append(r)
    return cs, out


def relax_weights(cx):
    lane = lane_ids((1, cx))
    weight = jnp.exp(lane.astype(jnp.float32) * (-1.0 / relax_depth)) / relax_time
    return jnp.where((lax.axis_index("stream") == 0) & (lane < cx // 2), weight, 0.0)


def first_step(*refs):
    fields, solid = refs[:2]
    arrived, base, sent = refs[2:9], refs[9], refs[10:15]
    q, kept, leaving, sems = refs[15], refs[16:23], refs[23:28], refs[28]
    got, xe, xo, ye, yo, ze, zo = kept
    carry_out, ye1, yo1, ze1, zo1 = leaving
    cz = fields.shape[1]
    coming = fetch(arrived, kept, sems)

    def fill(z, carry):
        for f in range(NF):
            q[f, z + 1, 8:24, :] = fields[f, z]
        return carry

    lax.fori_loop(0, cz, fill, 0, unroll=4)
    wait_all(coming)
    fill_ghosts(q, ye, yo, ze, zo)
    x_low = face_choice("stream")
    xg = ghosts_x(
        [jnp.where(x_low, xo[f], xe[f]) for f in range(NF)],
        [jnp.where(x_low, xe[f], xo[f]) for f in range(NF)],
    )
    relax = relax_weights(fields.shape[3])
    decay = (6.0 * viscous + relax, 6.0 * heat_diff + relax)
    zero = jnp.zeros((8, 128), jnp.float32)

    def body(g, accs):
        turned = [pltpu.roll(xg[f], (128 - 4 * INNER * g) & 127, 1) for f in range(NF)]
        parts = [zero] * NF
        for i in range(INNER):
            z = g * INNER + i
            damp2 = solid[z] * (2.0 / penalty)
            cs, rs = slab_rates(q, turned, damp2, decay, z, i)
            for f in range(NF):
                b = cs[f] + time_step * rs[f]
                base[f, z] = b
                parts[f] = packed_x(parts[f], b, i)
        return tuple(placed(accs[f], parts[f], g) for f in range(NF))

    accs = lax.fori_loop(0, cz // INNER, body, (zero,) * NF)
    total = got[0:ROWS]
    for i in range(1, got.shape[0] // ROWS):
        total = total + got[ROWS * i : ROWS * i + ROWS]
    for i in range(carry_out.shape[0]):
        carry_out[i, 0:ROWS] = total
        for f in range(NF):
            carry_out[i, ROWS + 8 * f : ROWS + 8 * f + 8] = accs[f]
    store_faces(base, ye1, yo1, ze1, zo1)
    wait_all(fetch(leaving, sent, sems))


def second_step(*refs):
    fields, base, solid = refs[:3]
    arrived, late = refs[3:9], refs[9:13]
    out, modal, q, target = refs[13:17]
    kept, late_kept, sems = refs[17:23], refs[23:27], refs[27]
    carried, plane_table, ye, yo, ze, zo = kept
    cells, geom_v, strips_v, shapes = late_kept
    cz, cy, cx = fields.shape[1:]
    spec = plane_table.shape[1] // 2
    n_stream = carried.shape[0]
    span_pos = lax.axis_index("span")
    vert_pos = lax.axis_index("vert")
    stream_pos = lax.axis_index("stream")
    coming = fetch(arrived, kept, sems)
    cells_h, geom_h, strips_h, shapes_h = late
    rest = fetch(
        (cells_h, geom_h.at[0, span_pos], strips_h.at[0, span_pos], shapes_h),
        late_kept,
        sems,
        len(coming),
    )

    wait_all(coming)
    low, high = carried[0, 0:8], carried[0, 8:16]
    for i in range(1, n_stream):
        low = low + carried[i, 0:8]
        high = high + carried[i, 8:16]
    one = jnp.where(lane_ids((1, 8)) == 0, 1.0, 0.0)
    target[...] = (
        mdot(plane_table[:, :spec], low, ((1,), (1,)))
        + mdot(plane_table[:, spec:], high, ((1,), (1,)))
        + one
    )
    n_edge = 2 * cz + 2 * cy
    pick = (
        lax.broadcasted_iota(jnp.int32, (n_edge, 128), 0) == lane_ids((n_edge, 128))
    ).astype(jnp.float32)
    e_low = mdot(pick, low, ((1,), (1,)))
    e_high = mdot(pick, high, ((1,), (1,)))
    relax = relax_weights(cx)
    decay = (6.0 * viscous + relax, 6.0 * heat_diff + relax)
    push = time_step * relax

    def edge_push(f):
        col = e_low[:, 5 + f : 6 + f] if f < 3 else e_high[:, 2 + f : 3 + f]
        if f == 0:
            col = col + 1.0
        col = col * push
        return (
            jnp.where(span_pos > 0, col[0:cz], 0.0),
            jnp.where(span_pos < lax.axis_size("span") - 1, col[cz : 2 * cz], 0.0),
            jnp.where(vert_pos > 0, col[2 * cz : 2 * cz + cy], 0.0),
            jnp.where(vert_pos < lax.axis_size("vert") - 1, col[2 * cz + cy :], 0.0),
        )

    fill_ghosts(q, ye, yo, ze, zo, edge_push)

    def pushing(g, carry):
        for i in range(4):
            z = g * 4 + i
            t = target[pl.ds(pl.multiple_of(z * cy, cy), cy), :]
            for f in range(NF):
                pushed = push * t[:, f : f + 1]
                q[f, z + 1, 8:24, :] = base[f, z] + pushed
                out[f, z] = fields[f, z] + pushed
        return carry

    lax.fori_loop(0, cz // 4, pushing, 0)
    west_at = jnp.maximum(stream_pos - 1, 0)
    east_at = jnp.minimum(stream_pos + 1, n_stream - 1)
    west, east = [], []
    for f in range(NF):
        rows = slice(ROWS + 8 * f, ROWS + 8 * f + 8)
        west.append(jnp.where(stream_pos > 0, carried[west_at, rows], 0.0))
        east.append(jnp.where(stream_pos < n_stream - 1, carried[east_at, rows], 0.0))
    xg = ghosts_x(west, east)

    def body(g, carry):
        turned = [pltpu.roll(xg[f], (128 - 4 * INNER * g) & 127, 1) for f in range(NF)]
        for i in range(INNER):
            z = g * INNER + i
            damp2 = solid[z] * (2.0 / penalty)
            cs, rs = slab_rates(q, turned, damp2, decay, z, i)
            for f in range(NF):
                out[f, z] = 0.5 * (out[f, z] + cs[f] + time_step * rs[f])
        return carry

    lax.fori_loop(0, cz // INNER, body, 0)

    pressure = jnp.transpose(jnp.reshape(out[3], (cz * cy, cx)))
    p_hi = pressure.astype(jnp.bfloat16)
    p_lo = (pressure - p_hi.astype(jnp.float32)).astype(jnp.bfloat16)
    parts = jnp.concatenate([p_hi, p_lo], axis=0)
    wait_all(rest)
    count = cells.shape[1]
    step = 512
    n_comp = geom_v.shape[0]
    forces = jnp.zeros((8, shapes.shape[2]), jnp.float32)
    for at in range(0, count, step):
        where = cells[:, at : at + step]
        rows = lax.broadcasted_iota(jnp.int32, (cz * cy, step), 0)
        hit = jnp.where(rows == (where >> 7), 1.0, 0.0).astype(jnp.bfloat16)
        picked = lax.dot_general(
            parts, hit, (((1,), (0,)), ((), ())), preferred_element_type=jnp.float32
        )
        picked = picked[:cx] + picked[cx:]
        lanes = lax.broadcasted_iota(jnp.int32, (cx, step), 0)
        sample = jnp.sum(jnp.where(lanes == (where & 127), picked, 0.0), axis=0, keepdims=True)
        traction = jnp.concatenate(
            [sample * geom_v[c, :, at : at + step] for c in range(n_comp)]
            + [jnp.zeros((8 - n_comp, step), jnp.float32)],
            axis=0,
        )
        strip = lax.broadcasted_iota(jnp.int32, (shapes.shape[2], step), 0)
        member = jnp.where(strip == strips_v[:, at : at + step], 1.0, 0.0)
        forces = forces + mdot(traction, member, ((1,), (1,)))
    total = jnp.zeros((1, shapes.shape[1]), jnp.float32)
    for c in range(n_comp):
        total = total + mdot(forces[c : c + 1], shapes[c], ((1,), (1,)))
    total = jnp.concatenate(
        [total, jnp.zeros((1, 128 - shapes.shape[1]), jnp.float32)], axis=1
    )
    modal[...] = jnp.broadcast_to(total, modal.shape)


def f32(*shape):
    return jax.ShapeDtypeStruct(shape, jnp.float32)


VM = pl.BlockSpec(memory_space=pltpu.VMEM)
HB = pl.BlockSpec(memory_space=pltpu.HBM)


def room(mib):
    return pltpu.CompilerParams(vmem_limit_bytes=mib * 1024 * 1024)


def buffers(arrays):
    return [pltpu.VMEM(x.shape, x.dtype) for x in arrays]


def swapped(block, axis, odd):
    pairs = []
    for i in range(odd, lax.axis_size(axis) - 1, 2):
        pairs += [(i, i + 1), (i + 1, i)]
    return lax.ppermute(block, axis, pairs)


def on_device(
    fields, solid_frac, panels, panel_owner, deck_cells, deck_geom, strip_ids, mode_shapes
):
    cz, cy, cx = fields.shape[1:]
    n_stream = lax.axis_size("stream")
    n_span = lax.axis_size("span")
    n_vert = lax.axis_size("vert")
    tiles = n_span * n_vert
    spec = panels.shape[2] // 2
    plane, edges, turn = wave_tables(cz, cy, n_span, n_vert, spec)
    operands = (
        panels.transpose(1, 0, 2),
        panel_owner.reshape(1, -1),
        jnp.asarray(turn),
        jnp.asarray(edges),
    )
    sent = pl.pallas_call(
        sum_panels,
        out_shape=f32(tiles * ROWS, 128),
        in_specs=[HB] * 4,
        out_specs=VM,
        scratch_shapes=buffers(operands) + [pltpu.SemaphoreType.DMA((4,))],
        compiler_params=room(60),
        name="panel_sums",
    )(*operands)
    got = lax.all_to_all(
        sent.reshape(tiles, ROWS, 128), ("span", "vert"), 0, 0, tiled=True
    ).reshape(tiles * ROWS, 128)
    yz_shapes = (f32(NF, cz, cx), f32(NF, cz, cx), f32(NF, cy, cx), f32(NF, cy, cx))

    def swap_yz(ye, yo, ze, zo):
        return (
            swapped(ye, "span", 0),
            swapped(yo, "span", 1),
            swapped(ze, "vert", 0),
            swapped(zo, "vert", 1),
        )

    xf, *faces = pl.pallas_call(
        pack_faces,
        out_shape=(f32(NF, 8, 128),) + yz_shapes,
        in_specs=[VM],
        out_specs=(VM,) * 5,
        compiler_params=room(52),
        name="pack_faces",
    )(fields)
    ghosts = (swapped(xf, "stream", 0), swapped(xf, "stream", 1)) + swap_yz(*faces)
    scratch = pltpu.VMEM((NF, cz + 2, 32, cx), jnp.float32)
    arrived = (got,) + ghosts
    leaving = (f32(n_stream, ROWS + 8 * NF, 128),) + yz_shapes
    base, carry, *faces = pl.pallas_call(
        first_step,
        out_shape=(f32(NF, cz, cy, cx),) + leaving,
        in_specs=[VM] * 2 + [HB] * 7,
        out_specs=(VM,) + (HB,) * 5,
        scratch_shapes=[scratch]
        + buffers(arrived)
        + buffers(leaving)
        + [pltpu.SemaphoreType.DMA((7,))],
        compiler_params=room(52),
        name="first_step",
    )(fields, solid_frac, *arrived)
    carried = lax.all_to_all(carry, "stream", 0, 0, tiled=True)
    ghosts = swap_yz(*faces)
    deck = deck_cells.shape[3]
    arrived = (carried, jnp.asarray(plane)) + ghosts
    cells = deck_cells.reshape(1, deck)
    shapes = mode_shapes.transpose(0, 2, 1)
    new_fields, modal = pl.pallas_call(
        second_step,
        out_shape=(f32(NF, cz, cy, cx), f32(tiles, 128)),
        in_specs=[VM] * 3 + [HB] * 10,
        out_specs=(VM, VM),
        scratch_shapes=[scratch, pltpu.VMEM((cz * cy, 8), jnp.float32)]
        + buffers(arrived)
        + buffers((cells, f32(3, 1, deck), strip_ids[0, 0], shapes))
        + [pltpu.SemaphoreType.DMA((10,))],
        compiler_params=room(52),
        name="second_step",
    )(
        fields,
        base,
        solid_frac,
        *arrived,
        cells,
        deck_geom.transpose(0, 1, 3, 2, 4),
        strip_ids,
        shapes,
    )
    part = lax.all_to_all(modal, ("span", "vert"), 0, 0, tiled=True)
    part = jnp.broadcast_to(jnp.sum(part, axis=0, keepdims=True), (n_stream, 128))
    part = lax.all_to_all(part, "stream", 0, 0, tiled=True)
    modal_force = jnp.sum(part, axis=0)[: mode_shapes.shape[2]]
    return (new_fields, modal_force)


def solution(mesh):
    return jax.shard_map(
        on_device,
        mesh=mesh,
        in_specs=(
            P(None, "vert", "span", "stream"),
            P("vert", "span", "stream"),
            P(("stream", "span", "vert"), None, None),
            P(("stream", "span", "vert"), None),
            P("vert", "span", "stream", None),
            P("vert", None, "stream", None, None),
            P("vert", None, "stream", None),
            P(),
        ),
        out_specs=(P(None, "vert", "span", "stream"), P()),
        check_vma=False,
    )
```

```python
import math

import jax
import jax.numpy as jnp
import ml_dtypes
import numpy as np
from jax import lax
from jax.experimental import pallas as pl
from jax.experimental.pallas import tpu as pltpu
from jax.sharding import PartitionSpec as P

time_step = 0.15
viscous = 0.05
heat_diff = 0.03
sound_sq = 1.0
buoyant = 0.5
penalty = 0.5
relax_time = 0.5
relax_depth = 8.0
wave_cols = 16

HI = lax.Precision.HIGHEST
NF = 5
ROWS = 16


def mdot(a, b, dims):
    return lax.dot_general(
        a, b, (dims, ((), ())), precision=HI, preferred_element_type=jnp.float32
    )


def split_np(a):
    hi = a.astype(ml_dtypes.bfloat16)
    return hi, (a - hi.astype(np.float32)).astype(ml_dtypes.bfloat16)


def split(a):
    hi = a.astype(jnp.bfloat16)
    return hi, (a - hi.astype(jnp.float32)).astype(jnp.bfloat16)


def bdot(a, b, dims):
    return lax.dot_general(a, b, (dims, ((), ())), preferred_element_type=jnp.float32)


def wave_tables(cz, cy, n_span, n_vert, spec):
    modes = np.arange(spec)
    across = (modes % wave_cols).astype(np.float64)
    upward = (modes // wave_cols).astype(np.float64)
    ny, nz = cy * n_span, cz * n_vert

    def basis(z, y):
        turn = across[None] * y[:, None] / ny + upward[None] * z[:, None] / nz
        angle = 2.0 * math.pi * turn
        return np.concatenate([np.cos(angle), np.sin(angle)], axis=1)

    z, y = np.arange(cz, dtype=np.float64), np.arange(cy, dtype=np.float64)
    plane = basis(np.repeat(z, cy), np.tile(y, cz)).astype(np.float32)
    edges = np.zeros((2 * spec, 128), np.float64)
    at = 0
    for part in (
        basis(z, 0 * z + cy - 1),
        basis(z, 0 * z),
        basis(0 * y + cz - 1, y),
        basis(0 * y, y),
    ):
        edges[:, at : at + part.shape[0]] = part.T
        at += part.shape[0]
    s, v = np.repeat(np.arange(n_span), n_vert), np.tile(np.arange(n_vert), n_span)
    turn = basis(1.0 * v * cz, 1.0 * s * cy).astype(np.float32)
    hi, lo = split_np(plane)
    plane = np.concatenate([hi, lo, hi], axis=1)
    hi, lo = split_np(edges.astype(np.float32))
    edges = np.concatenate([hi, lo, hi], axis=0)
    return plane, edges, turn


def fetch(sources, targets, sems, at=0):
    copies = [
        pltpu.make_async_copy(a, b, sems.at[at + i])
        for i, (a, b) in enumerate(zip(sources, targets))
    ]
    for c in copies:
        c.start()
    return copies


def wait_all(copies):
    for c in copies:
        c.wait()


def sum_panels(panels_h, owner_h, turn_h, edge_h, out, panels, owner, turn, edge_table, sems):
    wait_all(
        fetch((panels_h, owner_h, turn_h, edge_h), (panels, owner, turn, edge_table), sems)
    )
    n_vert = lax.axis_size("vert")
    tiles = turn.shape[0]
    spec = turn.shape[1] // 2
    held = owner.shape[1]
    named = jnp.where(
        owner[...] == lax.broadcasted_iota(jnp.int32, (tiles, held), 0), 1.0, 0.0
    ).astype(jnp.bfloat16)
    named = jnp.concatenate([named, named], axis=1)
    cos_t, sin_t = turn[:, :spec], turn[:, spec:]
    turned = []
    for f in range(NF):
        total = bdot(named, jnp.concatenate(split(panels[f]), axis=0), ((1,), (0,)))
        c, s = total[:, :spec], total[:, spec:]
        c2 = c * cos_t + s * sin_t
        s2 = s * cos_t - c * sin_t
        out[pl.ds(f, tiles, stride=ROWS), :] = c2
        out[pl.ds(8 + f, tiles, stride=ROWS), :] = s2
        turned.append(jnp.concatenate([c2, s2], axis=1))
    hi, lo = split(jnp.concatenate(turned, axis=0))
    edge = bdot(jnp.concatenate([hi, hi, lo], axis=1), edge_table[...], ((1,), (0,)))
    lane = lax.broadcasted_iota(jnp.int32, (tiles, 128), 1)
    for f in range(NF):
        e = edge[f * tiles : (f + 1) * tiles]
        row = jnp.where(
            lane < 32,
            jnp.roll(e, n_vert, 0),
            jnp.where(
                lane < 64,
                jnp.roll(e, -n_vert, 0),
                jnp.where(lane < 80, jnp.roll(e, 1, 0), jnp.roll(e, -1, 0)),
            ),
        )
        at = 5 + f if f < 3 else 10 + f
        out[pl.ds(at, tiles, stride=ROWS), :] = row
    out[pl.ds(15, tiles, stride=ROWS), :] = jnp.zeros((tiles, 128), jnp.float32)


def lane_ids(shape):
    return lax.broadcasted_iota(jnp.int32, shape, len(shape) - 1)


INNER = 8


def packed_x(acc, v, zi):
    lane = lane_ids((8, 128))
    for h in range(2):
        k = 2 * zi + h
        acc = jnp.where((lane >> 1) == k, pltpu.roll(v[8 * h : 8 * h + 8], 2 * k + 1, 1), acc)
    return acc


def placed(whole, part, zo):
    width = 4 * INNER
    lane = lane_ids((8, 128))
    return jnp.where(lane // width == zo, pltpu.roll(part, zo * width, 1), whole)


def face_choice(axis):
    return lax.rem(lax.axis_index(axis), 2) == 0


def store_faces(state, ye, yo, ze, zo):
    cz, cy = state.shape[1], state.shape[2]
    y_low, z_low = face_choice("span"), face_choice("vert")
    for f in range(NF):
        low, high = state[f, :, 0, :], state[f, :, cy - 1, :]
        ye[f] = jnp.where(y_low, high, low)
        yo[f] = jnp.where(y_low, low, high)
        low, high = state[f, 0], state[f, cz - 1]
        ze[f] = jnp.where(z_low, high, low)
        zo[f] = jnp.where(z_low, low, high)


def pack_faces(fields, xf, ye, yo, ze, zo):
    cz = fields.shape[1]
    zero = jnp.zeros((8, 128), jnp.float32)

    def body(g, accs):
        new = []
        for f in range(NF):
            part = zero
            for i in range(INNER):
                part = packed_x(part, fields[f, g * INNER + i], i)
            new.append(placed(accs[f], part, g))
        return tuple(new)

    accs = lax.fori_loop(0, cz // INNER, body, (zero,) * NF)
    for f in range(NF):
        xf[f] = accs[f]
    store_faces(fields, ye, yo, ze, zo)


def fill_ghosts(q, ye, yo, ze, zo, extra=None):
    cz = q.shape[1] - 2
    y_low, z_low = face_choice("span"), face_choice("vert")
    for f in range(NF):
        south = jnp.where(y_low, yo[f], ye[f])
        north = jnp.where(y_low, ye[f], yo[f])
        down = jnp.where(z_low, zo[f], ze[f])
        up = jnp.where(z_low, ze[f], zo[f])
        if extra is not None:
            es, en, ed, eu = extra(f)
            south, north, down, up = south + es, north + en, down + ed, up + eu
        q[f, 1 : cz + 1, 7, :] = south
        q[f, 1 : cz + 1, 24, :] = north
        q[f, 0, 8:24, :] = down
        q[f, cz + 1, 8:24, :] = up


def ghosts_x(west, east):
    lane = lane_ids((8, 128))
    return [jnp.where((lane & 1) == 0, west[f], pltpu.roll(east[f], 126, 1)) for f in range(NF)]


def slab_rates(q, xg, damp2, decay, z, zi):
    lane = lane_ids((16, 128))
    first, last = lane == 0, lane == 127
    cs, dx, dy, dz, rs = [], [], [], [], []
    for f in range(NF):
        c = q[f, z + 1, 8:24, :]
        up, down = q[f, z + 2, 8:24, :], q[f, z, 8:24, :]
        north, south = q[f, z + 1, 9:25, :], q[f, z + 1, 7:23, :]
        side = jnp.concatenate(
            [
                pltpu.roll(xg[f], (128 - 4 * zi) % 128, 1),
                pltpu.roll(xg[f], (126 - 4 * zi) % 128, 1),
            ],
            axis=0,
        )
        west = jnp.where(first, side, pltpu.roll(c, 1, 1))
        east = jnp.where(last, side, pltpu.roll(c, 127, 1))
        nu = heat_diff if f == 4 else viscous
        around = (east + west) + (north + south) + (up + down)
        cs.append(c)
        dx.append(east - west)
        dy.append(north - south)
        dz.append(up - down)
        rs.append(nu * around - decay[f == 4] * c)
    hu, hv, hw = 0.5 * cs[0], 0.5 * cs[1], 0.5 * cs[2]
    out = []
    for f in range(NF):
        r = rs[f] - (hu * dx[f] + hv * dy[f] + hw * dz[f])
        if f == 0:
            r = r - 0.5 * dx[3] - damp2 * hu
        elif f == 1:
            r = r - 0.5 * dy[3] - damp2 * hv
        elif f == 2:
            r = r - 0.5 * dz[3] - damp2 * hw + buoyant * cs[4]
        elif f == 3:
            r = r - (0.5 * sound_sq) * (dx[0] + dy[1] + dz[2])
        out.append(r)
    return cs, out


def relax_weights(cx):
    lane = lane_ids((1, cx))
    weight = jnp.exp(lane.astype(jnp.float32) * (-1.0 / relax_depth)) / relax_time
    return jnp.where((lax.axis_index("stream") == 0) & (lane < cx // 2), weight, 0.0)


def first_step(*refs):
    fields, solid = refs[:2]
    arrived, base_out, sent = refs[2:9], refs[9], refs[10:15]
    q, kept, leaving, base, sems, base_sems = refs[15], refs[16:23], refs[23:28], *refs[28:31]
    got, xe, xo, ye, yo, ze, zo = kept
    carry_out, ye1, yo1, ze1, zo1 = leaving
    cz = fields.shape[1]
    coming = fetch(arrived, kept, sems)

    def fill(z, carry):
        for f in range(NF):
            q[f, z + 1, 8:24, :] = fields[f, z]
        return carry

    lax.fori_loop(0, cz, fill, 0, unroll=4)
    wait_all(coming[1:])
    fill_ghosts(q, ye, yo, ze, zo)
    x_low = face_choice("stream")
    xg = ghosts_x(
        [jnp.where(x_low, xo[f], xe[f]) for f in range(NF)],
        [jnp.where(x_low, xe[f], xo[f]) for f in range(NF)],
    )
    relax = relax_weights(fields.shape[3])
    decay = (6.0 * viscous + relax, 6.0 * heat_diff + relax)
    zero = jnp.zeros((8, 128), jnp.float32)

    def body(g, accs):
        turned = [pltpu.roll(xg[f], (128 - 4 * INNER * g) & 127, 1) for f in range(NF)]
        parts = [zero] * NF
        for i in range(INNER):
            z = g * INNER + i
            damp2 = solid[z] * (2.0 / penalty)
            cs, rs = slab_rates(q, turned, damp2, decay, z, i)
            for f in range(NF):
                b = cs[f] + time_step * rs[f]
                base[f, z] = b
                parts[f] = packed_x(parts[f], b, i)
        chunk = pl.ds(pl.multiple_of(g * INNER, INNER), INNER)
        pltpu.make_async_copy(base.at[:, chunk], base_out.at[:, chunk], base_sems.at[g]).start()
        return tuple(placed(accs[f], parts[f], g) for f in range(NF))

    accs = lax.fori_loop(0, cz // INNER, body, (zero,) * NF)
    store_faces(base, ye1, yo1, ze1, zo1)
    going = fetch(leaving[1:], sent[1:], sems, 1)
    coming[0].wait()
    total = got[0:ROWS]
    for i in range(1, got.shape[0] // ROWS):
        total = total + got[ROWS * i : ROWS * i + ROWS]
    for i in range(carry_out.shape[0]):
        carry_out[i, 0:ROWS] = total
        for f in range(NF):
            carry_out[i, ROWS + 8 * f : ROWS + 8 * f + 8] = accs[f]
    wait_all(going + fetch(leaving[:1], sent[:1], sems))
    for g in range(cz // INNER):
        chunk = pl.ds(g * INNER, INNER)
        pltpu.make_async_copy(base.at[:, chunk], base_out.at[:, chunk], base_sems.at[g]).wait()


def second_step(*refs):
    fields, solid, base = refs[:3]
    arrived, late = refs[3:9], refs[9:13]
    out_h, modal, q, target = refs[13:17]
    kept, late_kept, out, sems, out_sems = refs[17:23], refs[23:27], *refs[27:30]
    carried, plane_table, ye, yo, ze, zo = kept
    cells, geom_v, strips_v, shapes = late_kept
    cz, cy, cx = fields.shape[1:]
    n_stream = carried.shape[0]
    span_pos = lax.axis_index("span")
    vert_pos = lax.axis_index("vert")
    stream_pos = lax.axis_index("stream")
    coming = fetch(arrived, kept, sems)
    get_base = pltpu.make_async_copy(base, q.at[:, 1 : cz + 1, 8:24, :], out_sems.at[0])
    get_base.start()
    cells_h, geom_h, strips_h, shapes_h = late
    rest = fetch(
        (cells_h, geom_h.at[0, span_pos], strips_h.at[0, span_pos], shapes_h),
        late_kept,
        sems,
        len(coming),
    )

    wait_all(coming[:2])
    low, high = carried[0, 0:8], carried[0, 8:16]
    for i in range(1, n_stream):
        low = low + carried[i, 0:8]
        high = high + carried[i, 8:16]
    one = jnp.where(lane_ids((1, 8)) == 0, 1.0, 0.0)
    hi, lo = split(jnp.concatenate([low, high], axis=1))
    target[...] = (
        bdot(plane_table[...], jnp.concatenate([hi, hi, lo], axis=1), ((1,), (1,))) + one
    )
    n_edge = 2 * cz + 2 * cy
    pick = (
        lax.broadcasted_iota(jnp.int32, (n_edge, 128), 0) == lane_ids((n_edge, 128))
    ).astype(jnp.bfloat16)
    pick = jnp.concatenate([pick, pick], axis=1)
    e_low = bdot(pick, jnp.concatenate(split(low), axis=1), ((1,), (1,)))
    e_high = bdot(pick, jnp.concatenate(split(high), axis=1), ((1,), (1,)))
    relax = relax_weights(cx)
    decay = (6.0 * viscous + relax, 6.0 * heat_diff + relax)
    push = time_step * relax

    def edge_push(f):
        col = e_low[:, 5 + f : 6 + f] if f < 3 else e_high[:, 2 + f : 3 + f]
        if f == 0:
            col = col + 1.0
        col = col * push
        return (
            jnp.where(span_pos > 0, col[0:cz], 0.0),
            jnp.where(span_pos < lax.axis_size("span") - 1, col[cz : 2 * cz], 0.0),
            jnp.where(vert_pos > 0, col[2 * cz : 2 * cz + cy], 0.0),
            jnp.where(vert_pos < lax.axis_size("vert") - 1, col[2 * cz + cy :], 0.0),
        )

    wait_all(coming[2:])
    fill_ghosts(q, ye, yo, ze, zo, edge_push)
    get_base.wait()

    def pushing(g, carry):
        for i in range(4):
            z = g * 4 + i
            t = target[pl.ds(pl.multiple_of(z * cy, cy), cy), :]
            for f in range(NF):
                pushed = push * t[:, f : f + 1]
                q[f, z + 1, 8:24, :] = q[f, z + 1, 8:24, :] + pushed
                out[f, z] = fields[f, z] + pushed
        return carry

    lax.fori_loop(0, cz // 4, pushing, 0)
    west_at = jnp.maximum(stream_pos - 1, 0)
    east_at = jnp.minimum(stream_pos + 1, n_stream - 1)
    west, east = [], []
    for f in range(NF):
        rows = slice(ROWS + 8 * f, ROWS + 8 * f + 8)
        west.append(jnp.where(stream_pos > 0, carried[west_at, rows], 0.0))
        east.append(jnp.where(stream_pos < n_stream - 1, carried[east_at, rows], 0.0))
    xg = ghosts_x(west, east)

    def body(g, carry):
        turned = [pltpu.roll(xg[f], (128 - 4 * INNER * g) & 127, 1) for f in range(NF)]
        for i in range(INNER):
            z = g * INNER + i
            damp2 = solid[z] * (2.0 / penalty)
            cs, rs = slab_rates(q, turned, damp2, decay, z, i)
            for f in range(NF):
                out[f, z] = 0.5 * (out[f, z] + cs[f] + time_step * rs[f])
        chunk = pl.ds(pl.multiple_of(g * INNER, INNER), INNER)
        pltpu.make_async_copy(out.at[:, chunk], out_h.at[:, chunk], out_sems.at[g + 1]).start()
        return carry

    lax.fori_loop(0, cz // INNER, body, 0)

    pressure = jnp.transpose(jnp.reshape(out[3], (cz * cy, cx)))
    p_hi = pressure.astype(jnp.bfloat16)
    p_lo = (pressure - p_hi.astype(jnp.float32)).astype(jnp.bfloat16)
    parts = jnp.concatenate([p_hi, p_lo], axis=0)
    wait_all(rest)
    count = cells.shape[1]
    step = 512
    n_comp = geom_v.shape[0]
    own = shapes.shape[2] // lax.axis_size("span")
    sums = [jnp.zeros((8, 128), jnp.float32)] * own
    for at in range(0, count, step):
        where = cells[:, at : at + step]
        rows = lax.broadcasted_iota(jnp.int32, (cz * cy, step), 0)
        hit = jnp.where(rows == (where >> 7), 1.0, 0.0).astype(jnp.bfloat16)
        picked = bdot(parts, hit, ((1,), (0,)))
        picked = picked[:cx] + picked[cx:]
        lanes = lax.broadcasted_iota(jnp.int32, (cx, step), 0)
        sample = jnp.sum(jnp.where(lanes == (where & 127), picked, 0.0), axis=0, keepdims=True)
        traction = jnp.concatenate(
            [sample * geom_v[c, :, at : at + step] for c in range(n_comp)]
            + [jnp.zeros((8 - n_comp, step), jnp.float32)],
            axis=0,
        )
        strip = strips_v[:, at : at + step] - span_pos * own
        for j in range(own):
            mine = jnp.where(strip == j, traction, 0.0)
            for k in range(0, step, 128):
                sums[j] = sums[j] + mine[:, k : k + 128]
    lane = lane_ids((8, shapes.shape[2]))
    spread = jnp.zeros((8, shapes.shape[2]), jnp.float32)
    for j in range(own):
        force = jnp.sum(sums[j], axis=1, keepdims=True)
        spread = jnp.where(lane == span_pos * own + j, force, spread)
    total = jnp.zeros(shapes.shape[1:], jnp.float32)
    for c in range(n_comp):
        total = total + shapes[c] * spread[c : c + 1]
    total = mdot(jnp.ones((8, shapes.shape[2]), jnp.float32), total, ((1,), (1,)))[0:1]
    total = jnp.concatenate(
        [total, jnp.zeros((1, 128 - shapes.shape[1]), jnp.float32)], axis=1
    )
    modal[...] = jnp.broadcast_to(total, modal.shape)
    for g in range(cz // INNER):
        chunk = pl.ds(g * INNER, INNER)
        pltpu.make_async_copy(out.at[:, chunk], out_h.at[:, chunk], out_sems.at[g + 1]).wait()


def f32(*shape):
    return jax.ShapeDtypeStruct(shape, jnp.float32)


VM = pl.BlockSpec(memory_space=pltpu.VMEM)
HB = pl.BlockSpec(memory_space=pltpu.HBM)


def room(mib):
    return pltpu.CompilerParams(vmem_limit_bytes=mib * 1024 * 1024)


def buffers(arrays):
    return [pltpu.VMEM(x.shape, x.dtype) for x in arrays]


def swapped(block, axis, odd):
    pairs = []
    for i in range(odd, lax.axis_size(axis) - 1, 2):
        pairs += [(i, i + 1), (i + 1, i)]
    return lax.ppermute(block, axis, pairs)


def on_device(
    fields, solid_frac, panels, panel_owner, deck_cells, deck_geom, strip_ids, mode_shapes
):
    cz, cy, cx = fields.shape[1:]
    n_stream = lax.axis_size("stream")
    n_span = lax.axis_size("span")
    n_vert = lax.axis_size("vert")
    tiles = n_span * n_vert
    spec = panels.shape[2] // 2
    plane, edges, turn = wave_tables(cz, cy, n_span, n_vert, spec)
    operands = (
        panels.transpose(1, 0, 2),
        panel_owner.reshape(1, -1),
        jnp.asarray(turn),
        jnp.asarray(edges),
    )
    sent = pl.pallas_call(
        sum_panels,
        out_shape=f32(tiles * ROWS, 128),
        in_specs=[HB] * 4,
        out_specs=VM,
        scratch_shapes=buffers(operands) + [pltpu.SemaphoreType.DMA((4,))],
        compiler_params=room(60),
        name="panel_sums",
    )(*operands)
    got = lax.all_to_all(
        sent.reshape(tiles, ROWS, 128), ("span", "vert"), 0, 0, tiled=True
    ).reshape(tiles * ROWS, 128)
    yz_shapes = (f32(NF, cz, cx), f32(NF, cz, cx), f32(NF, cy, cx), f32(NF, cy, cx))

    def swap_yz(ye, yo, ze, zo):
        return (
            swapped(ye, "span", 0),
            swapped(yo, "span", 1),
            swapped(ze, "vert", 0),
            swapped(zo, "vert", 1),
        )

    xf, *faces = pl.pallas_call(
        pack_faces,
        out_shape=(f32(NF, 8, 128),) + yz_shapes,
        in_specs=[VM],
        out_specs=(VM,) * 5,
        compiler_params=room(52),
        name="pack_faces",
    )(fields)
    ghosts = (swapped(xf, "stream", 0), swapped(xf, "stream", 1)) + swap_yz(*faces)
    scratch = pltpu.VMEM((NF, cz + 2, 32, cx), jnp.float32)
    arrived = (got,) + ghosts
    leaving = (f32(n_stream, ROWS + 8 * NF, 128),) + yz_shapes
    base, carry, *faces = pl.pallas_call(
        first_step,
        out_shape=(f32(NF, cz, cy, cx),) + leaving,
        in_specs=[VM] * 2 + [HB] * 7,
        out_specs=(HB,) * 6,
        scratch_shapes=[scratch]
        + buffers(arrived)
        + buffers(leaving)
        + [pltpu.VMEM((NF, cz, cy, cx), jnp.float32)]
        + [pltpu.SemaphoreType.DMA((7,)), pltpu.SemaphoreType.DMA((cz // INNER,))],
        compiler_params=room(52),
        name="first_step",
    )(fields, solid_frac, *arrived)
    carried = lax.all_to_all(carry, "stream", 0, 0, tiled=True)
    ghosts = swap_yz(*faces)
    deck = deck_cells.shape[3]
    arrived = (carried, jnp.asarray(plane)) + ghosts
    cells = deck_cells.reshape(1, deck)
    shapes = mode_shapes.transpose(0, 2, 1)
    new_fields, modal = pl.pallas_call(
        second_step,
        out_shape=(f32(NF, cz, cy, cx), f32(tiles, 128)),
        in_specs=[VM] * 2 + [HB] * 11,
        out_specs=(HB, VM),
        scratch_shapes=[scratch, pltpu.VMEM((cz * cy, 8), jnp.float32)]
        + buffers(arrived)
        + buffers((cells, f32(3, 1, deck), strip_ids[0, 0], shapes))
        + [pltpu.VMEM((NF, cz, cy, cx), jnp.float32)]
        + [pltpu.SemaphoreType.DMA((10,)), pltpu.SemaphoreType.DMA((cz // INNER + 1,))],
        compiler_params=room(52),
        name="second_step",
    )(
        fields,
        solid_frac,
        base,
        *arrived,
        cells,
        deck_geom.transpose(0, 1, 3, 2, 4),
        strip_ids,
        shapes,
    )
    part = lax.all_to_all(modal, ("span", "vert"), 0, 0, tiled=True)
    part = jnp.broadcast_to(jnp.sum(part, axis=0, keepdims=True), (n_stream, 128))
    part = lax.all_to_all(part, "stream", 0, 0, tiled=True)
    modal_force = jnp.sum(part, axis=0)[: mode_shapes.shape[2]]
    return (new_fields, modal_force)


def solution(mesh):
    return jax.shard_map(
        on_device,
        mesh=mesh,
        in_specs=(
            P(None, "vert", "span", "stream"),
            P("vert", "span", "stream"),
            P(("stream", "span", "vert"), None, None),
            P(("stream", "span", "vert"), None),
            P("vert", "span", "stream", None),
            P("vert", None, "stream", None, None),
            P("vert", None, "stream", None),
            P(),
        ),
        out_specs=(P(None, "vert", "span", "stream"), P()),
        check_vma=False,
    )
```

```python
import math

import jax
import jax.numpy as jnp
import ml_dtypes
import numpy as np
from jax import lax
from jax.experimental import pallas as pl
from jax.experimental.pallas import tpu as pltpu
from jax.sharding import PartitionSpec as P

time_step = 0.15
viscous = 0.05
heat_diff = 0.03
sound_sq = 1.0
buoyant = 0.5
penalty = 0.5
relax_time = 0.5
relax_depth = 8.0
wave_cols = 16

HI = lax.Precision.HIGHEST
NF = 5
ROWS = 16


def mdot(a, b, dims):
    return lax.dot_general(
        a, b, (dims, ((), ())), precision=HI, preferred_element_type=jnp.float32
    )


def split_np(a):
    hi = a.astype(ml_dtypes.bfloat16)
    return hi, (a - hi.astype(np.float32)).astype(ml_dtypes.bfloat16)


def split(a):
    hi = a.astype(jnp.bfloat16)
    return hi, (a - hi.astype(jnp.float32)).astype(jnp.bfloat16)


def bdot(a, b, dims):
    return lax.dot_general(a, b, (dims, ((), ())), preferred_element_type=jnp.float32)


def wave_tables(cz, cy, n_span, n_vert, spec):
    modes = np.arange(spec)
    across = (modes % wave_cols).astype(np.float64)
    upward = (modes // wave_cols).astype(np.float64)
    ny, nz = cy * n_span, cz * n_vert

    def basis(z, y):
        turn = across[None] * y[:, None] / ny + upward[None] * z[:, None] / nz
        angle = 2.0 * math.pi * turn
        return np.concatenate([np.cos(angle), np.sin(angle)], axis=1)

    z, y = np.arange(cz, dtype=np.float64), np.arange(cy, dtype=np.float64)
    plane = basis(np.repeat(z, cy), np.tile(y, cz)).astype(np.float32)
    edges = np.zeros((2 * spec, 128), np.float64)
    at = 0
    for part in (
        basis(z, 0 * z + cy - 1),
        basis(z, 0 * z),
        basis(0 * y + cz - 1, y),
        basis(0 * y, y),
    ):
        edges[:, at : at + part.shape[0]] = part.T
        at += part.shape[0]
    s, v = np.repeat(np.arange(n_span), n_vert), np.tile(np.arange(n_vert), n_span)
    turn = basis(1.0 * v * cz, 1.0 * s * cy).astype(np.float32)
    hi, lo = split_np(plane)
    plane = np.concatenate([hi, lo, hi], axis=1)
    hi, lo = split_np(edges.astype(np.float32))
    edges = np.concatenate([hi, lo, hi], axis=0)
    return plane, edges, turn


def fetch(sources, targets, sems, at=0):
    copies = [
        pltpu.make_async_copy(a, b, sems.at[at + i])
        for i, (a, b) in enumerate(zip(sources, targets))
    ]
    for c in copies:
        c.start()
    return copies


def wait_all(copies):
    for c in copies:
        c.wait()


def sum_panels(panels_h, owner_h, turn_h, edge_h, out, panels, owner, turn, edge_table, sems):
    wait_all(
        fetch((panels_h, owner_h, turn_h, edge_h), (panels, owner, turn, edge_table), sems)
    )
    n_vert = lax.axis_size("vert")
    tiles = turn.shape[0]
    spec = turn.shape[1] // 2
    held = owner.shape[1]
    named = jnp.where(
        owner[...] == lax.broadcasted_iota(jnp.int32, (tiles, held), 0), 1.0, 0.0
    ).astype(jnp.bfloat16)
    named = jnp.concatenate([named, named], axis=1)
    cos_t, sin_t = turn[:, :spec], turn[:, spec:]
    turned = []
    for f in range(NF):
        total = bdot(named, jnp.concatenate(split(panels[f]), axis=0), ((1,), (0,)))
        c, s = total[:, :spec], total[:, spec:]
        c2 = c * cos_t + s * sin_t
        s2 = s * cos_t - c * sin_t
        out[pl.ds(f, tiles, stride=ROWS), :] = c2
        out[pl.ds(8 + f, tiles, stride=ROWS), :] = s2
        turned.append(jnp.concatenate([c2, s2], axis=1))
    hi, lo = split(jnp.concatenate(turned, axis=0))
    edge = bdot(jnp.concatenate([hi, hi, lo], axis=1), edge_table[...], ((1,), (0,)))
    lane = lax.broadcasted_iota(jnp.int32, (tiles, 128), 1)
    for f in range(NF):
        e = edge[f * tiles : (f + 1) * tiles]
        row = jnp.where(
            lane < 32,
            jnp.roll(e, n_vert, 0),
            jnp.where(
                lane < 64,
                jnp.roll(e, -n_vert, 0),
                jnp.where(lane < 80, jnp.roll(e, 1, 0), jnp.roll(e, -1, 0)),
            ),
        )
        at = 5 + f if f < 3 else 10 + f
        out[pl.ds(at, tiles, stride=ROWS), :] = row
    out[pl.ds(15, tiles, stride=ROWS), :] = jnp.zeros((tiles, 128), jnp.float32)


def lane_ids(shape):
    return lax.broadcasted_iota(jnp.int32, shape, len(shape) - 1)


INNER = 8


def packed_x(acc, v, zi):
    lane = lane_ids((8, 128))
    for h in range(2):
        k = 2 * zi + h
        acc = jnp.where((lane >> 1) == k, pltpu.roll(v[8 * h : 8 * h + 8], 2 * k + 1, 1), acc)
    return acc


def placed(whole, part, zo):
    width = 4 * INNER
    lane = lane_ids((8, 128))
    return jnp.where(lane // width == zo, pltpu.roll(part, zo * width, 1), whole)


def face_choice(axis):
    return lax.rem(lax.axis_index(axis), 2) == 0


def store_faces(state, ye, yo, ze, zo):
    cz, cy = state.shape[1], state.shape[2]
    y_low, z_low = face_choice("span"), face_choice("vert")
    for f in range(NF):
        low, high = state[f, :, 0, :], state[f, :, cy - 1, :]
        ye[f] = jnp.where(y_low, high, low)
        yo[f] = jnp.where(y_low, low, high)
        low, high = state[f, 0], state[f, cz - 1]
        ze[f] = jnp.where(z_low, high, low)
        zo[f] = jnp.where(z_low, low, high)


def pack_faces(fields, xf, ye, yo, ze, zo):
    cz = fields.shape[1]
    zero = jnp.zeros((8, 128), jnp.float32)

    def body(g, accs):
        new = []
        for f in range(NF):
            part = zero
            for i in range(INNER):
                part = packed_x(part, fields[f, g * INNER + i], i)
            new.append(placed(accs[f], part, g))
        return tuple(new)

    accs = lax.fori_loop(0, cz // INNER, body, (zero,) * NF)
    for f in range(NF):
        xf[f] = accs[f]
    store_faces(fields, ye, yo, ze, zo)


def fill_ghosts(q, ye, yo, ze, zo, extra=None):
    cz = q.shape[1] - 2
    y_low, z_low = face_choice("span"), face_choice("vert")
    for f in range(NF):
        south = jnp.where(y_low, yo[f], ye[f])
        north = jnp.where(y_low, ye[f], yo[f])
        down = jnp.where(z_low, zo[f], ze[f])
        up = jnp.where(z_low, ze[f], zo[f])
        if extra is not None:
            es, en, ed, eu = extra(f)
            south, north, down, up = south + es, north + en, down + ed, up + eu
        q[f, 1 : cz + 1, 7, :] = south
        q[f, 1 : cz + 1, 24, :] = north
        q[f, 0, 8:24, :] = down
        q[f, cz + 1, 8:24, :] = up


def ghosts_x(west, east):
    lane = lane_ids((8, 128))
    return [jnp.where((lane & 1) == 0, west[f], pltpu.roll(east[f], 126, 1)) for f in range(NF)]


def slab_rates(q, xg, damp2, decay, z, zi):
    lane = lane_ids((16, 128))
    first, last = lane == 0, lane == 127
    cs, dx, dy, dz, rs = [], [], [], [], []
    for f in range(NF):
        c = q[f, z + 1, 8:24, :]
        up, down = q[f, z + 2, 8:24, :], q[f, z, 8:24, :]
        north, south = q[f, z + 1, 9:25, :], q[f, z + 1, 7:23, :]
        side = jnp.concatenate(
            [
                pltpu.roll(xg[f], (128 - 4 * zi) % 128, 1),
                pltpu.roll(xg[f], (126 - 4 * zi) % 128, 1),
            ],
            axis=0,
        )
        west = jnp.where(first, side, pltpu.roll(c, 1, 1))
        east = jnp.where(last, side, pltpu.roll(c, 127, 1))
        nu = heat_diff if f == 4 else viscous
        around = (east + west) + (north + south) + (up + down)
        cs.append(c)
        dx.append(east - west)
        dy.append(north - south)
        dz.append(up - down)
        rs.append(nu * around - decay[f == 4] * c)
    hu, hv, hw = 0.5 * cs[0], 0.5 * cs[1], 0.5 * cs[2]
    out = []
    for f in range(NF):
        r = rs[f] - (hu * dx[f] + hv * dy[f] + hw * dz[f])
        if f == 0:
            r = r - 0.5 * dx[3] - damp2 * hu
        elif f == 1:
            r = r - 0.5 * dy[3] - damp2 * hv
        elif f == 2:
            r = r - 0.5 * dz[3] - damp2 * hw + buoyant * cs[4]
        elif f == 3:
            r = r - (0.5 * sound_sq) * (dx[0] + dy[1] + dz[2])
        out.append(r)
    return cs, out


def relax_weights(cx):
    lane = lane_ids((1, cx))
    weight = jnp.exp(lane.astype(jnp.float32) * (-1.0 / relax_depth)) / relax_time
    return jnp.where((lax.axis_index("stream") == 0) & (lane < cx // 2), weight, 0.0)


def first_step(*refs):
    fields, solid = refs[:2]
    got, xe, xo, ye, yo, ze, zo = refs[2:9]
    base_out, carry_out, ye1, yo1, ze1, zo1 = refs[9:15]
    q, base, base_sems = refs[15:18]
    cz = fields.shape[1]

    def fill(z, carry):
        for f in range(NF):
            q[f, z + 1, 8:24, :] = fields[f, z]
        return carry

    lax.fori_loop(0, cz, fill, 0, unroll=4)
    fill_ghosts(q, ye, yo, ze, zo)
    x_low = face_choice("stream")
    xg = ghosts_x(
        [jnp.where(x_low, xo[f], xe[f]) for f in range(NF)],
        [jnp.where(x_low, xe[f], xo[f]) for f in range(NF)],
    )
    relax = relax_weights(fields.shape[3])
    decay = (6.0 * viscous + relax, 6.0 * heat_diff + relax)
    zero = jnp.zeros((8, 128), jnp.float32)

    def body(g, accs):
        turned = [pltpu.roll(xg[f], (128 - 4 * INNER * g) & 127, 1) for f in range(NF)]
        parts = [zero] * NF
        for i in range(INNER):
            z = g * INNER + i
            damp2 = solid[z] * (2.0 / penalty)
            cs, rs = slab_rates(q, turned, damp2, decay, z, i)
            for f in range(NF):
                b = cs[f] + time_step * rs[f]
                base[f, z] = b
                parts[f] = packed_x(parts[f], b, i)
        chunk = pl.ds(pl.multiple_of(g * INNER, INNER), INNER)
        pltpu.make_async_copy(base.at[:, chunk], base_out.at[:, chunk], base_sems.at[g]).start()
        return tuple(placed(accs[f], parts[f], g) for f in range(NF))

    accs = lax.fori_loop(0, cz // INNER, body, (zero,) * NF)
    store_faces(base, ye1, yo1, ze1, zo1)
    total = got[0:ROWS]
    for i in range(1, got.shape[0] // ROWS):
        total = total + got[ROWS * i : ROWS * i + ROWS]
    for i in range(carry_out.shape[0]):
        carry_out[i, 0:ROWS] = total
        for f in range(NF):
            carry_out[i, ROWS + 8 * f : ROWS + 8 * f + 8] = accs[f]
    for g in range(cz // INNER):
        chunk = pl.ds(g * INNER, INNER)
        pltpu.make_async_copy(base.at[:, chunk], base_out.at[:, chunk], base_sems.at[g]).wait()


def second_step(*refs):
    fields, solid, base = refs[:3]
    plane_h, late = refs[3], refs[9:13]
    carried, ye, yo, ze, zo = refs[4:9]
    out_h, modal, q, target = refs[13:17]
    plane_table, late_kept, out, sems, out_sems = refs[17], refs[18:22], *refs[22:25]
    cells, geom_v, strips_v, shapes = late_kept
    cz, cy, cx = fields.shape[1:]
    n_stream = carried.shape[0]
    span_pos = lax.axis_index("span")
    vert_pos = lax.axis_index("vert")
    stream_pos = lax.axis_index("stream")
    coming = fetch((plane_h,), (plane_table,), sems)
    get_base = pltpu.make_async_copy(base, q.at[:, 1 : cz + 1, 8:24, :], out_sems.at[0])
    get_base.start()
    cells_h, geom_h, strips_h, shapes_h = late
    rest = fetch(
        (cells_h, geom_h.at[0, span_pos], strips_h.at[0, span_pos], shapes_h),
        late_kept,
        sems,
        len(coming),
    )

    wait_all(coming)
    low, high = carried[0, 0:8], carried[0, 8:16]
    for i in range(1, n_stream):
        low = low + carried[i, 0:8]
        high = high + carried[i, 8:16]
    one = jnp.where(lane_ids((1, 8)) == 0, 1.0, 0.0)
    hi, lo = split(jnp.concatenate([low, high], axis=1))
    target[...] = (
        bdot(plane_table[...], jnp.concatenate([hi, hi, lo], axis=1), ((1,), (1,))) + one
    )
    n_edge = 2 * cz + 2 * cy
    pick = (
        lax.broadcasted_iota(jnp.int32, (n_edge, 128), 0) == lane_ids((n_edge, 128))
    ).astype(jnp.bfloat16)
    pick = jnp.concatenate([pick, pick], axis=1)
    e_low = bdot(pick, jnp.concatenate(split(low), axis=1), ((1,), (1,)))
    e_high = bdot(pick, jnp.concatenate(split(high), axis=1), ((1,), (1,)))
    relax = relax_weights(cx)
    decay = (6.0 * viscous + relax, 6.0 * heat_diff + relax)
    push = time_step * relax

    def edge_push(f):
        col = e_low[:, 5 + f : 6 + f] if f < 3 else e_high[:, 2 + f : 3 + f]
        if f == 0:
            col = col + 1.0
        col = col * push
        return (
            jnp.where(span_pos > 0, col[0:cz], 0.0),
            jnp.where(span_pos < lax.axis_size("span") - 1, col[cz : 2 * cz], 0.0),
            jnp.where(vert_pos > 0, col[2 * cz : 2 * cz + cy], 0.0),
            jnp.where(vert_pos < lax.axis_size("vert") - 1, col[2 * cz + cy :], 0.0),
        )

    fill_ghosts(q, ye, yo, ze, zo, edge_push)
    get_base.wait()

    def pushing(g, carry):
        for i in range(4):
            z = g * 4 + i
            t = target[pl.ds(pl.multiple_of(z * cy, cy), cy), :]
            for f in range(NF):
                pushed = push * t[:, f : f + 1]
                q[f, z + 1, 8:24, :] = q[f, z + 1, 8:24, :] + pushed
                out[f, z] = fields[f, z] + pushed
        return carry

    lax.fori_loop(0, cz // 4, pushing, 0)
    west_at = jnp.maximum(stream_pos - 1, 0)
    east_at = jnp.minimum(stream_pos + 1, n_stream - 1)
    west, east = [], []
    for f in range(NF):
        rows = slice(ROWS + 8 * f, ROWS + 8 * f + 8)
        west.append(jnp.where(stream_pos > 0, carried[west_at, rows], 0.0))
        east.append(jnp.where(stream_pos < n_stream - 1, carried[east_at, rows], 0.0))
    xg = ghosts_x(west, east)

    def body(g, carry):
        turned = [pltpu.roll(xg[f], (128 - 4 * INNER * g) & 127, 1) for f in range(NF)]
        for i in range(INNER):
            z = g * INNER + i
            damp2 = solid[z] * (2.0 / penalty)
            cs, rs = slab_rates(q, turned, damp2, decay, z, i)
            for f in range(NF):
                out[f, z] = 0.5 * (out[f, z] + cs[f] + time_step * rs[f])
        chunk = pl.ds(pl.multiple_of(g * INNER, INNER), INNER)
        pltpu.make_async_copy(out.at[:, chunk], out_h.at[:, chunk], out_sems.at[g + 1]).start()
        return carry

    lax.fori_loop(0, cz // INNER, body, 0)

    pressure = jnp.transpose(jnp.reshape(out[3], (cz * cy, cx)))
    p_hi = pressure.astype(jnp.bfloat16)
    p_lo = (pressure - p_hi.astype(jnp.float32)).astype(jnp.bfloat16)
    parts = jnp.concatenate([p_hi, p_lo], axis=0)
    wait_all(rest)
    count = cells.shape[1]
    step = 512
    n_comp = geom_v.shape[0]
    own = shapes.shape[2] // lax.axis_size("span")
    sums = [jnp.zeros((8, 128), jnp.float32)] * own
    for at in range(0, count, step):
        where = cells[:, at : at + step]
        rows = lax.broadcasted_iota(jnp.int32, (cz * cy, step), 0)
        hit = jnp.where(rows == (where >> 7), 1.0, 0.0).astype(jnp.bfloat16)
        picked = bdot(parts, hit, ((1,), (0,)))
        picked = picked[:cx] + picked[cx:]
        lanes = lax.broadcasted_iota(jnp.int32, (cx, step), 0)
        sample = jnp.sum(jnp.where(lanes == (where & 127), picked, 0.0), axis=0, keepdims=True)
        traction = jnp.concatenate(
            [sample * geom_v[c, :, at : at + step] for c in range(n_comp)]
            + [jnp.zeros((8 - n_comp, step), jnp.float32)],
            axis=0,
        )
        strip = strips_v[:, at : at + step] - span_pos * own
        for j in range(own):
            mine = jnp.where(strip == j, traction, 0.0)
            for k in range(0, step, 128):
                sums[j] = sums[j] + mine[:, k : k + 128]
    lane = lane_ids((8, shapes.shape[2]))
    spread = jnp.zeros((8, shapes.shape[2]), jnp.float32)
    for j in range(own):
        force = jnp.sum(sums[j], axis=1, keepdims=True)
        spread = jnp.where(lane == span_pos * own + j, force, spread)
    total = jnp.zeros(shapes.shape[1:], jnp.float32)
    for c in range(n_comp):
        total = total + shapes[c] * spread[c : c + 1]
    total = mdot(jnp.ones((8, shapes.shape[2]), jnp.float32), total, ((1,), (1,)))[0:1]
    total = jnp.concatenate(
        [total, jnp.zeros((1, 128 - shapes.shape[1]), jnp.float32)], axis=1
    )
    modal[...] = jnp.broadcast_to(total, modal.shape)
    for g in range(cz // INNER):
        chunk = pl.ds(g * INNER, INNER)
        pltpu.make_async_copy(out.at[:, chunk], out_h.at[:, chunk], out_sems.at[g + 1]).wait()


def f32(*shape):
    return jax.ShapeDtypeStruct(shape, jnp.float32)


VM = pl.BlockSpec(memory_space=pltpu.VMEM)
HB = pl.BlockSpec(memory_space=pltpu.HBM)


def room(mib):
    return pltpu.CompilerParams(vmem_limit_bytes=mib * 1024 * 1024)


def buffers(arrays):
    return [pltpu.VMEM(x.shape, x.dtype) for x in arrays]


def swapped(block, axis, odd):
    pairs = []
    for i in range(odd, lax.axis_size(axis) - 1, 2):
        pairs += [(i, i + 1), (i + 1, i)]
    return lax.ppermute(block, axis, pairs)


def on_device(
    fields, solid_frac, panels, panel_owner, deck_cells, deck_geom, strip_ids, mode_shapes
):
    cz, cy, cx = fields.shape[1:]
    n_stream = lax.axis_size("stream")
    n_span = lax.axis_size("span")
    n_vert = lax.axis_size("vert")
    tiles = n_span * n_vert
    spec = panels.shape[2] // 2
    plane, edges, turn = wave_tables(cz, cy, n_span, n_vert, spec)
    operands = (
        panels.transpose(1, 0, 2),
        panel_owner.reshape(1, -1),
        jnp.asarray(turn),
        jnp.asarray(edges),
    )
    sent = pl.pallas_call(
        sum_panels,
        out_shape=f32(tiles * ROWS, 128),
        in_specs=[HB] * 4,
        out_specs=VM,
        scratch_shapes=buffers(operands) + [pltpu.SemaphoreType.DMA((4,))],
        compiler_params=room(60),
        name="panel_sums",
    )(*operands)
    got = lax.all_to_all(
        sent.reshape(tiles, ROWS, 128), ("span", "vert"), 0, 0, tiled=True
    ).reshape(tiles * ROWS, 128)
    yz_shapes = (f32(NF, cz, cx), f32(NF, cz, cx), f32(NF, cy, cx), f32(NF, cy, cx))

    def swap_yz(ye, yo, ze, zo):
        return (
            swapped(ye, "span", 0),
            swapped(yo, "span", 1),
            swapped(ze, "vert", 0),
            swapped(zo, "vert", 1),
        )

    xf, *faces = pl.pallas_call(
        pack_faces,
        out_shape=(f32(NF, 8, 128),) + yz_shapes,
        in_specs=[VM],
        out_specs=(VM,) * 5,
        compiler_params=room(52),
        name="pack_faces",
    )(fields)
    ghosts = (swapped(xf, "stream", 0), swapped(xf, "stream", 1)) + swap_yz(*faces)
    scratch = pltpu.VMEM((NF, cz + 2, 32, cx), jnp.float32)
    arrived = (got,) + ghosts
    leaving = (f32(n_stream, ROWS + 8 * NF, 128),) + yz_shapes
    base, carry, *faces = pl.pallas_call(
        first_step,
        out_shape=(f32(NF, cz, cy, cx),) + leaving,
        in_specs=[VM] * 9,
        out_specs=(HB,) + (VM,) * 5,
        scratch_shapes=[
            scratch,
            pltpu.VMEM((NF, cz, cy, cx), jnp.float32),
            pltpu.SemaphoreType.DMA((cz // INNER,)),
        ],
        compiler_params=room(52),
        name="first_step",
    )(fields, solid_frac, *arrived)
    carried = lax.all_to_all(carry, "stream", 0, 0, tiled=True)
    ghosts = swap_yz(*faces)
    deck = deck_cells.shape[3]
    plane = jnp.asarray(plane)
    cells = deck_cells.reshape(1, deck)
    shapes = mode_shapes.transpose(0, 2, 1)
    new_fields, modal = pl.pallas_call(
        second_step,
        out_shape=(f32(NF, cz, cy, cx), f32(tiles, 128)),
        in_specs=[VM] * 2 + [HB] * 2 + [VM] * 5 + [HB] * 4,
        out_specs=(HB, VM),
        scratch_shapes=[scratch, pltpu.VMEM((cz * cy, 8), jnp.float32)]
        + buffers((plane, cells, f32(3, 1, deck), strip_ids[0, 0], shapes))
        + [pltpu.VMEM((NF, cz, cy, cx), jnp.float32)]
        + [pltpu.SemaphoreType.DMA((5,)), pltpu.SemaphoreType.DMA((cz // INNER + 1,))],
        compiler_params=room(52),
        name="second_step",
    )(
        fields,
        solid_frac,
        base,
        plane,
        carried,
        *ghosts,
        cells,
        deck_geom.transpose(0, 1, 3, 2, 4),
        strip_ids,
        shapes,
    )
    part = lax.all_to_all(modal, ("span", "vert"), 0, 0, tiled=True)
    part = jnp.broadcast_to(jnp.sum(part, axis=0, keepdims=True), (n_stream, 128))
    part = lax.all_to_all(part, "stream", 0, 0, tiled=True)
    modal_force = jnp.sum(part, axis=0)[: mode_shapes.shape[2]]
    return (new_fields, modal_force)


def solution(mesh):
    return jax.shard_map(
        on_device,
        mesh=mesh,
        in_specs=(
            P(None, "vert", "span", "stream"),
            P("vert", "span", "stream"),
            P(("stream", "span", "vert"), None, None),
            P(("stream", "span", "vert"), None),
            P("vert", "span", "stream", None),
            P("vert", None, "stream", None, None),
            P("vert", None, "stream", None),
            P(),
        ),
        out_specs=(P(None, "vert", "span", "stream"), P()),
        check_vma=False,
    )
```

```python
import math

import jax
import jax.numpy as jnp
import ml_dtypes
import numpy as np
from jax import lax
from jax.experimental import pallas as pl
from jax.experimental.pallas import tpu as pltpu
from jax.sharding import PartitionSpec as P

time_step = 0.15
viscous = 0.05
heat_diff = 0.03
sound_sq = 1.0
buoyant = 0.5
penalty = 0.5
relax_time = 0.5
relax_depth = 8.0
wave_cols = 16

HI = lax.Precision.HIGHEST
NF = 5
ROWS = 16


def mdot(a, b, dims):
    return lax.dot_general(
        a, b, (dims, ((), ())), precision=HI, preferred_element_type=jnp.float32
    )


def split_np(a):
    hi = a.astype(ml_dtypes.bfloat16)
    return hi, (a - hi.astype(np.float32)).astype(ml_dtypes.bfloat16)


def split(a):
    hi = a.astype(jnp.bfloat16)
    return hi, (a - hi.astype(jnp.float32)).astype(jnp.bfloat16)


def bdot(a, b, dims):
    return lax.dot_general(a, b, (dims, ((), ())), preferred_element_type=jnp.float32)


def wave_tables(cz, cy, n_span, n_vert, spec):
    modes = np.arange(spec)
    across = (modes % wave_cols).astype(np.float64)
    upward = (modes // wave_cols).astype(np.float64)
    ny, nz = cy * n_span, cz * n_vert

    def basis(z, y):
        turn = across[None] * y[:, None] / ny + upward[None] * z[:, None] / nz
        angle = 2.0 * math.pi * turn
        return np.concatenate([np.cos(angle), np.sin(angle)], axis=1)

    z, y = np.arange(cz, dtype=np.float64), np.arange(cy, dtype=np.float64)
    plane = basis(np.repeat(z, cy), np.tile(y, cz)).astype(np.float32)
    edges = np.zeros((2 * spec, 128), np.float64)
    at = 0
    for part in (
        basis(z, 0 * z + cy - 1),
        basis(z, 0 * z),
        basis(0 * y + cz - 1, y),
        basis(0 * y, y),
    ):
        edges[:, at : at + part.shape[0]] = part.T
        at += part.shape[0]
    s, v = np.repeat(np.arange(n_span), n_vert), np.tile(np.arange(n_vert), n_span)
    turn = basis(1.0 * v * cz, 1.0 * s * cy).astype(np.float32)
    hi, lo = split_np(plane)
    plane = np.concatenate([hi, lo, hi], axis=1)
    hi, lo = split_np(edges.astype(np.float32))
    edges = np.concatenate([hi, lo, hi], axis=0)
    return plane, edges, turn


def fetch(sources, targets, sems, at=0):
    copies = [
        pltpu.make_async_copy(a, b, sems.at[at + i])
        for i, (a, b) in enumerate(zip(sources, targets))
    ]
    for c in copies:
        c.start()
    return copies


def wait_all(copies):
    for c in copies:
        c.wait()


def sum_panels(panels_h, owner_h, turn_h, edge_h, out, panels, owner, turn, edge_table, sems):
    first = fetch((owner_h, turn_h), (owner, turn), sems)
    fields_in = fetch(
        [panels_h.at[f] for f in range(NF)], [panels.at[f] for f in range(NF)], sems, 2
    )
    last = fetch((edge_h,), (edge_table,), sems, 2 + NF)
    wait_all(first)
    n_vert = lax.axis_size("vert")
    tiles = turn.shape[0]
    spec = turn.shape[1] // 2
    held = owner.shape[1]
    named = jnp.where(
        owner[...] == lax.broadcasted_iota(jnp.int32, (tiles, held), 0), 1.0, 0.0
    ).astype(jnp.bfloat16)
    named = jnp.concatenate([named, named], axis=1)
    cos_t, sin_t = turn[:, :spec], turn[:, spec:]
    turned = []
    for f in range(NF):
        fields_in[f].wait()
        total = bdot(named, jnp.concatenate(split(panels[f]), axis=0), ((1,), (0,)))
        c, s = total[:, :spec], total[:, spec:]
        c2 = c * cos_t + s * sin_t
        s2 = s * cos_t - c * sin_t
        out[pl.ds(f, tiles, stride=ROWS), :] = c2
        out[pl.ds(8 + f, tiles, stride=ROWS), :] = s2
        turned.append(jnp.concatenate([c2, s2], axis=1))
    wait_all(last)
    hi, lo = split(jnp.concatenate(turned, axis=0))
    edge = bdot(jnp.concatenate([hi, hi, lo], axis=1), edge_table[...], ((1,), (0,)))
    lane = lax.broadcasted_iota(jnp.int32, (tiles, 128), 1)
    for f in range(NF):
        e = edge[f * tiles : (f + 1) * tiles]
        row = jnp.where(
            lane < 32,
            jnp.roll(e, n_vert, 0),
            jnp.where(
                lane < 64,
                jnp.roll(e, -n_vert, 0),
                jnp.where(lane < 80, jnp.roll(e, 1, 0), jnp.roll(e, -1, 0)),
            ),
        )
        at = 5 + f if f < 3 else 10 + f
        out[pl.ds(at, tiles, stride=ROWS), :] = row
    out[pl.ds(15, tiles, stride=ROWS), :] = jnp.zeros((tiles, 128), jnp.float32)


def lane_ids(shape):
    return lax.broadcasted_iota(jnp.int32, shape, len(shape) - 1)


INNER = 8


def packed_x(acc, v, zi):
    lane = lane_ids((8, 128))
    for h in range(2):
        k = 2 * zi + h
        acc = jnp.where((lane >> 1) == k, pltpu.roll(v[8 * h : 8 * h + 8], 2 * k + 1, 1), acc)
    return acc


def placed(whole, part, zo):
    width = 4 * INNER
    lane = lane_ids((8, 128))
    return jnp.where(lane // width == zo, pltpu.roll(part, zo * width, 1), whole)


def face_choice(axis):
    return lax.rem(lax.axis_index(axis), 2) == 0


def store_faces(state, ye, yo, ze, zo):
    cz, cy = state.shape[1], state.shape[2]
    y_low, z_low = face_choice("span"), face_choice("vert")
    for f in range(NF):
        low, high = state[f, :, 0, :], state[f, :, cy - 1, :]
        ye[f] = jnp.where(y_low, high, low)
        yo[f] = jnp.where(y_low, low, high)
        low, high = state[f, 0], state[f, cz - 1]
        ze[f] = jnp.where(z_low, high, low)
        zo[f] = jnp.where(z_low, low, high)


def pack_faces(fields, xf, ye, yo, ze, zo):
    cz = fields.shape[1]
    zero = jnp.zeros((8, 128), jnp.float32)

    def body(g, accs):
        new = []
        for f in range(NF):
            part = zero
            for i in range(INNER):
                part = packed_x(part, fields[f, g * INNER + i], i)
            new.append(placed(accs[f], part, g))
        return tuple(new)

    accs = lax.fori_loop(0, cz // INNER, body, (zero,) * NF)
    for f in range(NF):
        xf[f] = accs[f]
    store_faces(fields, ye, yo, ze, zo)


def fill_ghosts(q, ye, yo, ze, zo, extra=None):
    cz = q.shape[1] - 2
    y_low, z_low = face_choice("span"), face_choice("vert")
    for f in range(NF):
        south = jnp.where(y_low, yo[f], ye[f])
        north = jnp.where(y_low, ye[f], yo[f])
        down = jnp.where(z_low, zo[f], ze[f])
        up = jnp.where(z_low, ze[f], zo[f])
        if extra is not None:
            es, en, ed, eu = extra(f)
            south, north, down, up = south + es, north + en, down + ed, up + eu
        q[f, 1 : cz + 1, 7, :] = south
        q[f, 1 : cz + 1, 24, :] = north
        q[f, 0, 8:24, :] = down
        q[f, cz + 1, 8:24, :] = up


def ghosts_x(west, east):
    lane = lane_ids((8, 128))
    return [jnp.where((lane & 1) == 0, west[f], pltpu.roll(east[f], 126, 1)) for f in range(NF)]


def slab_rates(q, xg, damp2, decay, z, zi):
    lane = lane_ids((16, 128))
    first, last = lane == 0, lane == 127
    cs, dx, dy, dz, rs = [], [], [], [], []
    for f in range(NF):
        c = q[f, z + 1, 8:24, :]
        up, down = q[f, z + 2, 8:24, :], q[f, z, 8:24, :]
        north, south = q[f, z + 1, 9:25, :], q[f, z + 1, 7:23, :]
        side = jnp.concatenate(
            [
                pltpu.roll(xg[f], (128 - 4 * zi) % 128, 1),
                pltpu.roll(xg[f], (126 - 4 * zi) % 128, 1),
            ],
            axis=0,
        )
        west = jnp.where(first, side, pltpu.roll(c, 1, 1))
        east = jnp.where(last, side, pltpu.roll(c, 127, 1))
        nu = heat_diff if f == 4 else viscous
        around = (east + west) + (north + south) + (up + down)
        cs.append(c)
        dx.append(east - west)
        dy.append(north - south)
        dz.append(up - down)
        rs.append(nu * around - decay[f == 4] * c)
    hu, hv, hw = 0.5 * cs[0], 0.5 * cs[1], 0.5 * cs[2]
    out = []
    for f in range(NF):
        r = rs[f] - (hu * dx[f] + hv * dy[f] + hw * dz[f])
        if f == 0:
            r = r - 0.5 * dx[3] - damp2 * hu
        elif f == 1:
            r = r - 0.5 * dy[3] - damp2 * hv
        elif f == 2:
            r = r - 0.5 * dz[3] - damp2 * hw + buoyant * cs[4]
        elif f == 3:
            r = r - (0.5 * sound_sq) * (dx[0] + dy[1] + dz[2])
        out.append(r)
    return cs, out


def relax_weights(cx):
    lane = lane_ids((1, cx))
    weight = jnp.exp(lane.astype(jnp.float32) * (-1.0 / relax_depth)) / relax_time
    return jnp.where((lax.axis_index("stream") == 0) & (lane < cx // 2), weight, 0.0)


def first_step(*refs):
    fields, solid = refs[:2]
    got, xe, xo, ye, yo, ze, zo = refs[2:9]
    base_out, carry_out, ye1, yo1, ze1, zo1 = refs[9:15]
    q, base, base_sems, carry, carry_sems = refs[15:20]
    cz = fields.shape[1]
    total = got[0:ROWS]
    for i in range(1, got.shape[0] // ROWS):
        total = total + got[ROWS * i : ROWS * i + ROWS]
    carry[0:ROWS] = total

    def fill(z, carry):
        for f in range(NF):
            q[f, z + 1, 8:24, :] = fields[f, z]
        return carry

    lax.fori_loop(0, cz, fill, 0, unroll=4)
    fill_ghosts(q, ye, yo, ze, zo)
    x_low = face_choice("stream")
    xg = ghosts_x(
        [jnp.where(x_low, xo[f], xe[f]) for f in range(NF)],
        [jnp.where(x_low, xe[f], xo[f]) for f in range(NF)],
    )
    relax = relax_weights(fields.shape[3])
    decay = (6.0 * viscous + relax, 6.0 * heat_diff + relax)
    zero = jnp.zeros((8, 128), jnp.float32)

    def body(g, accs):
        turned = [pltpu.roll(xg[f], (128 - 4 * INNER * g) & 127, 1) for f in range(NF)]
        parts = [zero] * NF
        for i in range(INNER):
            z = g * INNER + i
            damp2 = solid[z] * (2.0 / penalty)
            cs, rs = slab_rates(q, turned, damp2, decay, z, i)
            for f in range(NF):
                b = cs[f] + time_step * rs[f]
                base[f, z] = b
                parts[f] = packed_x(parts[f], b, i)
        chunk = pl.ds(pl.multiple_of(g * INNER, INNER), INNER)
        pltpu.make_async_copy(base.at[:, chunk], base_out.at[:, chunk], base_sems.at[g]).start()
        return tuple(placed(accs[f], parts[f], g) for f in range(NF))

    accs = lax.fori_loop(0, cz // INNER, body, (zero,) * NF)
    for f in range(NF):
        carry[ROWS + 8 * f : ROWS + 8 * f + 8] = accs[f]
    n_stream = carry_out.shape[0]
    going = fetch([carry] * n_stream, [carry_out.at[i] for i in range(n_stream)], carry_sems)
    store_faces(base, ye1, yo1, ze1, zo1)
    wait_all(going)
    for g in range(cz // INNER):
        chunk = pl.ds(g * INNER, INNER)
        pltpu.make_async_copy(base.at[:, chunk], base_out.at[:, chunk], base_sems.at[g]).wait()


def second_step(*refs):
    fields, solid, base = refs[:3]
    plane_table, carried, ye, yo, ze, zo, cells, geom, strips, shapes = refs[3:13]
    out_h, modal, q, target, out, out_sems = refs[13:19]
    cz, cy, cx = fields.shape[1:]
    n_stream = carried.shape[0]
    span_pos = lax.axis_index("span")
    vert_pos = lax.axis_index("vert")
    stream_pos = lax.axis_index("stream")
    get_base = pltpu.make_async_copy(base, q.at[:, 1 : cz + 1, 8:24, :], out_sems.at[0])
    get_base.start()
    low, high = carried[0, 0:8], carried[0, 8:16]
    for i in range(1, n_stream):
        low = low + carried[i, 0:8]
        high = high + carried[i, 8:16]
    one = jnp.where(lane_ids((1, 8)) == 0, 1.0, 0.0)
    hi, lo = split(jnp.concatenate([low, high], axis=1))
    target[...] = (
        bdot(plane_table[...], jnp.concatenate([hi, hi, lo], axis=1), ((1,), (1,))) + one
    )
    n_edge = 2 * cz + 2 * cy
    pick = (
        lax.broadcasted_iota(jnp.int32, (n_edge, 128), 0) == lane_ids((n_edge, 128))
    ).astype(jnp.bfloat16)
    pick = jnp.concatenate([pick, pick], axis=1)
    e_low = bdot(pick, jnp.concatenate(split(low), axis=1), ((1,), (1,)))
    e_high = bdot(pick, jnp.concatenate(split(high), axis=1), ((1,), (1,)))
    relax = relax_weights(cx)
    decay = (6.0 * viscous + relax, 6.0 * heat_diff + relax)
    push = time_step * relax

    def edge_push(f):
        col = e_low[:, 5 + f : 6 + f] if f < 3 else e_high[:, 2 + f : 3 + f]
        if f == 0:
            col = col + 1.0
        col = col * push
        return (
            jnp.where(span_pos > 0, col[0:cz], 0.0),
            jnp.where(span_pos < lax.axis_size("span") - 1, col[cz : 2 * cz], 0.0),
            jnp.where(vert_pos > 0, col[2 * cz : 2 * cz + cy], 0.0),
            jnp.where(vert_pos < lax.axis_size("vert") - 1, col[2 * cz + cy :], 0.0),
        )

    fill_ghosts(q, ye, yo, ze, zo, edge_push)
    get_base.wait()

    def pushing(g, carry):
        for i in range(4):
            z = g * 4 + i
            t = target[pl.ds(pl.multiple_of(z * cy, cy), cy), :]
            for f in range(NF):
                pushed = push * t[:, f : f + 1]
                q[f, z + 1, 8:24, :] = q[f, z + 1, 8:24, :] + pushed
                out[f, z] = fields[f, z] + pushed
        return carry

    lax.fori_loop(0, cz // 4, pushing, 0)
    west_at = jnp.maximum(stream_pos - 1, 0)
    east_at = jnp.minimum(stream_pos + 1, n_stream - 1)
    west, east = [], []
    for f in range(NF):
        rows = slice(ROWS + 8 * f, ROWS + 8 * f + 8)
        west.append(jnp.where(stream_pos > 0, carried[west_at, rows], 0.0))
        east.append(jnp.where(stream_pos < n_stream - 1, carried[east_at, rows], 0.0))
    xg = ghosts_x(west, east)

    def body(g, carry):
        turned = [pltpu.roll(xg[f], (128 - 4 * INNER * g) & 127, 1) for f in range(NF)]
        for i in range(INNER):
            z = g * INNER + i
            damp2 = solid[z] * (2.0 / penalty)
            cs, rs = slab_rates(q, turned, damp2, decay, z, i)
            for f in range(NF):
                out[f, z] = 0.5 * (out[f, z] + cs[f] + time_step * rs[f])
        chunk = pl.ds(pl.multiple_of(g * INNER, INNER), INNER)
        pltpu.make_async_copy(out.at[:, chunk], out_h.at[:, chunk], out_sems.at[g + 1]).start()
        return carry

    lax.fori_loop(0, cz // INNER, body, 0)

    pressure = jnp.transpose(jnp.reshape(out[3], (cz * cy, cx)))
    p_hi = pressure.astype(jnp.bfloat16)
    p_lo = (pressure - p_hi.astype(jnp.float32)).astype(jnp.bfloat16)
    parts = jnp.concatenate([p_hi, p_lo], axis=0)
    count = cells.shape[1]
    step = 512
    n_comp = geom.shape[2]
    own = shapes.shape[2] // lax.axis_size("span")
    sums = [jnp.zeros((8, 128), jnp.float32)] * own
    for at in range(0, count, step):
        where = cells[:, at : at + step]
        rows = lax.broadcasted_iota(jnp.int32, (cz * cy, step), 0)
        hit = jnp.where(rows == (where >> 7), 1.0, 0.0).astype(jnp.bfloat16)
        picked = bdot(parts, hit, ((1,), (0,)))
        picked = picked[:cx] + picked[cx:]
        lanes = lax.broadcasted_iota(jnp.int32, (cx, step), 0)
        sample = jnp.sum(jnp.where(lanes == (where & 127), picked, 0.0), axis=0, keepdims=True)
        traction = jnp.concatenate(
            [sample * geom[0, span_pos, c, :, at : at + step] for c in range(n_comp)]
            + [jnp.zeros((8 - n_comp, step), jnp.float32)],
            axis=0,
        )
        strip = strips[0, span_pos, :, at : at + step] - span_pos * own
        for j in range(own):
            mine = jnp.where(strip == j, traction, 0.0)
            for k in range(0, step, 128):
                sums[j] = sums[j] + mine[:, k : k + 128]
    lane = lane_ids((8, shapes.shape[2]))
    spread = jnp.zeros((8, shapes.shape[2]), jnp.float32)
    for j in range(own):
        force = jnp.sum(sums[j], axis=1, keepdims=True)
        spread = jnp.where(lane == span_pos * own + j, force, spread)
    total = jnp.zeros(shapes.shape[1:], jnp.float32)
    for c in range(n_comp):
        total = total + shapes[c] * spread[c : c + 1]
    total = mdot(jnp.ones((8, shapes.shape[2]), jnp.float32), total, ((1,), (1,)))[0:1]
    total = jnp.concatenate(
        [total, jnp.zeros((1, 128 - shapes.shape[1]), jnp.float32)], axis=1
    )
    modal[...] = jnp.broadcast_to(total, modal.shape)
    for g in range(cz // INNER):
        chunk = pl.ds(g * INNER, INNER)
        pltpu.make_async_copy(out.at[:, chunk], out_h.at[:, chunk], out_sems.at[g + 1]).wait()


def f32(*shape):
    return jax.ShapeDtypeStruct(shape, jnp.float32)


VM = pl.BlockSpec(memory_space=pltpu.VMEM)
HB = pl.BlockSpec(memory_space=pltpu.HBM)


def room(mib):
    return pltpu.CompilerParams(vmem_limit_bytes=mib * 1024 * 1024)


def buffers(arrays):
    return [pltpu.VMEM(x.shape, x.dtype) for x in arrays]


def swapped(block, axis, odd):
    pairs = []
    for i in range(odd, lax.axis_size(axis) - 1, 2):
        pairs += [(i, i + 1), (i + 1, i)]
    return lax.ppermute(block, axis, pairs)


def on_device(
    fields, solid_frac, panels, panel_owner, deck_cells, deck_geom, strip_ids, mode_shapes
):
    cz, cy, cx = fields.shape[1:]
    n_stream = lax.axis_size("stream")
    n_span = lax.axis_size("span")
    n_vert = lax.axis_size("vert")
    tiles = n_span * n_vert
    spec = panels.shape[2] // 2
    plane, edges, turn = wave_tables(cz, cy, n_span, n_vert, spec)
    operands = (
        panels.transpose(1, 0, 2),
        panel_owner.reshape(1, -1),
        jnp.asarray(turn),
        jnp.asarray(edges),
    )
    sent = pl.pallas_call(
        sum_panels,
        out_shape=f32(tiles * ROWS, 128),
        in_specs=[HB] * 4,
        out_specs=VM,
        scratch_shapes=buffers(operands) + [pltpu.SemaphoreType.DMA((NF + 3,))],
        compiler_params=room(60),
        name="panel_sums",
    )(*operands)
    got = lax.all_to_all(
        sent.reshape(tiles, ROWS, 128), ("span", "vert"), 0, 0, tiled=True
    ).reshape(tiles * ROWS, 128)
    yz_shapes = (f32(NF, cz, cx), f32(NF, cz, cx), f32(NF, cy, cx), f32(NF, cy, cx))

    def swap_yz(ye, yo, ze, zo):
        return (
            swapped(ye, "span", 0),
            swapped(yo, "span", 1),
            swapped(ze, "vert", 0),
            swapped(zo, "vert", 1),
        )

    xf, *faces = pl.pallas_call(
        pack_faces,
        out_shape=(f32(NF, 8, 128),) + yz_shapes,
        in_specs=[VM],
        out_specs=(VM,) * 5,
        compiler_params=room(52),
        name="pack_faces",
    )(fields)
    ghosts = (swapped(xf, "stream", 0), swapped(xf, "stream", 1)) + swap_yz(*faces)
    scratch = pltpu.VMEM((NF, cz + 2, 32, cx), jnp.float32)
    arrived = (got,) + ghosts
    leaving = (f32(n_stream, ROWS + 8 * NF, 128),) + yz_shapes
    base, carry, *faces = pl.pallas_call(
        first_step,
        out_shape=(f32(NF, cz, cy, cx),) + leaving,
        in_specs=[VM] * 9,
        out_specs=(HB, HB) + (VM,) * 4,
        scratch_shapes=[
            scratch,
            pltpu.VMEM((NF, cz, cy, cx), jnp.float32),
            pltpu.SemaphoreType.DMA((cz // INNER,)),
            pltpu.VMEM((ROWS + 8 * NF, 128), jnp.float32),
            pltpu.SemaphoreType.DMA((n_stream,)),
        ],
        compiler_params=room(52),
        name="first_step",
    )(fields, solid_frac, *arrived)
    carried = lax.all_to_all(carry, "stream", 0, 0, tiled=True)
    ghosts = swap_yz(*faces)
    deck = deck_cells.shape[3]
    plane = jnp.asarray(plane)
    cells = deck_cells.reshape(1, deck)
    shapes = mode_shapes.transpose(0, 2, 1)
    new_fields, modal = pl.pallas_call(
        second_step,
        out_shape=(f32(NF, cz, cy, cx), f32(tiles, 128)),
        in_specs=[VM] * 2 + [HB] + [VM] * 10,
        out_specs=(HB, VM),
        scratch_shapes=[scratch, pltpu.VMEM((cz * cy, 8), jnp.float32)]
        + [pltpu.VMEM((NF, cz, cy, cx), jnp.float32)]
        + [pltpu.SemaphoreType.DMA((cz // INNER + 1,))],
        compiler_params=room(51),
        name="second_step",
    )(
        fields,
        solid_frac,
        base,
        plane,
        carried,
        *ghosts,
        cells,
        deck_geom.transpose(0, 1, 3, 2, 4),
        strip_ids,
        shapes,
    )
    part = lax.all_to_all(modal, ("span", "vert"), 0, 0, tiled=True)
    part = jnp.broadcast_to(jnp.sum(part, axis=0, keepdims=True), (n_stream, 128))
    part = lax.all_to_all(part, "stream", 0, 0, tiled=True)
    modal_force = jnp.sum(part, axis=0)[: mode_shapes.shape[2]]
    return (new_fields, modal_force)


def solution(mesh):
    return jax.shard_map(
        on_device,
        mesh=mesh,
        in_specs=(
            P(None, "vert", "span", "stream"),
            P("vert", "span", "stream"),
            P(("stream", "span", "vert"), None, None),
            P(("stream", "span", "vert"), None),
            P("vert", "span", "stream", None),
            P("vert", None, "stream", None, None),
            P("vert", None, "stream", None),
            P(),
        ),
        out_specs=(P(None, "vert", "span", "stream"), P()),
        check_vma=False,
    )
```

```python
import math

import jax
import jax.numpy as jnp
import ml_dtypes
import numpy as np
from jax import lax
from jax.experimental import pallas as pl
from jax.experimental.pallas import tpu as pltpu
from jax.sharding import PartitionSpec as P

time_step = 0.15
viscous = 0.05
heat_diff = 0.03
sound_sq = 1.0
buoyant = 0.5
penalty = 0.5
relax_time = 0.5
relax_depth = 8.0
wave_cols = 16

HI = lax.Precision.HIGHEST
NF = 5
ROWS = 16


def mdot(a, b, dims):
    return lax.dot_general(
        a, b, (dims, ((), ())), precision=HI, preferred_element_type=jnp.float32
    )


def split_np(a):
    hi = a.astype(ml_dtypes.bfloat16)
    return hi, (a - hi.astype(np.float32)).astype(ml_dtypes.bfloat16)


def split(a):
    hi = a.astype(jnp.bfloat16)
    return hi, (a - hi.astype(jnp.float32)).astype(jnp.bfloat16)


def bdot(a, b, dims):
    return lax.dot_general(a, b, (dims, ((), ())), preferred_element_type=jnp.float32)


def wave_tables(cz, cy, n_span, n_vert, spec):
    modes = np.arange(spec)
    across = (modes % wave_cols).astype(np.float64)
    upward = (modes // wave_cols).astype(np.float64)
    ny, nz = cy * n_span, cz * n_vert

    def basis(z, y):
        turn = across[None] * y[:, None] / ny + upward[None] * z[:, None] / nz
        angle = 2.0 * math.pi * turn
        return np.concatenate([np.cos(angle), np.sin(angle)], axis=1)

    z, y = np.arange(cz, dtype=np.float64), np.arange(cy, dtype=np.float64)
    plane = basis(np.repeat(z, cy), np.tile(y, cz)).astype(np.float32)
    edges = np.zeros((2 * spec, 128), np.float64)
    at = 0
    for part in (
        basis(z, 0 * z + cy - 1),
        basis(z, 0 * z),
        basis(0 * y + cz - 1, y),
        basis(0 * y, y),
    ):
        edges[:, at : at + part.shape[0]] = part.T
        at += part.shape[0]
    s, v = np.repeat(np.arange(n_span), n_vert), np.tile(np.arange(n_vert), n_span)
    turn = basis(1.0 * v * cz, 1.0 * s * cy).astype(np.float32)
    hi, lo = split_np(plane)
    plane = np.concatenate([hi, lo, hi], axis=1)
    hi, lo = split_np(edges.astype(np.float32))
    edges = np.concatenate([hi, lo, hi], axis=0)
    return plane, edges, turn


def fetch(sources, targets, sems, at=0):
    copies = [
        pltpu.make_async_copy(a, b, sems.at[at + i])
        for i, (a, b) in enumerate(zip(sources, targets))
    ]
    for c in copies:
        c.start()
    return copies


def wait_all(copies):
    for c in copies:
        c.wait()


def sum_panels(panels_h, owner_h, turn_h, edge_h, out, panels, owner, turn, edge_table, sems):
    wait_all(
        fetch((panels_h, owner_h, turn_h, edge_h), (panels, owner, turn, edge_table), sems)
    )
    n_vert = lax.axis_size("vert")
    tiles = turn.shape[0]
    spec = turn.shape[1] // 2
    held = owner.shape[1]
    named = jnp.where(
        owner[...] == lax.broadcasted_iota(jnp.int32, (tiles, held), 0), 1.0, 0.0
    ).astype(jnp.bfloat16)
    named = jnp.concatenate([named, named], axis=1)
    cos_t, sin_t = turn[:, :spec], turn[:, spec:]
    turned = []
    for f in range(NF):
        total = bdot(named, jnp.concatenate(split(panels[f]), axis=0), ((1,), (0,)))
        c, s = total[:, :spec], total[:, spec:]
        c2 = c * cos_t + s * sin_t
        s2 = s * cos_t - c * sin_t
        out[pl.ds(f, tiles, stride=ROWS), :] = c2
        out[pl.ds(8 + f, tiles, stride=ROWS), :] = s2
        turned.append(jnp.concatenate([c2, s2], axis=1))
    hi, lo = split(jnp.concatenate(turned, axis=0))
    edge = bdot(jnp.concatenate([hi, hi, lo], axis=1), edge_table[...], ((1,), (0,)))
    lane = lax.broadcasted_iota(jnp.int32, (tiles, 128), 1)
    for f in range(NF):
        e = edge[f * tiles : (f + 1) * tiles]
        row = jnp.where(
            lane < 32,
            jnp.roll(e, n_vert, 0),
            jnp.where(
                lane < 64,
                jnp.roll(e, -n_vert, 0),
                jnp.where(lane < 80, jnp.roll(e, 1, 0), jnp.roll(e, -1, 0)),
            ),
        )
        at = 5 + f if f < 3 else 10 + f
        out[pl.ds(at, tiles, stride=ROWS), :] = row
    out[pl.ds(15, tiles, stride=ROWS), :] = jnp.zeros((tiles, 128), jnp.float32)


def lane_ids(shape):
    return lax.broadcasted_iota(jnp.int32, shape, len(shape) - 1)


INNER = 8


def packed_x(acc, v, zi):
    lane = lane_ids((8, 128))
    for h in range(2):
        k = 2 * zi + h
        acc = jnp.where((lane >> 1) == k, pltpu.roll(v[8 * h : 8 * h + 8], 2 * k + 1, 1), acc)
    return acc


def placed(whole, part, zo):
    width = 4 * INNER
    lane = lane_ids((8, 128))
    return jnp.where(lane // width == zo, pltpu.roll(part, zo * width, 1), whole)


def face_choice(axis):
    return lax.rem(lax.axis_index(axis), 2) == 0


def store_faces(state, ye, yo, ze, zo):
    cz, cy = state.shape[1], state.shape[2]
    y_low, z_low = face_choice("span"), face_choice("vert")
    for f in range(NF):
        low, high = state[f, :, 0, :], state[f, :, cy - 1, :]
        ye[f] = jnp.where(y_low, high, low)
        yo[f] = jnp.where(y_low, low, high)
        low, high = state[f, 0], state[f, cz - 1]
        ze[f] = jnp.where(z_low, high, low)
        zo[f] = jnp.where(z_low, low, high)


def pack_faces(fields, xf, ye, yo, ze, zo):
    cz = fields.shape[1]
    zero = jnp.zeros((8, 128), jnp.float32)

    def body(g, accs):
        new = []
        for f in range(NF):
            part = zero
            for i in range(INNER):
                part = packed_x(part, fields[f, g * INNER + i], i)
            new.append(placed(accs[f], part, g))
        return tuple(new)

    accs = lax.fori_loop(0, cz // INNER, body, (zero,) * NF)
    for f in range(NF):
        xf[f] = accs[f]
    store_faces(fields, ye, yo, ze, zo)


def fill_ghosts(q, ye, yo, ze, zo, extra=None):
    cz = q.shape[1] - 2
    y_low, z_low = face_choice("span"), face_choice("vert")
    for f in range(NF):
        south = jnp.where(y_low, yo[f], ye[f])
        north = jnp.where(y_low, ye[f], yo[f])
        down = jnp.where(z_low, zo[f], ze[f])
        up = jnp.where(z_low, ze[f], zo[f])
        if extra is not None:
            es, en, ed, eu = extra(f)
            south, north, down, up = south + es, north + en, down + ed, up + eu
        q[f, 1 : cz + 1, 7, :] = south
        q[f, 1 : cz + 1, 24, :] = north
        q[f, 0, 8:24, :] = down
        q[f, cz + 1, 8:24, :] = up


def ghosts_x(west, east):
    lane = lane_ids((8, 128))
    return [jnp.where((lane & 1) == 0, west[f], pltpu.roll(east[f], 126, 1)) for f in range(NF)]


def slab_rates(q, xg, damp2, decay, z, zi):
    lane = lane_ids((16, 128))
    first, last = lane == 0, lane == 127
    cs, dx, dy, dz, rs = [], [], [], [], []
    for f in range(NF):
        c = q[f, z + 1, 8:24, :]
        up, down = q[f, z + 2, 8:24, :], q[f, z, 8:24, :]
        north, south = q[f, z + 1, 9:25, :], q[f, z + 1, 7:23, :]
        side = jnp.concatenate(
            [
                pltpu.roll(xg[f], (128 - 4 * zi) % 128, 1),
                pltpu.roll(xg[f], (126 - 4 * zi) % 128, 1),
            ],
            axis=0,
        )
        west = jnp.where(first, side, pltpu.roll(c, 1, 1))
        east = jnp.where(last, side, pltpu.roll(c, 127, 1))
        nu = heat_diff if f == 4 else viscous
        around = (east + west) + (north + south) + (up + down)
        cs.append(c)
        dx.append(east - west)
        dy.append(north - south)
        dz.append(up - down)
        rs.append(nu * around - decay[f == 4] * c)
    hu, hv, hw = 0.5 * cs[0], 0.5 * cs[1], 0.5 * cs[2]
    out = []
    for f in range(NF):
        r = rs[f] - (hu * dx[f] + hv * dy[f] + hw * dz[f])
        if f == 0:
            r = r - 0.5 * dx[3] - damp2 * hu
        elif f == 1:
            r = r - 0.5 * dy[3] - damp2 * hv
        elif f == 2:
            r = r - 0.5 * dz[3] - damp2 * hw + buoyant * cs[4]
        elif f == 3:
            r = r - (0.5 * sound_sq) * (dx[0] + dy[1] + dz[2])
        out.append(r)
    return cs, out


def relax_weights(cx):
    lane = lane_ids((1, cx))
    weight = jnp.exp(lane.astype(jnp.float32) * (-1.0 / relax_depth)) / relax_time
    return jnp.where((lax.axis_index("stream") == 0) & (lane < cx // 2), weight, 0.0)


def first_step(*refs):
    fields, solid = refs[:2]
    got, xe, xo, ye, yo, ze, zo = refs[2:9]
    base_out, carry_out, ye1, yo1, ze1, zo1 = refs[9:15]
    q, base, base_sems, carry, carry_sems = refs[15:20]
    cz = fields.shape[1]
    total = got[0:ROWS]
    for i in range(1, got.shape[0] // ROWS):
        total = total + got[ROWS * i : ROWS * i + ROWS]
    carry[0:ROWS] = total

    def fill(z, carry):
        for f in range(NF):
            q[f, z + 1, 8:24, :] = fields[f, z]
        return carry

    lax.fori_loop(0, cz, fill, 0, unroll=4)
    fill_ghosts(q, ye, yo, ze, zo)
    x_low = face_choice("stream")
    xg = ghosts_x(
        [jnp.where(x_low, xo[f], xe[f]) for f in range(NF)],
        [jnp.where(x_low, xe[f], xo[f]) for f in range(NF)],
    )
    relax = relax_weights(fields.shape[3])
    decay = (6.0 * viscous + relax, 6.0 * heat_diff + relax)
    zero = jnp.zeros((8, 128), jnp.float32)

    def body(g, accs):
        turned = [pltpu.roll(xg[f], (128 - 4 * INNER * g) & 127, 1) for f in range(NF)]
        parts = [zero] * NF
        for i in range(INNER):
            z = g * INNER + i
            damp2 = solid[z] * (2.0 / penalty)
            cs, rs = slab_rates(q, turned, damp2, decay, z, i)
            for f in range(NF):
                b = cs[f] + time_step * rs[f]
                base[f, z] = b
                parts[f] = packed_x(parts[f], b, i)
        chunk = pl.ds(pl.multiple_of(g * INNER, INNER), INNER)
        pltpu.make_async_copy(base.at[:, chunk], base_out.at[:, chunk], base_sems.at[g]).start()
        return tuple(placed(accs[f], parts[f], g) for f in range(NF))

    accs = lax.fori_loop(0, cz // INNER, body, (zero,) * NF)
    for f in range(NF):
        carry[ROWS + 8 * f : ROWS + 8 * f + 8] = accs[f]
    n_stream = carry_out.shape[0]
    going = fetch([carry] * n_stream, [carry_out.at[i] for i in range(n_stream)], carry_sems)
    store_faces(base, ye1, yo1, ze1, zo1)
    wait_all(going)
    for g in range(cz // INNER):
        chunk = pl.ds(g * INNER, INNER)
        pltpu.make_async_copy(base.at[:, chunk], base_out.at[:, chunk], base_sems.at[g]).wait()


def second_step(*refs):
    fields, solid, base = refs[:3]
    plane_table, carried, ye, yo, ze, zo, cells, geom, strips, shapes = refs[3:13]
    out_h, modal, q, target, out, out_sems = refs[13:19]
    cz, cy, cx = fields.shape[1:]
    n_stream = carried.shape[0]
    span_pos = lax.axis_index("span")
    vert_pos = lax.axis_index("vert")
    stream_pos = lax.axis_index("stream")
    get_base = pltpu.make_async_copy(base, q.at[:, 1 : cz + 1, 8:24, :], out_sems.at[0])
    get_base.start()
    low, high = carried[0, 0:8], carried[0, 8:16]
    for i in range(1, n_stream):
        low = low + carried[i, 0:8]
        high = high + carried[i, 8:16]
    one = jnp.where(lane_ids((1, 8)) == 0, 1.0, 0.0)
    hi, lo = split(jnp.concatenate([low, high], axis=1))
    target[...] = (
        bdot(plane_table[...], jnp.concatenate([hi, hi, lo], axis=1), ((1,), (1,))) + one
    )
    n_edge = 2 * cz + 2 * cy
    pick = (
        lax.broadcasted_iota(jnp.int32, (n_edge, 128), 0) == lane_ids((n_edge, 128))
    ).astype(jnp.bfloat16)
    pick = jnp.concatenate([pick, pick], axis=1)
    e_low = bdot(pick, jnp.concatenate(split(low), axis=1), ((1,), (1,)))
    e_high = bdot(pick, jnp.concatenate(split(high), axis=1), ((1,), (1,)))
    relax = relax_weights(cx)
    decay = (6.0 * viscous + relax, 6.0 * heat_diff + relax)
    push = time_step * relax

    def edge_push(f):
        col = e_low[:, 5 + f : 6 + f] if f < 3 else e_high[:, 2 + f : 3 + f]
        if f == 0:
            col = col + 1.0
        col = col * push
        return (
            jnp.where(span_pos > 0, col[0:cz], 0.0),
            jnp.where(span_pos < lax.axis_size("span") - 1, col[cz : 2 * cz], 0.0),
            jnp.where(vert_pos > 0, col[2 * cz : 2 * cz + cy], 0.0),
            jnp.where(vert_pos < lax.axis_size("vert") - 1, col[2 * cz + cy :], 0.0),
        )

    fill_ghosts(q, ye, yo, ze, zo, edge_push)
    get_base.wait()

    def pushing(g, carry):
        for i in range(4):
            z = g * 4 + i
            t = target[pl.ds(pl.multiple_of(z * cy, cy), cy), :]
            for f in range(NF):
                pushed = push * t[:, f : f + 1]
                q[f, z + 1, 8:24, :] = q[f, z + 1, 8:24, :] + pushed
                out[f, z] = fields[f, z] + pushed
        return carry

    lax.fori_loop(0, cz // 4, pushing, 0)
    west_at = jnp.maximum(stream_pos - 1, 0)
    east_at = jnp.minimum(stream_pos + 1, n_stream - 1)
    west, east = [], []
    for f in range(NF):
        rows = slice(ROWS + 8 * f, ROWS + 8 * f + 8)
        west.append(jnp.where(stream_pos > 0, carried[west_at, rows], 0.0))
        east.append(jnp.where(stream_pos < n_stream - 1, carried[east_at, rows], 0.0))
    xg = ghosts_x(west, east)

    def body(g, carry):
        turned = [pltpu.roll(xg[f], (128 - 4 * INNER * g) & 127, 1) for f in range(NF)]
        for i in range(INNER):
            z = g * INNER + i
            damp2 = solid[z] * (2.0 / penalty)
            cs, rs = slab_rates(q, turned, damp2, decay, z, i)
            for f in range(NF):
                out[f, z] = 0.5 * (out[f, z] + cs[f] + time_step * rs[f])
        chunk = pl.ds(pl.multiple_of(g * INNER, INNER), INNER)
        pltpu.make_async_copy(out.at[:, chunk], out_h.at[:, chunk], out_sems.at[g + 1]).start()
        return carry

    lax.fori_loop(0, cz // INNER, body, 0)

    pressure = jnp.transpose(jnp.reshape(out[3], (cz * cy, cx)))
    p_hi = pressure.astype(jnp.bfloat16)
    p_lo = (pressure - p_hi.astype(jnp.float32)).astype(jnp.bfloat16)
    parts = jnp.concatenate([p_hi, p_lo], axis=0)
    count = cells.shape[1]
    step = 512
    n_comp = geom.shape[2]
    own = shapes.shape[2] // lax.axis_size("span")
    sums = [jnp.zeros((8, 128), jnp.float32)] * own
    for at in range(0, count, step):
        where = cells[:, at : at + step]
        rows = lax.broadcasted_iota(jnp.int32, (cz * cy, step), 0)
        hit = jnp.where(rows == (where >> 7), 1.0, 0.0).astype(jnp.bfloat16)
        picked = bdot(parts, hit, ((1,), (0,)))
        picked = picked[:cx] + picked[cx:]
        lanes = lax.broadcasted_iota(jnp.int32, (cx, step), 0)
        sample = jnp.sum(jnp.where(lanes == (where & 127), picked, 0.0), axis=0, keepdims=True)
        traction = jnp.concatenate(
            [sample * geom[0, span_pos, c, :, at : at + step] for c in range(n_comp)]
            + [jnp.zeros((8 - n_comp, step), jnp.float32)],
            axis=0,
        )
        strip = strips[0, span_pos, :, at : at + step] - span_pos * own
        for j in range(own):
            mine = jnp.where(strip == j, traction, 0.0)
            for k in range(0, step, 128):
                sums[j] = sums[j] + mine[:, k : k + 128]
    lane = lane_ids((8, shapes.shape[2]))
    spread = jnp.zeros((8, shapes.shape[2]), jnp.float32)
    for j in range(own):
        force = jnp.sum(sums[j], axis=1, keepdims=True)
        spread = jnp.where(lane == span_pos * own + j, force, spread)
    total = jnp.zeros(shapes.shape[1:], jnp.float32)
    for c in range(n_comp):
        total = total + shapes[c] * spread[c : c + 1]
    total = mdot(jnp.ones((8, shapes.shape[2]), jnp.float32), total, ((1,), (1,)))[0:1]
    total = jnp.concatenate(
        [total, jnp.zeros((1, 128 - shapes.shape[1]), jnp.float32)], axis=1
    )
    modal[...] = jnp.broadcast_to(total, modal.shape)
    for g in range(cz // INNER):
        chunk = pl.ds(g * INNER, INNER)
        pltpu.make_async_copy(out.at[:, chunk], out_h.at[:, chunk], out_sems.at[g + 1]).wait()


def f32(*shape):
    return jax.ShapeDtypeStruct(shape, jnp.float32)


VM = pl.BlockSpec(memory_space=pltpu.VMEM)
HB = pl.BlockSpec(memory_space=pltpu.HBM)


def room(mib):
    return pltpu.CompilerParams(vmem_limit_bytes=mib * 1024 * 1024)


def buffers(arrays):
    return [pltpu.VMEM(x.shape, x.dtype) for x in arrays]


def swapped(block, axis, odd):
    pairs = []
    for i in range(odd, lax.axis_size(axis) - 1, 2):
        pairs += [(i, i + 1), (i + 1, i)]
    return lax.ppermute(block, axis, pairs)


def on_device(
    fields, solid_frac, panels, panel_owner, deck_cells, deck_geom, strip_ids, mode_shapes
):
    cz, cy, cx = fields.shape[1:]
    n_stream = lax.axis_size("stream")
    n_span = lax.axis_size("span")
    n_vert = lax.axis_size("vert")
    tiles = n_span * n_vert
    spec = panels.shape[2] // 2
    plane, edges, turn = wave_tables(cz, cy, n_span, n_vert, spec)
    operands = (
        panels.transpose(1, 0, 2),
        panel_owner.reshape(1, -1),
        jnp.asarray(turn),
        jnp.asarray(edges),
    )
    sent = pl.pallas_call(
        sum_panels,
        out_shape=f32(tiles * ROWS, 128),
        in_specs=[HB] * 4,
        out_specs=VM,
        scratch_shapes=buffers(operands) + [pltpu.SemaphoreType.DMA((4,))],
        compiler_params=room(60),
        name="panel_sums",
    )(*operands)
    got = lax.all_to_all(
        sent.reshape(tiles, ROWS, 128), ("span", "vert"), 0, 0, tiled=True
    ).reshape(tiles * ROWS, 128)
    yz_shapes = (f32(NF, cz, cx), f32(NF, cz, cx), f32(NF, cy, cx), f32(NF, cy, cx))

    def swap_yz(ye, yo, ze, zo):
        return (
            swapped(ye, "span", 0),
            swapped(yo, "span", 1),
            swapped(ze, "vert", 0),
            swapped(zo, "vert", 1),
        )

    xf, *faces = pl.pallas_call(
        pack_faces,
        out_shape=(f32(NF, 8, 128),) + yz_shapes,
        in_specs=[VM],
        out_specs=(VM,) * 5,
        compiler_params=room(52),
        name="pack_faces",
    )(fields)
    ghosts = (swapped(xf, "stream", 0), swapped(xf, "stream", 1)) + swap_yz(*faces)
    scratch = pltpu.VMEM((NF, cz + 2, 32, cx), jnp.float32)
    arrived = (got,) + ghosts
    leaving = (f32(n_stream, ROWS + 8 * NF, 128),) + yz_shapes
    base, carry, *faces = pl.pallas_call(
        first_step,
        out_shape=(f32(NF, cz, cy, cx),) + leaving,
        in_specs=[VM] * 9,
        out_specs=(HB, HB) + (VM,) * 4,
        scratch_shapes=[
            scratch,
            pltpu.VMEM((NF, cz, cy, cx), jnp.float32),
            pltpu.SemaphoreType.DMA((cz // INNER,)),
            pltpu.VMEM((ROWS + 8 * NF, 128), jnp.float32),
            pltpu.SemaphoreType.DMA((n_stream,)),
        ],
        compiler_params=room(52),
        name="first_step",
    )(fields, solid_frac, *arrived)
    carried = lax.all_to_all(carry, "stream", 0, 0, tiled=True)
    ghosts = swap_yz(*faces)
    deck = deck_cells.shape[3]
    plane = jnp.asarray(plane)
    cells = deck_cells.reshape(1, deck)
    shapes = mode_shapes.transpose(0, 2, 1)
    new_fields, modal = pl.pallas_call(
        second_step,
        out_shape=(f32(NF, cz, cy, cx), f32(n_span, 128)),
        in_specs=[VM] * 2 + [HB] + [VM] * 10,
        out_specs=(HB, VM),
        scratch_shapes=[scratch, pltpu.VMEM((cz * cy, 8), jnp.float32)]
        + [pltpu.VMEM((NF, cz, cy, cx), jnp.float32)]
        + [pltpu.SemaphoreType.DMA((cz // INNER + 1,))],
        compiler_params=room(51),
        name="second_step",
    )(
        fields,
        solid_frac,
        base,
        plane,
        carried,
        *ghosts,
        cells,
        deck_geom.transpose(0, 1, 3, 2, 4),
        strip_ids,
        shapes,
    )
    part = lax.all_to_all(modal, "span", 0, 0, tiled=True)
    part = jnp.broadcast_to(jnp.sum(part, axis=0, keepdims=True), (n_stream * n_vert, 128))
    part = lax.all_to_all(part, ("stream", "vert"), 0, 0, tiled=True)
    modal_force = jnp.sum(part, axis=0)[: mode_shapes.shape[2]]
    return (new_fields, modal_force)


def solution(mesh):
    return jax.shard_map(
        on_device,
        mesh=mesh,
        in_specs=(
            P(None, "vert", "span", "stream"),
            P("vert", "span", "stream"),
            P(("stream", "span", "vert"), None, None),
            P(("stream", "span", "vert"), None),
            P("vert", "span", "stream", None),
            P("vert", None, "stream", None, None),
            P("vert", None, "stream", None),
            P(),
        ),
        out_specs=(P(None, "vert", "span", "stream"), P()),
        check_vma=False,
    )
```

```python
import math

import jax
import jax.numpy as jnp
import ml_dtypes
import numpy as np
from jax import lax
from jax.experimental import pallas as pl
from jax.experimental.pallas import tpu as pltpu
from jax.sharding import PartitionSpec as P

time_step = 0.15
viscous = 0.05
heat_diff = 0.03
sound_sq = 1.0
buoyant = 0.5
penalty = 0.5
relax_time = 0.5
relax_depth = 8.0
wave_cols = 16

HI = lax.Precision.HIGHEST
NF = 5
ROWS = 16


def mdot(a, b, dims):
    return lax.dot_general(
        a, b, (dims, ((), ())), precision=HI, preferred_element_type=jnp.float32
    )


def split_np(a):
    hi = a.astype(ml_dtypes.bfloat16)
    return hi, (a - hi.astype(np.float32)).astype(ml_dtypes.bfloat16)


def split(a):
    hi = a.astype(jnp.bfloat16)
    return hi, (a - hi.astype(jnp.float32)).astype(jnp.bfloat16)


def bdot(a, b, dims):
    return lax.dot_general(a, b, (dims, ((), ())), preferred_element_type=jnp.float32)


def wave_tables(cz, cy, n_span, n_vert, spec):
    modes = np.arange(spec)
    across = (modes % wave_cols).astype(np.float64)
    upward = (modes // wave_cols).astype(np.float64)
    ny, nz = cy * n_span, cz * n_vert

    def basis(z, y):
        turn = across[None] * y[:, None] / ny + upward[None] * z[:, None] / nz
        angle = 2.0 * math.pi * turn
        return np.concatenate([np.cos(angle), np.sin(angle)], axis=1)

    z, y = np.arange(cz, dtype=np.float64), np.arange(cy, dtype=np.float64)
    plane = basis(np.repeat(z, cy), np.tile(y, cz)).astype(np.float32)
    edges = np.zeros((2 * spec, 128), np.float64)
    at = 0
    for part in (
        basis(z, 0 * z + cy - 1),
        basis(z, 0 * z),
        basis(0 * y + cz - 1, y),
        basis(0 * y, y),
    ):
        edges[:, at : at + part.shape[0]] = part.T
        at += part.shape[0]
    s, v = np.repeat(np.arange(n_span), n_vert), np.tile(np.arange(n_vert), n_span)
    turn = basis(1.0 * v * cz, 1.0 * s * cy).astype(np.float32)
    hi, lo = split_np(plane)
    plane = np.concatenate([hi, lo, hi], axis=1)
    hi, lo = split_np(edges.astype(np.float32))
    edges = np.concatenate([hi, lo, hi], axis=0)
    return plane, edges, turn


def fetch(sources, targets, sems, at=0):
    copies = [
        pltpu.make_async_copy(a, b, sems.at[at + i])
        for i, (a, b) in enumerate(zip(sources, targets))
    ]
    for c in copies:
        c.start()
    return copies


def wait_all(copies):
    for c in copies:
        c.wait()


def sum_panels(panels_h, owner_h, turn_h, edge_h, out, panels, owner, turn, edge_table, sems):
    wait_all(
        fetch((panels_h, owner_h, turn_h, edge_h), (panels, owner, turn, edge_table), sems)
    )
    n_vert = lax.axis_size("vert")
    tiles = turn.shape[0]
    spec = turn.shape[1] // 2
    held = owner.shape[1]
    named = jnp.where(
        owner[...] == lax.broadcasted_iota(jnp.int32, (tiles, held), 0), 1.0, 0.0
    ).astype(jnp.bfloat16)
    named = jnp.concatenate([named, named], axis=1)
    cos_t, sin_t = turn[:, :spec], turn[:, spec:]
    turned = []
    for f in range(NF):
        total = bdot(named, jnp.concatenate(split(panels[f]), axis=0), ((1,), (0,)))
        c, s = total[:, :spec], total[:, spec:]
        c2 = c * cos_t + s * sin_t
        s2 = s * cos_t - c * sin_t
        out[pl.ds(f, tiles, stride=ROWS), :] = c2
        out[pl.ds(8 + f, tiles, stride=ROWS), :] = s2
        turned.append(jnp.concatenate([c2, s2], axis=1))
    hi, lo = split(jnp.concatenate(turned, axis=0))
    edge = bdot(jnp.concatenate([hi, hi, lo], axis=1), edge_table[...], ((1,), (0,)))
    lane = lax.broadcasted_iota(jnp.int32, (tiles, 128), 1)
    for f in range(NF):
        e = edge[f * tiles : (f + 1) * tiles]
        row = jnp.where(
            lane < 32,
            jnp.roll(e, n_vert, 0),
            jnp.where(
                lane < 64,
                jnp.roll(e, -n_vert, 0),
                jnp.where(lane < 80, jnp.roll(e, 1, 0), jnp.roll(e, -1, 0)),
            ),
        )
        at = 5 + f if f < 3 else 10 + f
        out[pl.ds(at, tiles, stride=ROWS), :] = row
    out[pl.ds(15, tiles, stride=ROWS), :] = jnp.zeros((tiles, 128), jnp.float32)


def lane_ids(shape):
    return lax.broadcasted_iota(jnp.int32, shape, len(shape) - 1)


INNER = 8


def packed_x(acc, v, zi):
    lane = lane_ids((8, 128))
    for h in range(2):
        k = 2 * zi + h
        acc = jnp.where((lane >> 1) == k, pltpu.roll(v[8 * h : 8 * h + 8], 2 * k + 1, 1), acc)
    return acc


def placed(whole, part, zo):
    width = 4 * INNER
    lane = lane_ids((8, 128))
    return jnp.where(lane // width == zo, pltpu.roll(part, zo * width, 1), whole)


def face_choice(axis):
    return lax.rem(lax.axis_index(axis), 2) == 0


def store_faces(state, ye, yo, ze, zo):
    cz, cy = state.shape[1], state.shape[2]
    y_low, z_low = face_choice("span"), face_choice("vert")
    for f in range(NF):
        low, high = state[f, :, 0, :], state[f, :, cy - 1, :]
        ye[f] = jnp.where(y_low, high, low)
        yo[f] = jnp.where(y_low, low, high)
        low, high = state[f, 0], state[f, cz - 1]
        ze[f] = jnp.where(z_low, high, low)
        zo[f] = jnp.where(z_low, low, high)


def pack_faces(fields, xf, ye, yo, ze, zo):
    cz = fields.shape[1]
    zero = jnp.zeros((8, 128), jnp.float32)

    def body(g, accs):
        new = []
        for f in range(NF):
            part = zero
            for i in range(INNER):
                part = packed_x(part, fields[f, g * INNER + i], i)
            new.append(placed(accs[f], part, g))
        return tuple(new)

    accs = lax.fori_loop(0, cz // INNER, body, (zero,) * NF)
    for f in range(NF):
        xf[f] = accs[f]
    store_faces(fields, ye, yo, ze, zo)


def fill_ghosts(q, ye, yo, ze, zo, extra=None):
    cz = q.shape[1] - 2
    y_low, z_low = face_choice("span"), face_choice("vert")
    for f in range(NF):
        south = jnp.where(y_low, yo[f], ye[f])
        north = jnp.where(y_low, ye[f], yo[f])
        down = jnp.where(z_low, zo[f], ze[f])
        up = jnp.where(z_low, ze[f], zo[f])
        if extra is not None:
            es, en, ed, eu = extra(f)
            south, north, down, up = south + es, north + en, down + ed, up + eu
        q[f, 1 : cz + 1, 7, :] = south
        q[f, 1 : cz + 1, 24, :] = north
        q[f, 0, 8:24, :] = down
        q[f, cz + 1, 8:24, :] = up


def ghosts_x(west, east):
    lane = lane_ids((8, 128))
    return [jnp.where((lane & 1) == 0, west[f], pltpu.roll(east[f], 126, 1)) for f in range(NF)]


def slab_rates(q, xg, damp2, decay, z, zi):
    lane = lane_ids((16, 128))
    first, last = lane == 0, lane == 127
    cs, dx, dy, dz, rs = [], [], [], [], []
    for f in range(NF):
        c = q[f, z + 1, 8:24, :]
        up, down = q[f, z + 2, 8:24, :], q[f, z, 8:24, :]
        north, south = q[f, z + 1, 9:25, :], q[f, z + 1, 7:23, :]
        side = jnp.concatenate(
            [
                pltpu.roll(xg[f], (128 - 4 * zi) % 128, 1),
                pltpu.roll(xg[f], (126 - 4 * zi) % 128, 1),
            ],
            axis=0,
        )
        west = jnp.where(first, side, pltpu.roll(c, 1, 1))
        east = jnp.where(last, side, pltpu.roll(c, 127, 1))
        nu = heat_diff if f == 4 else viscous
        around = (east + west) + (north + south) + (up + down)
        cs.append(c)
        dx.append(east - west)
        dy.append(north - south)
        dz.append(up - down)
        rs.append(nu * around - decay[f == 4] * c)
    hu, hv, hw = 0.5 * cs[0], 0.5 * cs[1], 0.5 * cs[2]
    out = []
    for f in range(NF):
        r = rs[f] - (hu * dx[f] + hv * dy[f] + hw * dz[f])
        if f == 0:
            r = r - 0.5 * dx[3] - damp2 * hu
        elif f == 1:
            r = r - 0.5 * dy[3] - damp2 * hv
        elif f == 2:
            r = r - 0.5 * dz[3] - damp2 * hw + buoyant * cs[4]
        elif f == 3:
            r = r - (0.5 * sound_sq) * (dx[0] + dy[1] + dz[2])
        out.append(r)
    return cs, out


def relax_weights(cx):
    lane = lane_ids((1, cx))
    weight = jnp.exp(lane.astype(jnp.float32) * (-1.0 / relax_depth)) / relax_time
    return jnp.where((lax.axis_index("stream") == 0) & (lane < cx // 2), weight, 0.0)


def first_step(*refs):
    fields, solid = refs[:2]
    got, xe, xo, ye, yo, ze, zo = refs[2:9]
    base_out, carry_out, ye1, yo1, ze1, zo1 = refs[9:15]
    q, base, base_sems, carry, carry_sems = refs[15:20]
    cz = fields.shape[1]
    total = got[0:ROWS]
    for i in range(1, got.shape[0] // ROWS):
        total = total + got[ROWS * i : ROWS * i + ROWS]
    carry[0:ROWS] = total

    def fill(z, carry):
        for f in range(NF):
            q[f, z + 1, 8:24, :] = fields[f, z]
        return carry

    lax.fori_loop(0, cz, fill, 0, unroll=4)
    fill_ghosts(q, ye, yo, ze, zo)
    x_low = face_choice("stream")
    xg = ghosts_x(
        [jnp.where(x_low, xo[f], xe[f]) for f in range(NF)],
        [jnp.where(x_low, xe[f], xo[f]) for f in range(NF)],
    )
    relax = relax_weights(fields.shape[3])
    decay = (6.0 * viscous + relax, 6.0 * heat_diff + relax)
    zero = jnp.zeros((8, 128), jnp.float32)

    def body(g, accs):
        turned = [pltpu.roll(xg[f], (128 - 4 * INNER * g) & 127, 1) for f in range(NF)]
        parts = [zero] * NF
        for i in range(INNER):
            z = g * INNER + i
            damp2 = solid[z] * (2.0 / penalty)
            cs, rs = slab_rates(q, turned, damp2, decay, z, i)
            for f in range(NF):
                b = cs[f] + time_step * rs[f]
                base[f, z] = b
                parts[f] = packed_x(parts[f], b, i)
        chunk = pl.ds(pl.multiple_of(g * INNER, INNER), INNER)
        pltpu.make_async_copy(base.at[:, chunk], base_out.at[:, chunk], base_sems.at[g]).start()
        return tuple(placed(accs[f], parts[f], g) for f in range(NF))

    accs = lax.fori_loop(0, cz // INNER, body, (zero,) * NF)
    for f in range(NF):
        carry[ROWS + 8 * f : ROWS + 8 * f + 8] = accs[f]
    n_stream = carry_out.shape[0]
    going = fetch([carry] * n_stream, [carry_out.at[i] for i in range(n_stream)], carry_sems)
    store_faces(base, ye1, yo1, ze1, zo1)
    wait_all(going)
    for g in range(cz // INNER):
        chunk = pl.ds(g * INNER, INNER)
        pltpu.make_async_copy(base.at[:, chunk], base_out.at[:, chunk], base_sems.at[g]).wait()


def second_step(*refs):
    fields, solid, base = refs[:3]
    plane_table, carried, ye, yo, ze, zo, cells, geom, strips, shapes = refs[3:13]
    out_h, modal, q, target, out, out_sems = refs[13:19]
    cz, cy, cx = fields.shape[1:]
    n_stream = carried.shape[0]
    span_pos = lax.axis_index("span")
    vert_pos = lax.axis_index("vert")
    stream_pos = lax.axis_index("stream")
    get_base = pltpu.make_async_copy(base, q.at[:, 1 : cz + 1, 8:24, :], out_sems.at[0])
    get_base.start()
    relax = relax_weights(cx)
    decay = (6.0 * viscous + relax, 6.0 * heat_diff + relax)

    @pl.when(stream_pos == 0)
    def _():
        low, high = carried[0, 0:8], carried[0, 8:16]
        for i in range(1, n_stream):
            low = low + carried[i, 0:8]
            high = high + carried[i, 8:16]
        one = jnp.where(lane_ids((1, 8)) == 0, 1.0, 0.0)
        hi, lo = split(jnp.concatenate([low, high], axis=1))
        target[...] = (
            bdot(plane_table[...], jnp.concatenate([hi, hi, lo], axis=1), ((1,), (1,))) + one
        )
        n_edge = 2 * cz + 2 * cy
        pick = (
            lax.broadcasted_iota(jnp.int32, (n_edge, 128), 0) == lane_ids((n_edge, 128))
        ).astype(jnp.bfloat16)
        pick = jnp.concatenate([pick, pick], axis=1)
        e_low = bdot(pick, jnp.concatenate(split(low), axis=1), ((1,), (1,)))
        e_high = bdot(pick, jnp.concatenate(split(high), axis=1), ((1,), (1,)))
        push = time_step * relax

        def edge_push(f):
            col = e_low[:, 5 + f : 6 + f] if f < 3 else e_high[:, 2 + f : 3 + f]
            if f == 0:
                col = col + 1.0
            col = col * push
            return (
                jnp.where(span_pos > 0, col[0:cz], 0.0),
                jnp.where(span_pos < lax.axis_size("span") - 1, col[cz : 2 * cz], 0.0),
                jnp.where(vert_pos > 0, col[2 * cz : 2 * cz + cy], 0.0),
                jnp.where(vert_pos < lax.axis_size("vert") - 1, col[2 * cz + cy :], 0.0),
            )

        fill_ghosts(q, ye, yo, ze, zo, edge_push)
        get_base.wait()

        def pushing(g, carry):
            for i in range(4):
                z = g * 4 + i
                t = target[pl.ds(pl.multiple_of(z * cy, cy), cy), :]
                for f in range(NF):
                    pushed = push * t[:, f : f + 1]
                    q[f, z + 1, 8:24, :] = q[f, z + 1, 8:24, :] + pushed
                    out[f, z] = fields[f, z] + pushed
            return carry

        lax.fori_loop(0, cz // 4, pushing, 0)

    @pl.when(stream_pos > 0)
    def _():
        fill_ghosts(q, ye, yo, ze, zo)

        def keep(z, carry):
            for f in range(NF):
                out[f, z] = fields[f, z]
            return carry

        lax.fori_loop(0, cz, keep, 0, unroll=4)
        get_base.wait()

    west_at = jnp.maximum(stream_pos - 1, 0)
    east_at = jnp.minimum(stream_pos + 1, n_stream - 1)
    west, east = [], []
    for f in range(NF):
        rows = slice(ROWS + 8 * f, ROWS + 8 * f + 8)
        west.append(jnp.where(stream_pos > 0, carried[west_at, rows], 0.0))
        east.append(jnp.where(stream_pos < n_stream - 1, carried[east_at, rows], 0.0))
    xg = ghosts_x(west, east)

    def body(g, carry):
        turned = [pltpu.roll(xg[f], (128 - 4 * INNER * g) & 127, 1) for f in range(NF)]
        for i in range(INNER):
            z = g * INNER + i
            damp2 = solid[z] * (2.0 / penalty)
            cs, rs = slab_rates(q, turned, damp2, decay, z, i)
            for f in range(NF):
                out[f, z] = 0.5 * (out[f, z] + cs[f] + time_step * rs[f])
        chunk = pl.ds(pl.multiple_of(g * INNER, INNER), INNER)
        pltpu.make_async_copy(out.at[:, chunk], out_h.at[:, chunk], out_sems.at[g + 1]).start()
        return carry

    lax.fori_loop(0, cz // INNER, body, 0)

    pressure = jnp.transpose(jnp.reshape(out[3], (cz * cy, cx)))
    p_hi = pressure.astype(jnp.bfloat16)
    p_lo = (pressure - p_hi.astype(jnp.float32)).astype(jnp.bfloat16)
    parts = jnp.concatenate([p_hi, p_lo], axis=0)
    count = cells.shape[1]
    step = 512
    n_comp = geom.shape[2]
    own = shapes.shape[2] // lax.axis_size("span")
    sums = [jnp.zeros((8, 128), jnp.float32)] * own
    for at in range(0, count, step):
        where = cells[:, at : at + step]
        rows = lax.broadcasted_iota(jnp.int32, (cz * cy, step), 0)
        hit = jnp.where(rows == (where >> 7), 1.0, 0.0).astype(jnp.bfloat16)
        picked = bdot(parts, hit, ((1,), (0,)))
        picked = picked[:cx] + picked[cx:]
        lanes = lax.broadcasted_iota(jnp.int32, (cx, step), 0)
        sample = jnp.sum(jnp.where(lanes == (where & 127), picked, 0.0), axis=0, keepdims=True)
        traction = jnp.concatenate(
            [sample * geom[0, span_pos, c, :, at : at + step] for c in range(n_comp)]
            + [jnp.zeros((8 - n_comp, step), jnp.float32)],
            axis=0,
        )
        strip = strips[0, span_pos, :, at : at + step] - span_pos * own
        for j in range(own):
            mine = jnp.where(strip == j, traction, 0.0)
            for k in range(0, step, 128):
                sums[j] = sums[j] + mine[:, k : k + 128]
    lane = lane_ids((8, shapes.shape[2]))
    spread = jnp.zeros((8, shapes.shape[2]), jnp.float32)
    for j in range(own):
        force = jnp.sum(sums[j], axis=1, keepdims=True)
        spread = jnp.where(lane == span_pos * own + j, force, spread)
    total = jnp.zeros(shapes.shape[1:], jnp.float32)
    for c in range(n_comp):
        total = total + shapes[c] * spread[c : c + 1]
    total = mdot(jnp.ones((8, shapes.shape[2]), jnp.float32), total, ((1,), (1,)))[0:1]
    total = jnp.concatenate(
        [total, jnp.zeros((1, 128 - shapes.shape[1]), jnp.float32)], axis=1
    )
    modal[...] = jnp.broadcast_to(total, modal.shape)
    for g in range(cz // INNER):
        chunk = pl.ds(g * INNER, INNER)
        pltpu.make_async_copy(out.at[:, chunk], out_h.at[:, chunk], out_sems.at[g + 1]).wait()


def f32(*shape):
    return jax.ShapeDtypeStruct(shape, jnp.float32)


VM = pl.BlockSpec(memory_space=pltpu.VMEM)
HB = pl.BlockSpec(memory_space=pltpu.HBM)


def room(mib):
    return pltpu.CompilerParams(vmem_limit_bytes=mib * 1024 * 1024)


def buffers(arrays):
    return [pltpu.VMEM(x.shape, x.dtype) for x in arrays]


def swapped(block, axis, odd):
    pairs = []
    for i in range(odd, lax.axis_size(axis) - 1, 2):
        pairs += [(i, i + 1), (i + 1, i)]
    return lax.ppermute(block, axis, pairs)


def on_device(
    fields, solid_frac, panels, panel_owner, deck_cells, deck_geom, strip_ids, mode_shapes
):
    cz, cy, cx = fields.shape[1:]
    n_stream = lax.axis_size("stream")
    n_span = lax.axis_size("span")
    n_vert = lax.axis_size("vert")
    tiles = n_span * n_vert
    spec = panels.shape[2] // 2
    plane, edges, turn = wave_tables(cz, cy, n_span, n_vert, spec)
    operands = (
        panels.transpose(1, 0, 2),
        panel_owner.reshape(1, -1),
        jnp.asarray(turn),
        jnp.asarray(edges),
    )
    sent = pl.pallas_call(
        sum_panels,
        out_shape=f32(tiles * ROWS, 128),
        in_specs=[HB] * 4,
        out_specs=VM,
        scratch_shapes=buffers(operands) + [pltpu.SemaphoreType.DMA((4,))],
        compiler_params=room(60),
        name="panel_sums",
    )(*operands)
    got = lax.all_to_all(
        sent.reshape(tiles, ROWS, 128), ("span", "vert"), 0, 0, tiled=True
    ).reshape(tiles * ROWS, 128)
    yz_shapes = (f32(NF, cz, cx), f32(NF, cz, cx), f32(NF, cy, cx), f32(NF, cy, cx))

    def swap_yz(ye, yo, ze, zo):
        return (
            swapped(ye, "span", 0),
            swapped(yo, "span", 1),
            swapped(ze, "vert", 0),
            swapped(zo, "vert", 1),
        )

    xf, *faces = pl.pallas_call(
        pack_faces,
        out_shape=(f32(NF, 8, 128),) + yz_shapes,
        in_specs=[VM],
        out_specs=(VM,) * 5,
        compiler_params=room(52),
        name="pack_faces",
    )(fields)
    ghosts = (swapped(xf, "stream", 0), swapped(xf, "stream", 1)) + swap_yz(*faces)
    scratch = pltpu.VMEM((NF, cz + 2, 32, cx), jnp.float32)
    arrived = (got,) + ghosts
    leaving = (f32(n_stream, ROWS + 8 * NF, 128),) + yz_shapes
    base, carry, *faces = pl.pallas_call(
        first_step,
        out_shape=(f32(NF, cz, cy, cx),) + leaving,
        in_specs=[VM] * 9,
        out_specs=(HB, HB) + (VM,) * 4,
        scratch_shapes=[
            scratch,
            pltpu.VMEM((NF, cz, cy, cx), jnp.float32),
            pltpu.SemaphoreType.DMA((cz // INNER,)),
            pltpu.VMEM((ROWS + 8 * NF, 128), jnp.float32),
            pltpu.SemaphoreType.DMA((n_stream,)),
        ],
        compiler_params=room(52),
        name="first_step",
    )(fields, solid_frac, *arrived)
    carried = lax.all_to_all(carry, "stream", 0, 0, tiled=True)
    ghosts = swap_yz(*faces)
    deck = deck_cells.shape[3]
    plane = jnp.asarray(plane)
    cells = deck_cells.reshape(1, deck)
    shapes = mode_shapes.transpose(0, 2, 1)
    new_fields, modal = pl.pallas_call(
        second_step,
        out_shape=(f32(NF, cz, cy, cx), f32(n_span, 128)),
        in_specs=[VM] * 2 + [HB] + [VM] * 10,
        out_specs=(HB, VM),
        scratch_shapes=[scratch, pltpu.VMEM((cz * cy, 8), jnp.float32)]
        + [pltpu.VMEM((NF, cz, cy, cx), jnp.float32)]
        + [pltpu.SemaphoreType.DMA((cz // INNER + 1,))],
        compiler_params=room(51),
        name="second_step",
    )(
        fields,
        solid_frac,
        base,
        plane,
        carried,
        *ghosts,
        cells,
        deck_geom.transpose(0, 1, 3, 2, 4),
        strip_ids,
        shapes,
    )
    part = lax.all_to_all(modal, "span", 0, 0, tiled=True)
    part = jnp.broadcast_to(jnp.sum(part, axis=0, keepdims=True), (n_stream * n_vert, 128))
    part = lax.all_to_all(part, ("stream", "vert"), 0, 0, tiled=True)
    modal_force = jnp.sum(part, axis=0)[: mode_shapes.shape[2]]
    return (new_fields, modal_force)


def solution(mesh):
    return jax.shard_map(
        on_device,
        mesh=mesh,
        in_specs=(
            P(None, "vert", "span", "stream"),
            P("vert", "span", "stream"),
            P(("stream", "span", "vert"), None, None),
            P(("stream", "span", "vert"), None),
            P("vert", "span", "stream", None),
            P("vert", None, "stream", None, None),
            P("vert", None, "stream", None),
            P(),
        ),
        out_specs=(P(None, "vert", "span", "stream"), P()),
        check_vma=False,
    )
```

```python
import math

import jax
import jax.numpy as jnp
import ml_dtypes
import numpy as np
from jax import lax
from jax.experimental import pallas as pl
from jax.experimental.pallas import tpu as pltpu
from jax.sharding import PartitionSpec as P

time_step = 0.15
viscous = 0.05
heat_diff = 0.03
sound_sq = 1.0
buoyant = 0.5
penalty = 0.5
relax_time = 0.5
relax_depth = 8.0
wave_cols = 16

HI = lax.Precision.HIGHEST
NF = 5
ROWS = 16


def mdot(a, b, dims):
    return lax.dot_general(
        a, b, (dims, ((), ())), precision=HI, preferred_element_type=jnp.float32
    )


def split_np(a):
    hi = a.astype(ml_dtypes.bfloat16)
    return hi, (a - hi.astype(np.float32)).astype(ml_dtypes.bfloat16)


def split(a):
    hi = a.astype(jnp.bfloat16)
    return hi, (a - hi.astype(jnp.float32)).astype(jnp.bfloat16)


def bdot(a, b, dims):
    return lax.dot_general(a, b, (dims, ((), ())), preferred_element_type=jnp.float32)


def wave_tables(cz, cy, n_span, n_vert, spec):
    modes = np.arange(spec)
    across = (modes % wave_cols).astype(np.float64)
    upward = (modes // wave_cols).astype(np.float64)
    ny, nz = cy * n_span, cz * n_vert

    def basis(z, y):
        turn = across[None] * y[:, None] / ny + upward[None] * z[:, None] / nz
        angle = 2.0 * math.pi * turn
        return np.concatenate([np.cos(angle), np.sin(angle)], axis=1)

    z, y = np.arange(cz, dtype=np.float64), np.arange(cy, dtype=np.float64)
    plane = basis(np.repeat(z, cy), np.tile(y, cz)).astype(np.float32)
    edges = np.zeros((2 * spec, 128), np.float64)
    at = 0
    for part in (
        basis(z, 0 * z + cy - 1),
        basis(z, 0 * z),
        basis(0 * y + cz - 1, y),
        basis(0 * y, y),
    ):
        edges[:, at : at + part.shape[0]] = part.T
        at += part.shape[0]
    s, v = np.repeat(np.arange(n_span), n_vert), np.tile(np.arange(n_vert), n_span)
    turn = basis(1.0 * v * cz, 1.0 * s * cy).astype(np.float32)
    hi, lo = split_np(plane)
    plane = np.concatenate([hi, lo, hi], axis=1)
    hi, lo = split_np(edges.astype(np.float32))
    edges = np.concatenate([hi, lo, hi], axis=0)
    return plane, edges, turn


def fetch(sources, targets, sems, at=0):
    copies = [
        pltpu.make_async_copy(a, b, sems.at[at + i])
        for i, (a, b) in enumerate(zip(sources, targets))
    ]
    for c in copies:
        c.start()
    return copies


def wait_all(copies):
    for c in copies:
        c.wait()


def sum_panels(panels_h, owner_h, turn_h, edge_h, out, panels, owner, turn, edge_table, sems):
    wait_all(
        fetch((panels_h, owner_h, turn_h, edge_h), (panels, owner, turn, edge_table), sems)
    )
    n_vert = lax.axis_size("vert")
    tiles = turn.shape[0]
    spec = turn.shape[1] // 2
    held = owner.shape[1]
    named = jnp.where(
        owner[...] == lax.broadcasted_iota(jnp.int32, (tiles, held), 0), 1.0, 0.0
    ).astype(jnp.bfloat16)
    named = jnp.concatenate([named, named], axis=1)
    cos_t, sin_t = turn[:, :spec], turn[:, spec:]
    turned = []
    for f in range(NF):
        total = bdot(named, jnp.concatenate(split(panels[f]), axis=0), ((1,), (0,)))
        c, s = total[:, :spec], total[:, spec:]
        c2 = c * cos_t + s * sin_t
        s2 = s * cos_t - c * sin_t
        out[pl.ds(f, tiles, stride=ROWS), :] = c2
        out[pl.ds(8 + f, tiles, stride=ROWS), :] = s2
        turned.append(jnp.concatenate([c2, s2], axis=1))
    hi, lo = split(jnp.concatenate(turned, axis=0))
    edge = bdot(jnp.concatenate([hi, hi, lo], axis=1), edge_table[...], ((1,), (0,)))
    lane = lax.broadcasted_iota(jnp.int32, (tiles, 128), 1)
    for f in range(NF):
        e = edge[f * tiles : (f + 1) * tiles]
        row = jnp.where(
            lane < 32,
            jnp.roll(e, n_vert, 0),
            jnp.where(
                lane < 64,
                jnp.roll(e, -n_vert, 0),
                jnp.where(lane < 80, jnp.roll(e, 1, 0), jnp.roll(e, -1, 0)),
            ),
        )
        at = 5 + f if f < 3 else 10 + f
        out[pl.ds(at, tiles, stride=ROWS), :] = row
    out[pl.ds(15, tiles, stride=ROWS), :] = jnp.zeros((tiles, 128), jnp.float32)


def lane_ids(shape):
    return lax.broadcasted_iota(jnp.int32, shape, len(shape) - 1)


INNER = 8
WIDE = 16


def packed_x(acc, v, zi):
    lane = lane_ids((8, 128))
    for h in range(2):
        k = 2 * zi + h
        acc = jnp.where((lane >> 1) == k, pltpu.roll(v[8 * h : 8 * h + 8], 2 * k + 1, 1), acc)
    return acc


def placed(whole, part, zo, inner):
    width = 4 * inner
    lane = lane_ids((8, 128))
    return jnp.where(lane // width == zo, pltpu.roll(part, zo * width, 1), whole)


def face_choice(axis):
    return lax.rem(lax.axis_index(axis), 2) == 0


def store_faces(state, ye, yo, ze, zo):
    cz, cy = state.shape[1], state.shape[2]
    y_low, z_low = face_choice("span"), face_choice("vert")
    for f in range(NF):
        low, high = state[f, :, 0, :], state[f, :, cy - 1, :]
        ye[f] = jnp.where(y_low, high, low)
        yo[f] = jnp.where(y_low, low, high)
        low, high = state[f, 0], state[f, cz - 1]
        ze[f] = jnp.where(z_low, high, low)
        zo[f] = jnp.where(z_low, low, high)


def pack_faces(fields, xf, ye, yo, ze, zo):
    cz = fields.shape[1]
    zero = jnp.zeros((8, 128), jnp.float32)

    def body(g, accs):
        new = []
        for f in range(NF):
            part = zero
            for i in range(WIDE):
                part = packed_x(part, fields[f, g * WIDE + i], i)
            new.append(placed(accs[f], part, g, WIDE))
        return tuple(new)

    accs = lax.fori_loop(0, cz // WIDE, body, (zero,) * NF)
    for f in range(NF):
        xf[f] = accs[f]
    store_faces(fields, ye, yo, ze, zo)


def fill_ghosts(q, ye, yo, ze, zo, extra=None):
    cz = q.shape[1] - 2
    y_low, z_low = face_choice("span"), face_choice("vert")
    for f in range(NF):
        south = jnp.where(y_low, yo[f], ye[f])
        north = jnp.where(y_low, ye[f], yo[f])
        down = jnp.where(z_low, zo[f], ze[f])
        up = jnp.where(z_low, ze[f], zo[f])
        if extra is not None:
            es, en, ed, eu = extra(f)
            south, north, down, up = south + es, north + en, down + ed, up + eu
        q[f, 1 : cz + 1, 7, :] = south
        q[f, 1 : cz + 1, 24, :] = north
        q[f, 0, 8:24, :] = down
        q[f, cz + 1, 8:24, :] = up


def ghosts_x(west, east):
    lane = lane_ids((8, 128))
    return [jnp.where((lane & 1) == 0, west[f], pltpu.roll(east[f], 126, 1)) for f in range(NF)]


def slab_rates(q, xg, damp2, decay, z, zi):
    lane = lane_ids((16, 128))
    first, last = lane == 0, lane == 127
    cs, dx, dy, dz, rs = [], [], [], [], []
    for f in range(NF):
        c = q[f, z + 1, 8:24, :]
        up, down = q[f, z + 2, 8:24, :], q[f, z, 8:24, :]
        north, south = q[f, z + 1, 9:25, :], q[f, z + 1, 7:23, :]
        side = jnp.concatenate(
            [
                pltpu.roll(xg[f], (128 - 4 * zi) % 128, 1),
                pltpu.roll(xg[f], (126 - 4 * zi) % 128, 1),
            ],
            axis=0,
        )
        west = jnp.where(first, side, pltpu.roll(c, 1, 1))
        east = jnp.where(last, side, pltpu.roll(c, 127, 1))
        nu = heat_diff if f == 4 else viscous
        around = (east + west) + (north + south) + (up + down)
        cs.append(c)
        dx.append(east - west)
        dy.append(north - south)
        dz.append(up - down)
        rs.append(nu * around - decay[f == 4] * c)
    hu, hv, hw = 0.5 * cs[0], 0.5 * cs[1], 0.5 * cs[2]
    out = []
    for f in range(NF):
        r = rs[f] - (hu * dx[f] + hv * dy[f] + hw * dz[f])
        if f == 0:
            r = r - 0.5 * dx[3] - damp2 * hu
        elif f == 1:
            r = r - 0.5 * dy[3] - damp2 * hv
        elif f == 2:
            r = r - 0.5 * dz[3] - damp2 * hw + buoyant * cs[4]
        elif f == 3:
            r = r - (0.5 * sound_sq) * (dx[0] + dy[1] + dz[2])
        out.append(r)
    return cs, out


def relax_weights(cx):
    lane = lane_ids((1, cx))
    weight = jnp.exp(lane.astype(jnp.float32) * (-1.0 / relax_depth)) / relax_time
    return jnp.where((lax.axis_index("stream") == 0) & (lane < cx // 2), weight, 0.0)


def first_step(*refs):
    fields, solid = refs[:2]
    got, xe, xo, ye, yo, ze, zo = refs[2:9]
    base_out, carry_out, ye1, yo1, ze1, zo1 = refs[9:15]
    q, base, base_sems, carry, carry_sems = refs[15:20]
    cz = fields.shape[1]
    total = got[0:ROWS]
    for i in range(1, got.shape[0] // ROWS):
        total = total + got[ROWS * i : ROWS * i + ROWS]
    carry[0:ROWS] = total

    def fill(z, carry):
        for f in range(NF):
            q[f, z + 1, 8:24, :] = fields[f, z]
        return carry

    lax.fori_loop(0, cz, fill, 0, unroll=4)
    fill_ghosts(q, ye, yo, ze, zo)
    x_low = face_choice("stream")
    xg = ghosts_x(
        [jnp.where(x_low, xo[f], xe[f]) for f in range(NF)],
        [jnp.where(x_low, xe[f], xo[f]) for f in range(NF)],
    )
    relax = relax_weights(fields.shape[3])
    decay = (6.0 * viscous + relax, 6.0 * heat_diff + relax)
    zero = jnp.zeros((8, 128), jnp.float32)

    def body(g, accs):
        turned = [pltpu.roll(xg[f], (128 - 4 * INNER * g) & 127, 1) for f in range(NF)]
        parts = [zero] * NF
        for i in range(INNER):
            z = g * INNER + i
            damp2 = solid[z] * (2.0 / penalty)
            cs, rs = slab_rates(q, turned, damp2, decay, z, i)
            for f in range(NF):
                b = cs[f] + time_step * rs[f]
                base[f, z] = b
                parts[f] = packed_x(parts[f], b, i)
        chunk = pl.ds(pl.multiple_of(g * INNER, INNER), INNER)
        pltpu.make_async_copy(base.at[:, chunk], base_out.at[:, chunk], base_sems.at[g]).start()
        return tuple(placed(accs[f], parts[f], g, INNER) for f in range(NF))

    accs = lax.fori_loop(0, cz // INNER, body, (zero,) * NF)
    for f in range(NF):
        carry[ROWS + 8 * f : ROWS + 8 * f + 8] = accs[f]
    n_stream = carry_out.shape[0]
    going = fetch([carry] * n_stream, [carry_out.at[i] for i in range(n_stream)], carry_sems)
    store_faces(base, ye1, yo1, ze1, zo1)
    wait_all(going)
    for g in range(cz // INNER):
        chunk = pl.ds(g * INNER, INNER)
        pltpu.make_async_copy(base.at[:, chunk], base_out.at[:, chunk], base_sems.at[g]).wait()


def second_step(*refs):
    fields, solid, base = refs[:3]
    plane_table, carried, ye, yo, ze, zo, cells, geom, strips, shapes = refs[3:13]
    out_h, modal, q, target, out, out_sems = refs[13:19]
    cz, cy, cx = fields.shape[1:]
    n_stream = carried.shape[0]
    span_pos = lax.axis_index("span")
    vert_pos = lax.axis_index("vert")
    stream_pos = lax.axis_index("stream")
    get_base = pltpu.make_async_copy(base, q.at[:, 1 : cz + 1, 8:24, :], out_sems.at[0])
    get_base.start()
    relax = relax_weights(cx)
    decay = (6.0 * viscous + relax, 6.0 * heat_diff + relax)

    @pl.when(stream_pos == 0)
    def _():
        low, high = carried[0, 0:8], carried[0, 8:16]
        for i in range(1, n_stream):
            low = low + carried[i, 0:8]
            high = high + carried[i, 8:16]
        one = jnp.where(lane_ids((1, 8)) == 0, 1.0, 0.0)
        hi, lo = split(jnp.concatenate([low, high], axis=1))
        target[...] = (
            bdot(plane_table[...], jnp.concatenate([hi, hi, lo], axis=1), ((1,), (1,))) + one
        )
        n_edge = 2 * cz + 2 * cy
        pick = (
            lax.broadcasted_iota(jnp.int32, (n_edge, 128), 0) == lane_ids((n_edge, 128))
        ).astype(jnp.bfloat16)
        pick = jnp.concatenate([pick, pick], axis=1)
        e_low = bdot(pick, jnp.concatenate(split(low), axis=1), ((1,), (1,)))
        e_high = bdot(pick, jnp.concatenate(split(high), axis=1), ((1,), (1,)))
        push = time_step * relax

        def edge_push(f):
            col = e_low[:, 5 + f : 6 + f] if f < 3 else e_high[:, 2 + f : 3 + f]
            if f == 0:
                col = col + 1.0
            col = col * push
            return (
                jnp.where(span_pos > 0, col[0:cz], 0.0),
                jnp.where(span_pos < lax.axis_size("span") - 1, col[cz : 2 * cz], 0.0),
                jnp.where(vert_pos > 0, col[2 * cz : 2 * cz + cy], 0.0),
                jnp.where(vert_pos < lax.axis_size("vert") - 1, col[2 * cz + cy :], 0.0),
            )

        fill_ghosts(q, ye, yo, ze, zo, edge_push)
        get_base.wait()

        def pushing(g, carry):
            for i in range(4):
                z = g * 4 + i
                t = target[pl.ds(pl.multiple_of(z * cy, cy), cy), :]
                for f in range(NF):
                    pushed = push * t[:, f : f + 1]
                    q[f, z + 1, 8:24, :] = q[f, z + 1, 8:24, :] + pushed
                    out[f, z] = fields[f, z] + pushed
            return carry

        lax.fori_loop(0, cz // 4, pushing, 0)

    @pl.when(stream_pos > 0)
    def _():
        fill_ghosts(q, ye, yo, ze, zo)

        def keep(z, carry):
            for f in range(NF):
                out[f, z] = fields[f, z]
            return carry

        lax.fori_loop(0, cz, keep, 0, unroll=4)
        get_base.wait()

    west_at = jnp.maximum(stream_pos - 1, 0)
    east_at = jnp.minimum(stream_pos + 1, n_stream - 1)
    west, east = [], []
    for f in range(NF):
        rows = slice(ROWS + 8 * f, ROWS + 8 * f + 8)
        west.append(jnp.where(stream_pos > 0, carried[west_at, rows], 0.0))
        east.append(jnp.where(stream_pos < n_stream - 1, carried[east_at, rows], 0.0))
    xg = ghosts_x(west, east)

    def body(g, carry):
        turned = [pltpu.roll(xg[f], (128 - 4 * WIDE * g) & 127, 1) for f in range(NF)]
        for i in range(WIDE):
            z = g * WIDE + i
            damp2 = solid[z] * (2.0 / penalty)
            cs, rs = slab_rates(q, turned, damp2, decay, z, i)
            for f in range(NF):
                out[f, z] = 0.5 * (out[f, z] + cs[f] + time_step * rs[f])
        chunk = pl.ds(pl.multiple_of(g * WIDE, WIDE), WIDE)
        pltpu.make_async_copy(out.at[:, chunk], out_h.at[:, chunk], out_sems.at[g + 1]).start()
        return carry

    lax.fori_loop(0, cz // WIDE, body, 0)

    pressure = jnp.transpose(jnp.reshape(out[3], (cz * cy, cx)))
    p_hi = pressure.astype(jnp.bfloat16)
    p_lo = (pressure - p_hi.astype(jnp.float32)).astype(jnp.bfloat16)
    parts = jnp.concatenate([p_hi, p_lo], axis=0)
    count = cells.shape[1]
    step = 512
    n_comp = geom.shape[2]
    own = shapes.shape[2] // lax.axis_size("span")
    sums = [jnp.zeros((8, 128), jnp.float32)] * own
    for at in range(0, count, step):
        where = cells[:, at : at + step]
        rows = lax.broadcasted_iota(jnp.int32, (cz * cy, step), 0)
        hit = jnp.where(rows == (where >> 7), 1.0, 0.0).astype(jnp.bfloat16)
        picked = bdot(parts, hit, ((1,), (0,)))
        picked = picked[:cx] + picked[cx:]
        lanes = lax.broadcasted_iota(jnp.int32, (cx, step), 0)
        sample = jnp.sum(jnp.where(lanes == (where & 127), picked, 0.0), axis=0, keepdims=True)
        traction = jnp.concatenate(
            [sample * geom[0, span_pos, c, :, at : at + step] for c in range(n_comp)]
            + [jnp.zeros((8 - n_comp, step), jnp.float32)],
            axis=0,
        )
        strip = strips[0, span_pos, :, at : at + step] - span_pos * own
        for j in range(own):
            mine = jnp.where(strip == j, traction, 0.0)
            for k in range(0, step, 128):
                sums[j] = sums[j] + mine[:, k : k + 128]
    lane = lane_ids((8, shapes.shape[2]))
    spread = jnp.zeros((8, shapes.shape[2]), jnp.float32)
    for j in range(own):
        force = jnp.sum(sums[j], axis=1, keepdims=True)
        spread = jnp.where(lane == span_pos * own + j, force, spread)
    total = jnp.zeros(shapes.shape[1:], jnp.float32)
    for c in range(n_comp):
        total = total + shapes[c] * spread[c : c + 1]
    total = mdot(jnp.ones((8, shapes.shape[2]), jnp.float32), total, ((1,), (1,)))[0:1]
    total = jnp.concatenate(
        [total, jnp.zeros((1, 128 - shapes.shape[1]), jnp.float32)], axis=1
    )
    modal[...] = jnp.broadcast_to(total, modal.shape)
    for g in range(cz // WIDE):
        chunk = pl.ds(g * WIDE, WIDE)
        pltpu.make_async_copy(out.at[:, chunk], out_h.at[:, chunk], out_sems.at[g + 1]).wait()


def f32(*shape):
    return jax.ShapeDtypeStruct(shape, jnp.float32)


VM = pl.BlockSpec(memory_space=pltpu.VMEM)
HB = pl.BlockSpec(memory_space=pltpu.HBM)


def room(mib):
    return pltpu.CompilerParams(vmem_limit_bytes=mib * 1024 * 1024)


def buffers(arrays):
    return [pltpu.VMEM(x.shape, x.dtype) for x in arrays]


def swapped(block, axis, odd):
    pairs = []
    for i in range(odd, lax.axis_size(axis) - 1, 2):
        pairs += [(i, i + 1), (i + 1, i)]
    return lax.ppermute(block, axis, pairs)


def on_device(
    fields, solid_frac, panels, panel_owner, deck_cells, deck_geom, strip_ids, mode_shapes
):
    cz, cy, cx = fields.shape[1:]
    n_stream = lax.axis_size("stream")
    n_span = lax.axis_size("span")
    n_vert = lax.axis_size("vert")
    tiles = n_span * n_vert
    spec = panels.shape[2] // 2
    plane, edges, turn = wave_tables(cz, cy, n_span, n_vert, spec)
    operands = (
        panels.transpose(1, 0, 2),
        panel_owner.reshape(1, -1),
        jnp.asarray(turn),
        jnp.asarray(edges),
    )
    sent = pl.pallas_call(
        sum_panels,
        out_shape=f32(tiles * ROWS, 128),
        in_specs=[HB] * 4,
        out_specs=VM,
        scratch_shapes=buffers(operands) + [pltpu.SemaphoreType.DMA((4,))],
        compiler_params=room(60),
        name="panel_sums",
    )(*operands)
    got = lax.all_to_all(
        sent.reshape(tiles, ROWS, 128), ("span", "vert"), 0, 0, tiled=True
    ).reshape(tiles * ROWS, 128)
    yz_shapes = (f32(NF, cz, cx), f32(NF, cz, cx), f32(NF, cy, cx), f32(NF, cy, cx))

    def swap_yz(ye, yo, ze, zo):
        return (
            swapped(ye, "span", 0),
            swapped(yo, "span", 1),
            swapped(ze, "vert", 0),
            swapped(zo, "vert", 1),
        )

    xf, *faces = pl.pallas_call(
        pack_faces,
        out_shape=(f32(NF, 8, 128),) + yz_shapes,
        in_specs=[VM],
        out_specs=(VM,) * 5,
        compiler_params=room(52),
        name="pack_faces",
    )(fields)
    ghosts = (swapped(xf, "stream", 0), swapped(xf, "stream", 1)) + swap_yz(*faces)
    scratch = pltpu.VMEM((NF, cz + 2, 32, cx), jnp.float32)
    arrived = (got,) + ghosts
    leaving = (f32(n_stream, ROWS + 8 * NF, 128),) + yz_shapes
    base, carry, *faces = pl.pallas_call(
        first_step,
        out_shape=(f32(NF, cz, cy, cx),) + leaving,
        in_specs=[VM] * 9,
        out_specs=(HB, HB) + (VM,) * 4,
        scratch_shapes=[
            scratch,
            pltpu.VMEM((NF, cz, cy, cx), jnp.float32),
            pltpu.SemaphoreType.DMA((cz // INNER,)),
            pltpu.VMEM((ROWS + 8 * NF, 128), jnp.float32),
            pltpu.SemaphoreType.DMA((n_stream,)),
        ],
        compiler_params=room(52),
        name="first_step",
    )(fields, solid_frac, *arrived)
    carried = lax.all_to_all(carry, "stream", 0, 0, tiled=True)
    ghosts = swap_yz(*faces)
    deck = deck_cells.shape[3]
    plane = jnp.asarray(plane)
    cells = deck_cells.reshape(1, deck)
    shapes = mode_shapes.transpose(0, 2, 1)
    new_fields, modal = pl.pallas_call(
        second_step,
        out_shape=(f32(NF, cz, cy, cx), f32(n_span, 128)),
        in_specs=[VM] * 2 + [HB] + [VM] * 10,
        out_specs=(HB, VM),
        scratch_shapes=[scratch, pltpu.VMEM((cz * cy, 8), jnp.float32)]
        + [pltpu.VMEM((NF, cz, cy, cx), jnp.float32)]
        + [pltpu.SemaphoreType.DMA((cz // INNER + 1,))],
        compiler_params=room(51),
        name="second_step",
    )(
        fields,
        solid_frac,
        base,
        plane,
        carried,
        *ghosts,
        cells,
        deck_geom.transpose(0, 1, 3, 2, 4),
        strip_ids,
        shapes,
    )
    part = lax.all_to_all(modal, "span", 0, 0, tiled=True)
    part = jnp.broadcast_to(jnp.sum(part, axis=0, keepdims=True), (n_stream * n_vert, 128))
    part = lax.all_to_all(part, ("stream", "vert"), 0, 0, tiled=True)
    modal_force = jnp.sum(part, axis=0)[: mode_shapes.shape[2]]
    return (new_fields, modal_force)


def solution(mesh):
    return jax.shard_map(
        on_device,
        mesh=mesh,
        in_specs=(
            P(None, "vert", "span", "stream"),
            P("vert", "span", "stream"),
            P(("stream", "span", "vert"), None, None),
            P(("stream", "span", "vert"), None),
            P("vert", "span", "stream", None),
            P("vert", None, "stream", None, None),
            P("vert", None, "stream", None),
            P(),
        ),
        out_specs=(P(None, "vert", "span", "stream"), P()),
        check_vma=False,
    )
```
